32 devices in a mesh: ctx: 8 (over z, core), fsdp: 4 (over y, x).
Axes of the slice: x: 2, y: 2, z: 4, core: 2. Of those that a mesh axis runs over, the one named last changes fastest.
Arguments:
- block_input: bfloat16 [4, 2048, 1024], P('fsdp', 'ctx'), may hold values from -6 to 6
- cotangent: bfloat16 [4, 2048, 1024], P('fsdp', 'ctx'), may hold values from -6 to 6
- seq_lengths: int32 [4], P('fsdp'), may hold values from 512 to 2048, as said below
- block_table: int32 [16], replicated, may hold values from 0 to 15, each once
- query_proj: float32 [1024, 2048], P('fsdp'), may hold values from -0.1875 to 0.1875
- key_proj: float32 [1024, 1024], P('fsdp'), may hold values from -0.1875 to 0.1875
- value_proj: float32 [1024, 1024], P('fsdp'), may hold values from -0.1875 to 0.1875
- output_proj: float32 [2048, 1024], P('fsdp'), may hold values from -1 to 1
- gate_proj: float32 [1024, 3072], P('fsdp'), may hold values from -0.1875 to 0.1875
- up_proj: float32 [1024, 3072], P('fsdp'), may hold values from -0.1875 to 0.1875
- down_proj: float32 [3072, 1024], P('fsdp'), may hold values from -0.109375 to 0.109375
- attn_norm: float32 [1024], P('fsdp'), may hold values from 0.1 to 1.9
- ffn_norm: float32 [1024], P('fsdp'), may hold values from 0.1 to 1.9
- query_norm: float32 [128], P('fsdp'), may hold values from 0.1 to 1.9
- key_norm: float32 [128], P('fsdp'), may hold values from 0.1 to 1.9
Outputs:
- block_output: bfloat16 [4, 2048, 1024], P('fsdp', 'ctx')
- grad_input: float32 [4, 2048, 1024], P('fsdp', 'ctx')
- grad_query: float32 [1024, 2048], P('fsdp')
- grad_key: float32 [1024, 1024], P('fsdp')
- grad_value: float32 [1024, 1024], P('fsdp')
- grad_output: float32 [2048, 1024], P('fsdp')
- grad_gate: float32 [1024, 3072], P('fsdp')
- grad_up: float32 [1024, 3072], P('fsdp')
- grad_down: float32 [3072, 1024], P('fsdp')
- grad_attnnorm: float32 [1024], P('fsdp')
- grad_ffnnorm: float32 [1024], P('fsdp')
- grad_qnorm: float32 [128], P('fsdp')
- grad_knorm: float32 [128], P('fsdp')
The draws below stay inside these ranges and needn't reach their ends.
Inputs may be any that keep to these rules, and one draw needn't show every extreme that they name: `seq_lengths`: slots at positions from a sequence's length on are padding. Some sequence has exactly 2048 valid tokens and some exactly 512. `block_table`: each block number appears exactly once; stored blocks 2c and 2c + 1 lie on index c of ctx.
All inputs are finite; a program needn't handle non-finite values.
Results may differ from the reference program's by a relative error of at most 0.018.
Values may be sent and summed in bfloat16 or wider, within the bound.
No kernel may reach another device: no remote copies, remote signals or barrier semaphores. Data moves between devices by JAX's collectives and lax.ppermute only.
A program may use at most 256 MiB of HBM per device.

```python
import math
import jax
import jax.numpy as jnp
from jax import lax

D = 1024
HQ = 16
KV = 8
HD = 128
FF = 3072
SLOT_DEV = 256
SEQ_SLOTS = 2048
BLOCKS = 16
SEQS = 4


def draw_seq_lengths(key, part):
    lowest = SEQ_SLOTS // 4
    highest = SEQ_SLOTS
    drawn = jax.random.randint(jax.random.fold_in(key, 11), (SEQS,), lowest, highest + 1)
    chosen = jax.random.permutation(jax.random.fold_in(key, 12), SEQS)
    drawn = drawn.at[chosen[0]].set(highest)
    drawn = drawn.at[chosen[1]].set(lowest)
    return drawn.astype(jnp.int32)


def shard_levels(own_key, shape, shards, least, high):
    level = 1.0
    for position, blocks in shards:
        draws = jax.random.uniform(jax.random.fold_in(jax.random.fold_in(own_key, 6), position), (blocks,), jnp.float32, least / len(shards), high / len(shards))
        level = level * jnp.repeat(jnp.exp(draws), shape[position] // blocks).reshape((-1,) + (1,) * (len(shape) - 1 - position))
    return level


def gaussian(key, extent, deviation, bound, pieces=(), kind=jnp.bfloat16):
    values = deviation * jax.random.normal(key, extent, jnp.float32)
    if pieces:
        values = values * shard_levels(key, extent, pieces, -0.22, 0.18)
    return jnp.clip(values, -bound, bound).astype(kind)


def setup_inputs(seed: int = 0) -> dict:
    streams_of = jax.random.split(jax.random.key(seed), 16)
    return {
        "block_input": gaussian(streams_of[0], (SEQS, SEQ_SLOTS, D), 1.0, 6.0, ((0, 4), (1, 8))),
        "cotangent": gaussian(streams_of[1], (SEQS, SEQ_SLOTS, D), 1.0, 6.0, ((0, 4), (1, 8))),
        "seq_lengths": draw_seq_lengths(jax.random.fold_in(streams_of[15], 71), 0),
        "block_table": jax.random.permutation(streams_of[3], BLOCKS).astype(jnp.int32),
        "query_proj": gaussian(streams_of[4], (D, HQ * HD), D ** -0.5, 0.1875, ((0, 4),), jnp.float32),
        "key_proj": gaussian(streams_of[5], (D, KV * HD), D ** -0.5, 0.1875, ((0, 4),), jnp.float32),
        "value_proj": gaussian(streams_of[6], (D, KV * HD), D ** -0.5, 0.1875, ((0, 4),), jnp.float32),
        "output_proj": gaussian(streams_of[7], (HQ * HD, D), (max(1, HQ * HD * 32 // SEQ_SLOTS)) ** -0.5, 1.0, ((0, 4),), jnp.float32),
        "gate_proj": gaussian(streams_of[8], (D, FF), D ** -0.5, 0.1875, ((0, 4),), jnp.float32),
        "up_proj": gaussian(streams_of[9], (D, FF), D ** -0.5, 0.1875, ((0, 4),), jnp.float32),
        "down_proj": gaussian(streams_of[10], (FF, D), FF ** -0.5, 0.109375, ((0, 4),), jnp.float32),
        "attn_norm": jnp.clip(1.0 + 0.18 * jax.random.normal(streams_of[11], (D,), jnp.float32), 0.1, 1.9),
        "ffn_norm": jnp.clip(1.0 + 0.18 * jax.random.normal(streams_of[12], (D,), jnp.float32), 0.1, 1.9),
        "query_norm": jnp.clip(1.0 + 0.18 * jax.random.normal(streams_of[13], (HD,), jnp.float32), 0.1, 1.9),
        "key_norm": jnp.clip(1.0 + 0.18 * jax.random.normal(streams_of[14], (HD,), jnp.float32), 0.1, 1.9),
    }


EPS = 1e-06
THETA = 1000000.0

@jax.custom_vjp
def low(v):
    return lax.optimization_barrier(v.astype(jnp.bfloat16)).astype(jnp.float32)

@jax.custom_vjp
def low_back(v):
    return v

def low_keep(v):
    return (low(v), None)

def low_pass(kept, grad):
    return (grad,)

def back_keep(v):
    return (v, None)

def back_low(kept, grad):
    return (low(grad),)
low.defvjp(low_keep, low_pass)
low_back.defvjp(back_keep, back_low)

def norm_rows(values):
    return values * lax.rsqrt(lax.optimization_barrier(jnp.mean(values * values, axis=-1, keepdims=True)) + EPS)

def rope_tables(positions, head_size):
    halfway = head_size // 2
    frequency = THETA ** (-(jnp.arange(halfway).astype(jnp.float32) * 2.0 / head_size))
    angles = positions.astype(jnp.float32)[:, None] * frequency[None, :]
    cosine = jnp.cos(angles)
    sine_table = jnp.sin(angles)
    return (jnp.concatenate([cosine, cosine], -1)[:, None, :], jnp.concatenate([sine_table, sine_table], -1)[:, None, :])

def rotate(values, cosine, sine_table):
    halfway = values.shape[-1] // 2
    turned = jnp.concatenate([-values[..., halfway:], values[..., :halfway]], -1)
    return values * cosine + turned * sine_table

def layer(params, inputs, positions, length):
    query_proj, key_proj, value_proj, output_proj, gate_proj, up_proj, down_proj, attn_norm, ffn_norm, query_norm, key_norm = [low(master) for master in params]
    highest = lax.Precision.HIGHEST
    slot_count = inputs.shape[0]
    group_size = HQ // KV
    score_scale = 1.0 / math.sqrt(HD)
    live_rows = (positions < length).astype(jnp.float32)[:, None]
    normed_low = low(norm_rows(inputs) * attn_norm)
    query_raw = low_back(jnp.dot(normed_low, query_proj, precision=highest)).reshape(slot_count, HQ, HD)
    key_raw = low_back(jnp.dot(normed_low, key_proj, precision=highest)).reshape(slot_count, KV, HD)
    value_raw = low_back(jnp.dot(normed_low, value_proj, precision=highest))
    cosine, sine_table = rope_tables(positions, HD)
    query_low = low(rotate(norm_rows(query_raw) * query_norm, cosine, sine_table)).reshape(slot_count, KV, group_size, HD)
    key_low = low(rotate(norm_rows(key_raw) * key_norm, cosine, sine_table))
    value_low = low(value_raw).reshape(slot_count, KV, HD)
    query_span = 512 if slot_count % 512 == 0 else slot_count
    block_count = slot_count // query_span

    def attend(block_args):
        query_block, pos_block = block_args
        scores = low_back(jnp.einsum('qngd,knd->ngqk', query_block, key_low, precision=highest) * score_scale)
        allowed = (positions[None, :] <= pos_block[:, None]) & (positions[None, :] < length)
        masked = jnp.where(allowed, scores, -1e+30)
        attn_probs = low(jax.nn.softmax(masked, axis=-1))
        return jnp.einsum('ngqk,knd->qngd', attn_probs, value_low, precision=highest)
    mixed_heads = lax.map(jax.checkpoint(attend), (query_low.reshape(block_count, query_span, KV, group_size, HD), positions.reshape(block_count, query_span)))
    attended = low(low_back(mixed_heads.reshape(slot_count, HQ * HD)))
    resid = inputs + low_back(jnp.dot(attended, output_proj, precision=highest))
    mid_low = low(norm_rows(resid) * ffn_norm)
    gate_val = low_back(jnp.dot(mid_low, gate_proj, precision=highest))
    up_val = low_back(jnp.dot(mid_low, up_proj, precision=highest))
    hidden_low = low(jax.nn.silu(gate_val) * up_val)
    ffn_out = low_back(jnp.dot(hidden_low, down_proj, precision=highest))
    return (resid + ffn_out) * live_rows

def reference(block_input, cotangent, seq_lengths, block_table, query_proj, key_proj, value_proj, output_proj, gate_proj, up_proj, down_proj, attn_norm, ffn_norm, query_norm, key_norm):
    params = (query_proj, key_proj, value_proj, output_proj, gate_proj, up_proj, down_proj, attn_norm, ffn_norm, query_norm, key_norm)
    half_slots = SLOT_DEV // 2
    offsets = jnp.arange(half_slots, dtype=jnp.int32)
    positions = (block_table.astype(jnp.int32)[:, None] * half_slots + offsets[None, :]).reshape(-1).astype(jnp.int32)

    def one_seq(carry, entries):
        inputs, upstream, length = entries
        result, pullback = jax.vjp(lambda weights, values: layer(weights, values, positions, length), params, inputs.astype(jnp.float32))
        weight_grads, input_grad = pullback(upstream.astype(jnp.float32))
        carry = jax.tree.map(lambda running, addend: running + addend, carry, weight_grads)
        return (carry, (result.astype(jnp.bfloat16), input_grad))
    zero_grads = jax.tree.map(jnp.zeros_like, params)
    grads, (outputs, input_grads) = lax.scan(one_seq, zero_grads, (block_input, cotangent, seq_lengths))
    return (outputs, input_grads, grads[0], grads[1], grads[2], grads[3], grads[4], grads[5], grads[6], grads[7], grads[8], grads[9], grads[10])
```

```python
import functools
import math

import jax
import jax.numpy as jnp
from jax import lax
from jax.experimental import pallas as pl
from jax.experimental.pallas import tpu as pltpu
from jax.sharding import PartitionSpec as P

EPS = 1e-06
THETA = 1000000.0
BF = jnp.bfloat16
F32 = jnp.float32
LOG2E = math.log2(math.e)
VMEM_LIMIT = 56 * 1024 * 1024


def dot_nn(left, right):
    return lax.dot_general(left, right, (((1,), (0,)), ((), ())), preferred_element_type=F32)


def dot_nt(left, right):
    return lax.dot_general(left, right, (((1,), (1,)), ((), ())), preferred_element_type=F32)


def dot_tn(left, right):
    return lax.dot_general(left, right, (((0,), (0,)), ((), ())), preferred_element_type=F32)


def norm_back(values, gain_vec, upstream_grad):
    inverse = lax.rsqrt(jnp.mean(values * values, axis=-1, keepdims=True) + EPS)
    normed = values * inverse
    gain_terms = upstream_grad * normed
    gained = upstream_grad * gain_vec
    grad_values = inverse * (gained - normed * jnp.mean(gained * normed, axis=-1, keepdims=True))
    return (grad_values, gain_terms)


def qkv_kernel(parts, heads, hd, order, *refs):
    x_refs = refs[:parts]
    gain, weight, gq, gk, cos, sin, a_out, raw_out, low_out = refs[parts:]
    x = jnp.concatenate([r[...] for r in x_refs], axis=0).astype(F32)
    a = (x * lax.rsqrt(jnp.mean(x * x, axis=-1, keepdims=True) + EPS) * gain[...]).astype(BF)
    a_out[...] = a
    raw = dot_nn(a, weight[...])
    c, s = cos[...], sin[...]
    for h in range(heads + 1):
        u = raw[:, h * hd : (h + 1) * hd]
        raw_out[:, h * hd : (h + 1) * hd] = u
        g = gq[...] if h < heads else gk[...]
        n = u * lax.rsqrt(jnp.mean(u * u, axis=-1, keepdims=True) + EPS) * g
        low_out[:, h * hd : (h + 1) * hd] = (n * c + pltpu.roll(n, hd // 2, axis=1) * s).astype(BF)
    low_out[:, (heads + 1) * hd :] = raw[:, (heads + 1) * hd :].astype(BF)


def qkv_call(order, x_all, gain, weight, gq, gk, cos, sin, heads, hd, blk):
    total, width = x_all.shape
    cols = weight.shape[1]
    parts = 4
    step = parts * blk
    grid = (total // step,)
    x_specs = [
        pl.BlockSpec((blk, width), functools.partial(lambda k, i, o: (o[parts * i + k], 0), k))
        for k in range(parts)
    ]
    const = lambda i, o: (0, 0)
    rows = lambda i, o: (i, 0)
    return pl.pallas_call(
        functools.partial(qkv_kernel, parts, heads, hd),
        out_shape=(
            jax.ShapeDtypeStruct((total, width), BF),
            jax.ShapeDtypeStruct((total, (heads + 1) * hd), F32),
            jax.ShapeDtypeStruct((total, cols), BF),
        ),
        grid_spec=pltpu.PrefetchScalarGridSpec(
            num_scalar_prefetch=1,
            grid=grid,
            in_specs=x_specs
            + [
                pl.BlockSpec((1, width), const),
                pl.BlockSpec(weight.shape, const),
                pl.BlockSpec((1, hd), const),
                pl.BlockSpec((1, hd), const),
                pl.BlockSpec((step, hd), rows),
                pl.BlockSpec((step, hd), rows),
            ],
            out_specs=(
                pl.BlockSpec((step, width), rows),
                pl.BlockSpec((step, (heads + 1) * hd), rows),
                pl.BlockSpec((step, cols), rows),
            ),
        ),
        compiler_params=pltpu.CompilerParams(vmem_limit_bytes=VMEM_LIMIT),
        cost_estimate=pl.CostEstimate(
            flops=2 * total * width * cols, bytes_accessed=total * width * 4, transcendentals=0
        ),
        name="qkv",
    )(order, *([x_all] * parts), gain, weight, gq, gk, cos, sin)


TILE = 256


def stack_heads(ref, start, heads, hd):
    return jnp.concatenate(
        [ref[pl.ds(start, TILE), h * hd : (h + 1) * hd] for h in range(heads)], axis=0
    )


def attn_kernel(heads, hd, blk, scale, order, length_ref, low, o_out, o32_out, lse_out, vext, acc):
    total = low.shape[0]
    length = length_ref[0]
    kcol, vcol = heads * hd, (heads + 1) * hd
    rows = heads * TILE
    vext[:, :hd] = low[:, vcol : vcol + hd]
    vext[:, hd:] = jnp.ones((total, hd), BF)
    full = length // TILE
    ends = pl.cdiv(length, TILE)

    @pl.loop(0, total // TILE)
    def _(i):
        qs = pl.multiple_of(i * TILE, TILE)
        q = stack_heads(low, qs, heads, hd)
        acc[...] = jnp.zeros_like(acc)

        def tile(j, masked):
            ks = pl.multiple_of(j * TILE, TILE)
            s = dot_nt(q, low[pl.ds(ks, TILE), kcol : kcol + hd])
            p = jnp.exp2(s * (scale * LOG2E))
            if masked:
                kpos = ks + lax.broadcasted_iota(jnp.int32, (rows, TILE), 1)
                qpos = qs + lax.broadcasted_iota(jnp.int32, (rows, TILE), 0) % TILE
                p = jnp.where((kpos <= qpos) & (kpos < length), p, 0.0)
            acc[...] += dot_nn(p.astype(BF), vext[pl.ds(ks, TILE), :])

        clean = jnp.minimum(i, full)

        @pl.loop(0, clean)
        def _(j):
            tile(j, False)

        @pl.loop(clean, jnp.minimum(i + 1, ends))
        def _(j):
            tile(j, True)

        total_p = acc[:, hd:]
        o = acc[:, :hd] / total_p
        lse_out[i] = jnp.log2(total_p).T[:8]
        for h in range(heads):
            cut = slice(h * hd, (h + 1) * hd)
            part = o[h * TILE : (h + 1) * TILE]
            o32_out[pl.ds(qs, TILE), cut] = part
            for b in range(TILE // blk):
                to = pl.multiple_of(order[i * (TILE // blk) + b] * blk, blk)
                o_out[pl.ds(to, blk), cut] = part[b * blk : (b + 1) * blk].astype(BF)


def attn_call(order, length, low, heads, hd, blk, scale):
    total = low.shape[0]
    tiles = total // TILE
    return pl.pallas_call(
        functools.partial(attn_kernel, heads, hd, blk, scale),
        out_shape=(
            jax.ShapeDtypeStruct((total, heads * hd), BF),
            jax.ShapeDtypeStruct((total, heads * hd), F32),
            jax.ShapeDtypeStruct((tiles, 8, heads * TILE), F32),
        ),
        in_specs=[
            pl.BlockSpec(memory_space=pltpu.SMEM),
            pl.BlockSpec(memory_space=pltpu.SMEM),
            pl.BlockSpec(memory_space=pltpu.VMEM),
        ],
        out_specs=(
            pl.BlockSpec(memory_space=pltpu.VMEM),
            pl.BlockSpec(memory_space=pltpu.VMEM),
            pl.BlockSpec(memory_space=pltpu.VMEM),
        ),
        scratch_shapes=[
            pltpu.VMEM((total, 2 * hd), BF),
            pltpu.VMEM((heads * TILE, 2 * hd), F32),
        ],
        compiler_params=pltpu.CompilerParams(vmem_limit_bytes=VMEM_LIMIT),
        cost_estimate=pl.CostEstimate(
            flops=3 * heads * total * total * hd,
            bytes_accessed=total * heads * hd * 12,
            transcendentals=heads * total * total // 2,
        ),
        name="attn_fwd",
    )(order, length, low)


def attn_back_kernel(
    heads, hd, blk, scale, order, length_ref, low, do_ref, o32, lse, dq_out, dkv_out, do_s, delta, dkv
):
    total = low.shape[0]
    tiles = total // TILE
    length = length_ref[0]
    kcol, vcol = heads * hd, (heads + 1) * hd
    rows = heads * TILE

    @pl.loop(0, tiles)
    def _(i):
        qs = pl.multiple_of(i * TILE, TILE)
        for b in range(TILE // blk):
            frm = pl.multiple_of(order[i * (TILE // blk) + b] * blk, blk)
            do_s[pl.ds(qs + b * blk, blk), :] = do_ref[pl.ds(frm, blk), :]
        do_t = stack_heads(do_s, qs, heads, hd).astype(F32) * stack_heads(o32, qs, heads, hd)
        delta[i] = lax.dot_general(
            jnp.ones((8, hd), F32),
            do_t,
            (((1,), (1,)), ((), ())),
            preferred_element_type=F32,
            precision=lax.Precision.HIGHEST,
        )
        dq_out[pl.ds(qs, TILE), :] = jnp.zeros((TILE, heads * hd), F32)

    full = length // TILE

    @pl.loop(0, tiles)
    def _(j):
        ks = pl.multiple_of(j * TILE, TILE)
        k = low[pl.ds(ks, TILE), kcol : kcol + hd]
        v = low[pl.ds(ks, TILE), vcol : vcol + hd]
        dkv[...] = jnp.zeros_like(dkv)

        def tile(i, masked):
            qs = pl.multiple_of(i * TILE, TILE)
            q = stack_heads(low, qs, heads, hd)
            do = stack_heads(do_s, qs, heads, hd)
            s = dot_nt(k, q)
            p = jnp.exp2(s * (scale * LOG2E) - lse[i][:1])
            if masked:
                kpos = ks + lax.broadcasted_iota(jnp.int32, (TILE, rows), 0)
                qpos = qs + lax.broadcasted_iota(jnp.int32, (TILE, rows), 1) % TILE
                p = jnp.where((kpos <= qpos) & (kpos < length), p, 0.0)
            dp = dot_nt(v, do)
            ds = (p * (dp - delta[i][:1])).astype(BF)
            dkv[:, :hd] += dot_nn(ds, q)
            dkv[:, hd:] += dot_nn(p.astype(BF), do)
            dq = dot_tn(ds, k)
            for h in range(heads):
                dq_out[pl.ds(qs, TILE), h * hd : (h + 1) * hd] += dq[h * TILE : (h + 1) * TILE]

        masked_end = jnp.where(j < full, j + 1, tiles)

        @pl.loop(j, masked_end)
        def _(i):
            tile(i, True)

        @pl.loop(masked_end, tiles)
        def _(i):
            tile(i, False)

        dkv_out[pl.ds(ks, TILE), :hd] = dkv[:, :hd] * scale
        dkv_out[pl.ds(ks, TILE), hd:] = dkv[:, hd:]

    dq_out[...] = dq_out[...] * scale


def attn_back_call(order, length, low, do, o32, lse, heads, hd, blk, scale):
    total = low.shape[0]
    tiles = total // TILE
    smem = pl.BlockSpec(memory_space=pltpu.SMEM)
    vmem = pl.BlockSpec(memory_space=pltpu.VMEM)
    return pl.pallas_call(
        functools.partial(attn_back_kernel, heads, hd, blk, scale),
        out_shape=(
            jax.ShapeDtypeStruct((total, heads * hd), F32),
            jax.ShapeDtypeStruct((total, 2 * hd), F32),
        ),
        in_specs=[smem, smem, vmem, vmem, vmem, vmem],
        out_specs=(vmem, vmem),
        scratch_shapes=[
            pltpu.VMEM((total, heads * hd), BF),
            pltpu.VMEM((tiles, 8, heads * TILE), F32),
            pltpu.VMEM((TILE, 2 * hd), F32),
        ],
        compiler_params=pltpu.CompilerParams(vmem_limit_bytes=VMEM_LIMIT),
        cost_estimate=pl.CostEstimate(
            flops=5 * heads * total * total * hd,
            bytes_accessed=total * heads * hd * 16,
            transcendentals=heads * total * total // 2,
        ),
        name="attn_bwd",
    )(order, length, low, do, o32, lse)


def head_back_kernel(parts, blk, heads, hd, order, dq, dkv, raw, weight, gq, gk, cos, sin, *outs):
    da_outs = outs[:1]
    low_out, gain_out = outs[1], outs[2]

    @pl.when(pl.program_id(0) == 0)
    def _():
        gain_out[...] = jnp.zeros_like(gain_out)

    c, s = cos[...], sin[...]
    pieces = []
    for h in range(heads + 1):
        cut = slice(h * hd, (h + 1) * hd)
        g_rot = dq[:, cut] if h < heads else dkv[:, :hd]
        e = g_rot * c + pltpu.roll(g_rot * s, hd // 2, axis=1)
        dv, terms = norm_back(raw[:, cut], gq[...] if h < heads else gk[...], e)
        low = dv.astype(BF)
        low_out[:, cut] = low
        pieces.append(low)
        row = 0 if h < heads else 1
        gain_out[row : row + 1, :] += jnp.sum(terms, axis=0, keepdims=True)
    low = dkv[:, hd:].astype(BF)
    low_out[:, (heads + 1) * hd :] = low
    pieces.append(low)
    da_outs[0][...] = dot_nt(jnp.concatenate(pieces, axis=1), weight[...]).astype(BF)


def head_back_call(order, dq, dkv, raw, weight, gq, gk, cos, sin, heads, hd, blk):
    total = dq.shape[0]
    width, cols = weight.shape
    step = 512
    const = lambda i, o: (0, 0)
    rows = lambda i, o: (i, 0)
    return pl.pallas_call(
        functools.partial(head_back_kernel, 4, blk, heads, hd),
        out_shape=(
            jax.ShapeDtypeStruct((total, width), BF),
            jax.ShapeDtypeStruct((total, cols), BF),
            jax.ShapeDtypeStruct((8, hd), F32),
        ),
        grid_spec=pltpu.PrefetchScalarGridSpec(
            num_scalar_prefetch=1,
            grid=(total // step,),
            in_specs=[
                pl.BlockSpec((step, heads * hd), rows),
                pl.BlockSpec((step, 2 * hd), rows),
                pl.BlockSpec((step, (heads + 1) * hd), rows),
                pl.BlockSpec(weight.shape, const),
                pl.BlockSpec((1, hd), const),
                pl.BlockSpec((1, hd), const),
                pl.BlockSpec((step, hd), rows),
                pl.BlockSpec((step, hd), rows),
            ],
            out_specs=(
                pl.BlockSpec((step, width), rows),
                pl.BlockSpec((step, cols), rows),
                pl.BlockSpec((8, hd), const),
            ),
        ),
        compiler_params=pltpu.CompilerParams(vmem_limit_bytes=VMEM_LIMIT),
        cost_estimate=pl.CostEstimate(
            flops=2 * total * width * cols, bytes_accessed=total * width * 4, transcendentals=0
        ),
        name="head_bwd",
    )(order, dq, dkv, raw, weight, gq, gk, cos, sin)


def place_kernel(order, src, dst):
    dst[...] = src[...]


def to_stored(order, values, blk):
    total, width = values.shape
    return pl.pallas_call(
        place_kernel,
        out_shape=jax.ShapeDtypeStruct((total, width), values.dtype),
        grid_spec=pltpu.PrefetchScalarGridSpec(
            num_scalar_prefetch=1,
            grid=(total // blk,),
            in_specs=[pl.BlockSpec((blk, width), lambda i, o: (i, 0))],
            out_specs=pl.BlockSpec((blk, width), lambda i, o: (o[i], 0)),
        ),
        name="to_stored",
    )(order, values)


def body(
    block_input,
    cotangent,
    seq_lengths,
    block_table,
    query_proj,
    key_proj,
    value_proj,
    output_proj,
    gate_proj,
    up_proj,
    down_proj,
    attn_norm,
    ffn_norm,
    query_norm,
    key_norm,
):
    C = lax.axis_size("ctx")
    F = lax.axis_size("fsdp")
    c_idx = lax.axis_index("ctx")
    f_idx = lax.axis_index("fsdp")
    T, D = block_input.shape[1:]
    S = T * C
    blocks = block_table.shape[0]
    blk = S // blocks
    hd = query_norm.shape[0] * F
    HQ = query_proj.shape[1] // hd
    KV = key_proj.shape[1] // hd
    FF = gate_proj.shape[1]
    heads = HQ // C
    rep = max(1, C // KV)
    FFl = FF // F
    R = D // (F * C)
    scale = 1.0 / math.sqrt(hd)
    length = seq_lengths.astype(jnp.int32)
    own_blocks = lax.dynamic_slice_in_dim(block_table, c_idx * (blocks // C), blocks // C)
    own_pos = (own_blocks[:, None] * blk + jnp.arange(blk, dtype=jnp.int32)[None, :]).reshape(-1)
    live = (own_pos < length[0]).astype(F32)[:, None]
    order = jnp.argsort(block_table).astype(jnp.int32)

    def gather_f(v):
        return lax.all_to_all(jnp.broadcast_to(v[None], (F,) + v.shape), "fsdp", 0, 0)

    def exchange_f(v):
        return lax.all_to_all(v, "fsdp", 0, 0)

    def exchange_c(v):
        return lax.all_to_all(v, "ctx", 0, 0)

    x_all = lax.all_gather(block_input[0], "ctx", axis=0, tiled=True)
    kv_at = (c_idx // rep) * hd
    w_own = jnp.concatenate(
        [
            lax.dynamic_slice_in_dim(query_proj, c_idx * heads * hd, heads * hd, 1),
            lax.dynamic_slice_in_dim(key_proj, kv_at, hd, 1),
            lax.dynamic_slice_in_dim(value_proj, kv_at, hd, 1),
        ],
        axis=1,
    ).astype(BF)
    w_heads = gather_f(w_own).reshape(D, (heads + 2) * hd)
    gains = lax.all_gather(
        jnp.concatenate([attn_norm, ffn_norm, query_norm, key_norm]).astype(BF), "fsdp", axis=0
    ).astype(F32)
    g1 = gains[:, : D // F].reshape(1, D)
    g2 = gains[:, D // F : 2 * D // F].reshape(1, D)
    gq = gains[:, 2 * D // F : (2 * D + hd) // F].reshape(1, hd)
    gk = gains[:, (2 * D + hd) // F :].reshape(1, hd)
    wo_full = lax.all_gather(output_proj.astype(BF), "fsdp", axis=0, tiled=True)
    gy = (cotangent[0].astype(F32) * live).astype(BF)
    gy_all = gather_f(gy).reshape(F * T, D)
    wgu_low = jnp.concatenate(
        [gate_proj.astype(BF).reshape(D // F, F, FFl), up_proj.astype(BF).reshape(D // F, F, FFl)],
        axis=2,
    )
    wgu = exchange_f(jnp.swapaxes(wgu_low, 0, 1)).reshape(D, 2 * FFl)
    wd = down_proj.astype(BF)

    half = hd // 2
    frequency = THETA ** (-(jnp.arange(half).astype(F32) * 2.0 / hd))
    angles = jnp.arange(S, dtype=jnp.int32).astype(F32)[:, None] * frequency[None, :]
    cos_t, sin_t = jnp.cos(angles), jnp.sin(angles)
    cos_t = jnp.concatenate([cos_t, cos_t], -1)
    sin_t = jnp.concatenate([-sin_t, sin_t], -1)
    a_s, raw, low = qkv_call(order, x_all, g1, w_heads, gq, gk, cos_t, sin_t, heads, hd, blk)
    o_st, o32, lse = attn_call(order, length, low, heads, hd, blk, scale)
    o_nat = exchange_c(o_st.reshape(C, T, heads * hd))
    wo_heads = wo_full.reshape(C, heads * hd, D)
    x = block_input[0].astype(F32)
    h = x + jnp.einsum("ctd,cdn->tn", o_nat, wo_heads, preferred_element_type=F32)

    m_own = (h * lax.rsqrt(jnp.mean(h * h, axis=-1, keepdims=True) + EPS) * g2).astype(BF)
    m = gather_f(m_own).reshape(F * T, D)
    gu = dot_nn(m, wgu)
    gate, up = gu[:, :FFl], gu[:, FFl:]
    sig = jax.nn.sigmoid(gate)
    silu = gate * sig
    hidden = (silu * up).astype(BF)
    dhid = dot_nt(gy_all, wd)
    dup = (dhid * silu).astype(BF)
    dgate = (dhid * up * sig * (1.0 + gate * (1.0 - sig))).astype(BF)
    dgu = jnp.concatenate([dgate, dup], axis=1)
    dm_part = dot_nt(dgu, wgu).astype(BF).reshape(F, T, D)
    dm = jnp.sum(exchange_f(dm_part).astype(F32), axis=0)
    dv, ffn_terms = norm_back(h, g2, dm)
    gy32 = gy.astype(F32)
    dh = gy32 + dv
    dhb = dh.astype(BF)

    do_nat = jnp.einsum("tn,cdn->ctd", dhb, wo_heads, preferred_element_type=F32).astype(BF)
    do_st = exchange_c(do_nat).reshape(S, heads * hd)
    dq, dkv = attn_back_call(order, length, low, do_st, o32, lse, heads, hd, blk, scale)
    da_part, dqkv, head_gains = head_back_call(
        order, dq, dkv, raw, w_heads, gq, gk, cos_t, sin_t, heads, hd, blk
    )
    da = lax.psum_scatter(
        to_stored(order, da_part, blk), "ctx", scatter_dimension=0, tiled=True
    ).astype(F32)
    dx, attn_terms = norm_back(x, g1, da)
    grad_input = (dh + dx)[None]

    ffn_part = dot_nn(hidden, wd).astype(BF).reshape(F, T, D)
    ffn = jnp.sum(exchange_f(ffn_part).astype(F32), axis=0)
    block_output = ((h + ffn) * live).astype(BF)[None]

    ggu = dot_tn(m, dgu).astype(BF).reshape(F, C, R, 2 * FFl)
    ggu = jnp.swapaxes(ggu, 0, 1).reshape(C * F * R, 2 * FFl)
    ggu = lax.psum_scatter(ggu, "ctx", scatter_dimension=0, tiled=True)
    ggu = exchange_f(ggu.reshape(F, R, 2 * FFl))
    ggu = lax.all_gather(ggu, "ctx", axis=0)
    ggu = jnp.transpose(ggu, (0, 2, 1, 3)).reshape(D // F, F, 2 * FFl)
    grad_gate = ggu[:, :, :FFl].reshape(D // F, FF).astype(F32)
    grad_up = ggu[:, :, FFl:].reshape(D // F, FF).astype(F32)

    dhb_all = gather_f(dhb)
    o_f = exchange_f(o_nat.reshape(F, C // F, T, heads * hd))
    go = jnp.einsum("sctd,stn->cdn", o_f, dhb_all, preferred_element_type=F32)
    go = go.astype(BF).reshape(C, -1, D)
    gd = dot_tn(hidden, gy_all).astype(BF).reshape(C, -1, D)
    n_o = go.shape[1]
    god = jnp.concatenate([go, gd], axis=1)
    god = lax.psum_scatter(god.reshape(-1, D), "ctx", scatter_dimension=0, tiled=True)
    god = lax.all_gather(god, "ctx", axis=0)
    grad_output = god[:, :n_o].reshape(-1, D).astype(F32)
    grad_down = god[:, n_o:].reshape(-1, D).astype(F32)

    gqkv = dot_tn(a_s, dqkv).astype(BF).reshape(F, D // F, (heads + 2) * hd)
    gqkv = jnp.sum(exchange_f(gqkv).astype(F32), axis=0).astype(BF)
    gqkv = lax.all_gather(gqkv, "ctx", axis=0).astype(F32)
    grad_query = jnp.swapaxes(gqkv[:, :, : heads * hd], 0, 1).reshape(D // F, HQ * hd)
    gkv = gqkv[:, :, heads * hd :]
    gkv = jnp.sum(gkv.reshape(C // rep, rep, D // F, 2 * hd), axis=1)
    grad_key = jnp.swapaxes(gkv[:, :, :hd], 0, 1).reshape(D // F, KV * hd)
    grad_value = jnp.swapaxes(gkv[:, :, hd:], 0, 1).reshape(D // F, KV * hd)

    small = jnp.concatenate(
        [jnp.sum(attn_terms, axis=0), jnp.sum(ffn_terms, axis=0), head_gains[0], head_gains[1]]
    )
    small = lax.psum(small, ("ctx", "fsdp"))
    own = lambda lo, n: lax.dynamic_slice_in_dim(small, lo + f_idx * (n // F), n // F)
    return (
        block_output,
        grad_input,
        grad_query,
        grad_key,
        grad_value,
        grad_output,
        grad_gate,
        grad_up,
        grad_down,
        own(0, D),
        own(D, D),
        own(2 * D, hd),
        own(2 * D + hd, hd),
    )


def solution(mesh):
    matrix, vector = P("fsdp", None), P("fsdp")
    rows = P("fsdp", "ctx", None)
    in_specs = (rows, rows, vector, P()) + (matrix,) * 7 + (vector,) * 4
    out_specs = (rows, rows) + (matrix,) * 7 + (vector,) * 4
    return jax.shard_map(body, mesh=mesh, in_specs=in_specs, out_specs=out_specs, check_vma=False)
```

```python
import functools
import math

import jax
import jax.numpy as jnp
from jax import lax
from jax.experimental import pallas as pl
from jax.experimental.pallas import tpu as pltpu
from jax.sharding import PartitionSpec as P

EPS = 1e-06
THETA = 1000000.0
BF = jnp.bfloat16
F32 = jnp.float32
LOG2E = math.log2(math.e)
VMEM_LIMIT = 56 * 1024 * 1024


def dot_nn(left, right):
    return lax.dot_general(left, right, (((1,), (0,)), ((), ())), preferred_element_type=F32)


def dot_nt(left, right):
    return lax.dot_general(left, right, (((1,), (1,)), ((), ())), preferred_element_type=F32)


def dot_tn(left, right):
    return lax.dot_general(left, right, (((0,), (0,)), ((), ())), preferred_element_type=F32)


def norm_back(values, gain_vec, upstream_grad):
    inverse = lax.rsqrt(jnp.mean(values * values, axis=-1, keepdims=True) + EPS)
    normed = values * inverse
    gain_terms = upstream_grad * normed
    gained = upstream_grad * gain_vec
    grad_values = inverse * (gained - normed * jnp.mean(gained * normed, axis=-1, keepdims=True))
    return (grad_values, gain_terms)


def qkv_kernel(parts, heads, hd, order, *refs):
    x_refs = refs[:parts]
    gain, weight, gq, gk, cos, sin, a_out, raw_out, low_out = refs[parts:]
    x = jnp.concatenate([r[...] for r in x_refs], axis=0).astype(F32)
    a = (x * lax.rsqrt(jnp.mean(x * x, axis=-1, keepdims=True) + EPS) * gain[...]).astype(BF)
    a_out[...] = a
    raw = dot_nn(a, weight[...])
    c, s = cos[...], sin[...]
    for h in range(heads + 1):
        u = raw[:, h * hd : (h + 1) * hd]
        raw_out[:, h * hd : (h + 1) * hd] = u
        g = gq[...] if h < heads else gk[...]
        n = u * lax.rsqrt(jnp.mean(u * u, axis=-1, keepdims=True) + EPS) * g
        low_out[:, h * hd : (h + 1) * hd] = (n * c + pltpu.roll(n, hd // 2, axis=1) * s).astype(BF)
    low_out[:, (heads + 1) * hd :] = raw[:, (heads + 1) * hd :].astype(BF)


def qkv_call(order, x_all, gain, weight, gq, gk, cos, sin, heads, hd, blk):
    total, width = x_all.shape
    cols = weight.shape[1]
    parts = 4
    step = parts * blk
    grid = (total // step,)
    x_specs = [
        pl.BlockSpec((blk, width), functools.partial(lambda k, i, o: (o[parts * i + k], 0), k))
        for k in range(parts)
    ]
    const = lambda i, o: (0, 0)
    rows = lambda i, o: (i, 0)
    return pl.pallas_call(
        functools.partial(qkv_kernel, parts, heads, hd),
        out_shape=(
            jax.ShapeDtypeStruct((total, width), BF),
            jax.ShapeDtypeStruct((total, (heads + 1) * hd), F32),
            jax.ShapeDtypeStruct((total, cols), BF),
        ),
        grid_spec=pltpu.PrefetchScalarGridSpec(
            num_scalar_prefetch=1,
            grid=grid,
            in_specs=x_specs
            + [
                pl.BlockSpec((1, width), const),
                pl.BlockSpec(weight.shape, const),
                pl.BlockSpec((1, hd), const),
                pl.BlockSpec((1, hd), const),
                pl.BlockSpec((step, hd), rows),
                pl.BlockSpec((step, hd), rows),
            ],
            out_specs=(
                pl.BlockSpec((step, width), rows),
                pl.BlockSpec((step, (heads + 1) * hd), rows),
                pl.BlockSpec((step, cols), rows),
            ),
        ),
        compiler_params=pltpu.CompilerParams(vmem_limit_bytes=VMEM_LIMIT),
        cost_estimate=pl.CostEstimate(
            flops=20 * total * width * cols, bytes_accessed=total * width * 4, transcendentals=0
        ),
        name="qkv",
    )(order, *([x_all] * parts), gain, weight, gq, gk, cos, sin)


TILE = 256


def stack_heads(ref, start, heads, hd):
    return jnp.concatenate(
        [ref[pl.ds(start, TILE), h * hd : (h + 1) * hd] for h in range(heads)], axis=0
    )


def attn_kernel(heads, hd, blk, scale, order, length_ref, low, o_out, o32_out, lse_out, vext, acc):
    total = low.shape[0]
    length = length_ref[0]
    kcol, vcol = heads * hd, (heads + 1) * hd
    rows = heads * TILE
    vext[:, :hd] = low[:, vcol : vcol + hd]
    vext[:, hd:] = jnp.ones((total, hd), BF)
    full = length // TILE
    ends = pl.cdiv(length, TILE)

    @pl.loop(0, total // TILE)
    def _(i):
        qs = pl.multiple_of(i * TILE, TILE)
        q = stack_heads(low, qs, heads, hd)
        acc[...] = jnp.zeros_like(acc)

        def tile(j, masked):
            ks = pl.multiple_of(j * TILE, TILE)
            s = dot_nt(q, low[pl.ds(ks, TILE), kcol : kcol + hd])
            p = jnp.exp2(s * (scale * LOG2E))
            if masked:
                kpos = ks + lax.broadcasted_iota(jnp.int32, (rows, TILE), 1)
                qpos = qs + lax.broadcasted_iota(jnp.int32, (rows, TILE), 0) % TILE
                p = jnp.where((kpos <= qpos) & (kpos < length), p, 0.0)
            acc[...] += dot_nn(p.astype(BF), vext[pl.ds(ks, TILE), :])

        clean = jnp.minimum(i, full)

        @pl.loop(0, clean)
        def _(j):
            tile(j, False)

        @pl.loop(clean, jnp.minimum(i + 1, ends))
        def _(j):
            tile(j, True)

        total_p = acc[:, hd:]
        o = acc[:, :hd] / total_p
        lse_out[i] = jnp.log2(total_p).T[:8]
        for h in range(heads):
            cut = slice(h * hd, (h + 1) * hd)
            part = o[h * TILE : (h + 1) * TILE]
            o32_out[pl.ds(qs, TILE), cut] = part
            for b in range(TILE // blk):
                to = pl.multiple_of(order[i * (TILE // blk) + b] * blk, blk)
                o_out[pl.ds(to, blk), cut] = part[b * blk : (b + 1) * blk].astype(BF)


def attn_call(order, length, low, heads, hd, blk, scale):
    total = low.shape[0]
    tiles = total // TILE
    return pl.pallas_call(
        functools.partial(attn_kernel, heads, hd, blk, scale),
        out_shape=(
            jax.ShapeDtypeStruct((total, heads * hd), BF),
            jax.ShapeDtypeStruct((total, heads * hd), F32),
            jax.ShapeDtypeStruct((tiles, 8, heads * TILE), F32),
        ),
        in_specs=[
            pl.BlockSpec(memory_space=pltpu.SMEM),
            pl.BlockSpec(memory_space=pltpu.SMEM),
            pl.BlockSpec(memory_space=pltpu.VMEM),
        ],
        out_specs=(
            pl.BlockSpec(memory_space=pltpu.VMEM),
            pl.BlockSpec(memory_space=pltpu.VMEM),
            pl.BlockSpec(memory_space=pltpu.VMEM),
        ),
        scratch_shapes=[
            pltpu.VMEM((total, 2 * hd), BF),
            pltpu.VMEM((heads * TILE, 2 * hd), F32),
        ],
        compiler_params=pltpu.CompilerParams(vmem_limit_bytes=VMEM_LIMIT),
        cost_estimate=pl.CostEstimate(
            flops=120 * heads * total * total * hd // 2,
            bytes_accessed=total * heads * hd * 12,
            transcendentals=heads * total * total // 2,
        ),
        name="attn_fwd",
    )(order, length, low)


def attn_back_kernel(
    heads, hd, blk, scale, order, length_ref, low, do_ref, o32, lse, dq_out, dkv_out, do_s, delta, dkv
):
    total = low.shape[0]
    tiles = total // TILE
    length = length_ref[0]
    kcol, vcol = heads * hd, (heads + 1) * hd
    rows = heads * TILE

    @pl.loop(0, tiles)
    def _(i):
        qs = pl.multiple_of(i * TILE, TILE)
        for b in range(TILE // blk):
            frm = pl.multiple_of(order[i * (TILE // blk) + b] * blk, blk)
            do_s[pl.ds(qs + b * blk, blk), :] = do_ref[pl.ds(frm, blk), :]
        do_t = stack_heads(do_s, qs, heads, hd).astype(F32) * stack_heads(o32, qs, heads, hd)
        delta[i] = lax.dot_general(
            jnp.ones((8, hd), F32),
            do_t,
            (((1,), (1,)), ((), ())),
            preferred_element_type=F32,
            precision=lax.Precision.HIGHEST,
        )
        dq_out[pl.ds(qs, TILE), :] = jnp.zeros((TILE, heads * hd), F32)

    full = length // TILE

    @pl.loop(0, tiles)
    def _(j):
        ks = pl.multiple_of(j * TILE, TILE)
        k = low[pl.ds(ks, TILE), kcol : kcol + hd]
        v = low[pl.ds(ks, TILE), vcol : vcol + hd]
        dkv[...] = jnp.zeros_like(dkv)

        def tile(i, masked):
            qs = pl.multiple_of(i * TILE, TILE)
            q = stack_heads(low, qs, heads, hd)
            do = stack_heads(do_s, qs, heads, hd)
            s = dot_nt(k, q)
            p = jnp.exp2(s * (scale * LOG2E) - lse[i][:1])
            if masked:
                kpos = ks + lax.broadcasted_iota(jnp.int32, (TILE, rows), 0)
                qpos = qs + lax.broadcasted_iota(jnp.int32, (TILE, rows), 1) % TILE
                p = jnp.where((kpos <= qpos) & (kpos < length), p, 0.0)
            dp = dot_nt(v, do)
            ds = (p * (dp - delta[i][:1])).astype(BF)
            dkv[:, :hd] += dot_nn(ds, q)
            dkv[:, hd:] += dot_nn(p.astype(BF), do)
            dq = dot_tn(ds, k)
            for h in range(heads):
                dq_out[pl.ds(qs, TILE), h * hd : (h + 1) * hd] += dq[h * TILE : (h + 1) * TILE]

        masked_end = jnp.where(j < full, j + 1, tiles)

        @pl.loop(j, masked_end)
        def _(i):
            tile(i, True)

        @pl.loop(masked_end, tiles)
        def _(i):
            tile(i, False)

        dkv_out[pl.ds(ks, TILE), :hd] = dkv[:, :hd] * scale
        dkv_out[pl.ds(ks, TILE), hd:] = dkv[:, hd:]

    dq_out[...] = dq_out[...] * scale


def attn_back_call(order, length, low, do, o32, lse, heads, hd, blk, scale):
    total = low.shape[0]
    tiles = total // TILE
    smem = pl.BlockSpec(memory_space=pltpu.SMEM)
    vmem = pl.BlockSpec(memory_space=pltpu.VMEM)
    return pl.pallas_call(
        functools.partial(attn_back_kernel, heads, hd, blk, scale),
        out_shape=(
            jax.ShapeDtypeStruct((total, heads * hd), F32),
            jax.ShapeDtypeStruct((total, 2 * hd), F32),
        ),
        in_specs=[smem, smem, vmem, vmem, vmem, vmem],
        out_specs=(vmem, vmem),
        scratch_shapes=[
            pltpu.VMEM((total, heads * hd), BF),
            pltpu.VMEM((tiles, 8, heads * TILE), F32),
            pltpu.VMEM((TILE, 2 * hd), F32),
        ],
        compiler_params=pltpu.CompilerParams(vmem_limit_bytes=VMEM_LIMIT),
        cost_estimate=pl.CostEstimate(
            flops=600 * heads * total * total * hd // 2,
            bytes_accessed=total * heads * hd * 16,
            transcendentals=heads * total * total // 2,
        ),
        name="attn_bwd",
    )(order, length, low, do, o32, lse)


def head_back_kernel(parts, blk, heads, hd, order, *refs):
    x_refs = refs[:parts]
    dq, dkv, raw, weight, go, gq, gk, cos, sin = refs[parts : parts + 9]
    send_out, low_out, gain_out, attn_out = refs[parts + 9 :]
    i = pl.program_id(0)

    @pl.when(i == 0)
    def _():
        gain_out[...] = jnp.zeros_like(gain_out)
        attn_out[...] = jnp.zeros_like(attn_out)
        rows_own = send_out.shape[1] - go.shape[1]
        for c in range(go.shape[0]):
            send_out[c, rows_own:, :] = go[c]

    c, s = cos[...], sin[...]
    pieces = []
    for h in range(heads + 1):
        cut = slice(h * hd, (h + 1) * hd)
        g_rot = dq[:, cut] if h < heads else dkv[:, :hd]
        e = g_rot * c + pltpu.roll(g_rot * s, hd // 2, axis=1)
        dv, terms = norm_back(raw[:, cut], gq[...] if h < heads else gk[...], e)
        low = dv.astype(BF)
        low_out[:, cut] = low
        pieces.append(low)
        row = 0 if h < heads else 1
        gain_out[row : row + 1, :] += jnp.sum(terms, axis=0, keepdims=True)
    low = dkv[:, hd:].astype(BF)
    low_out[:, (heads + 1) * hd :] = low
    pieces.append(low)
    da = dot_nt(jnp.concatenate(pieces, axis=1), weight[...])
    per = (send_out.shape[1] - go.shape[1]) // blk
    for k in range(parts):
        x = x_refs[k][...].astype(F32)
        part = da[k * blk : (k + 1) * blk]
        normed = x * lax.rsqrt(jnp.mean(x * x, axis=-1, keepdims=True) + EPS)
        attn_out[...] += jnp.sum(part * normed, axis=0, keepdims=True)
        at = order[parts * i + k]
        send_out[at // per, pl.ds(pl.multiple_of((at % per) * blk, blk), blk), :] = part.astype(BF)


def head_back_call(order, x_all, dq, dkv, raw, weight, go, gq, gk, cos, sin, heads, hd, blk, ctx):
    total = dq.shape[0]
    width, cols = weight.shape
    parts = 4
    step = parts * blk
    const = lambda i, o: (0, 0)
    const3 = lambda i, o: (0, 0, 0)
    rows = lambda i, o: (i, 0)
    x_specs = [
        pl.BlockSpec((blk, width), functools.partial(lambda k, i, o: (o[parts * i + k], 0), k))
        for k in range(parts)
    ]
    send = (ctx, total // ctx + go.shape[1], width)
    return pl.pallas_call(
        functools.partial(head_back_kernel, parts, blk, heads, hd),
        out_shape=(
            jax.ShapeDtypeStruct(send, BF),
            jax.ShapeDtypeStruct((total, cols), BF),
            jax.ShapeDtypeStruct((8, hd), F32),
            jax.ShapeDtypeStruct((1, width), F32),
        ),
        grid_spec=pltpu.PrefetchScalarGridSpec(
            num_scalar_prefetch=1,
            grid=(total // step,),
            in_specs=x_specs
            + [
                pl.BlockSpec((step, heads * hd), rows),
                pl.BlockSpec((step, 2 * hd), rows),
                pl.BlockSpec((step, (heads + 1) * hd), rows),
                pl.BlockSpec(weight.shape, const),
                pl.BlockSpec(go.shape, const3),
                pl.BlockSpec((1, hd), const),
                pl.BlockSpec((1, hd), const),
                pl.BlockSpec((step, hd), rows),
                pl.BlockSpec((step, hd), rows),
            ],
            out_specs=(
                pl.BlockSpec(send, const3),
                pl.BlockSpec((step, cols), rows),
                pl.BlockSpec((8, hd), const),
                pl.BlockSpec((1, width), const),
            ),
        ),
        compiler_params=pltpu.CompilerParams(vmem_limit_bytes=VMEM_LIMIT),
        cost_estimate=pl.CostEstimate(
            flops=2 * total * width * cols, bytes_accessed=total * width * 6, transcendentals=0
        ),
        name="head_bwd",
    )(order, *([x_all] * parts), dq, dkv, raw, weight, go, gq, gk, cos, sin)


def resid_kernel(core_ref, o, wo_a, wo_b, x, g2, h_out, m_out):
    core = core_ref[0]
    h = x[...].astype(F32)
    for f in range(wo_a.shape[0]):
        h = h + dot_nn(o[2 * f + core], wo_a[f])
        h = h + dot_nn(o[2 * f + 1 - core], wo_b[f])
    h_out[...] = h
    m_out[...] = (h * lax.rsqrt(jnp.mean(h * h, axis=-1, keepdims=True) + EPS) * g2[...]).astype(BF)


def resid_call(core, o, wo_a, wo_b, x, g2):
    T, D = x.shape
    smem = pl.BlockSpec(memory_space=pltpu.SMEM)
    vmem = pl.BlockSpec(memory_space=pltpu.VMEM)
    return pl.pallas_call(
        resid_kernel,
        out_shape=(jax.ShapeDtypeStruct((T, D), F32), jax.ShapeDtypeStruct((T, D), BF)),
        in_specs=[smem] + [vmem] * 5,
        out_specs=(vmem, vmem),
        compiler_params=pltpu.CompilerParams(vmem_limit_bytes=VMEM_LIMIT),
        cost_estimate=pl.CostEstimate(
            flops=2 * o.size * D, bytes_accessed=2 * (o.size + 2 * wo_a.size), transcendentals=0
        ),
        name="resid",
    )(core, o, wo_a, wo_b, x, g2)


def ffn_kernel(core_ref, m, gy, wgu_a, wgu_b, wd, hid_out, dgu_out, dm_out, wgu):
    ffl = wd.shape[0]

    @pl.when(pl.program_id(0) == 0)
    def _():
        core = core_ref[0]
        n = wgu_a.shape[1]
        for f in range(wgu_a.shape[0]):
            wgu[pl.ds(pl.multiple_of((2 * f + core) * n, n), n), :] = wgu_a[f]
            wgu[pl.ds(pl.multiple_of((2 * f + 1 - core) * n, n), n), :] = wgu_b[f]

    gu = dot_nn(m[0], wgu[...])
    dhid = dot_nt(gy[0], wd[...])
    gate, up = gu[:, :ffl], gu[:, ffl:]
    sig = 1.0 / (1.0 + jnp.exp(-gate))
    silu = gate * sig
    hid_out[0] = (silu * up).astype(BF)
    dgu_out[0, :, :ffl] = (dhid * up * (sig + silu * (1.0 - sig))).astype(BF)
    dgu_out[0, :, ffl:] = (dhid * silu).astype(BF)
    dm_out[0] = dot_nt(dgu_out[0], wgu[...]).astype(BF)


def ffn_call(core, m, gy, wgu_a, wgu_b, wd):
    F, T, D = m.shape
    ffl = wd.shape[0]
    step = lambda i: (i, 0, 0)
    const3 = lambda i: (0, 0, 0)
    return pl.pallas_call(
        ffn_kernel,
        out_shape=(
            jax.ShapeDtypeStruct((F, T, ffl), BF),
            jax.ShapeDtypeStruct((F, T, 2 * ffl), BF),
            jax.ShapeDtypeStruct((F, T, D), BF),
        ),
        grid=(F,),
        in_specs=[
            pl.BlockSpec(memory_space=pltpu.SMEM),
            pl.BlockSpec((1, T, D), step),
            pl.BlockSpec((1, T, D), step),
            pl.BlockSpec(wgu_a.shape, const3),
            pl.BlockSpec(wgu_b.shape, const3),
            pl.BlockSpec(wd.shape, lambda i: (0, 0)),
        ],
        out_specs=(
            pl.BlockSpec((1, T, ffl), step),
            pl.BlockSpec((1, T, 2 * ffl), step),
            pl.BlockSpec((1, T, D), step),
        ),
        scratch_shapes=[pltpu.VMEM((D, 2 * ffl), BF)],
        compiler_params=pltpu.CompilerParams(vmem_limit_bytes=VMEM_LIMIT),
        cost_estimate=pl.CostEstimate(
            flops=10 * F * T * D * ffl,
            bytes_accessed=2 * (3 * F * T * D + 3 * F * T * ffl + 3 * D * ffl),
            transcendentals=F * T * ffl,
        ),
        name="ffn",
    )(core, m, gy, wgu_a, wgu_b, wd)


def resid_back_kernel(core_ref, dm, h, gy, g2, wo_a, wo_b, dh_out, dhb_out, do_out, gain_out):
    core = core_ref[0]
    total = dm[0].astype(F32)
    for f in range(1, dm.shape[0]):
        total = total + dm[f].astype(F32)
    dv, terms = norm_back(h[...], g2[...], total)
    gain_out[...] = jnp.sum(terms, axis=0, keepdims=True)
    dh = gy[...].astype(F32) + dv
    dh_out[...] = dh
    low = dh.astype(BF)
    dhb_out[...] = low
    for f in range(wo_a.shape[0]):
        do_out[2 * f + core] = dot_nt(low, wo_a[f]).astype(BF)
        do_out[2 * f + 1 - core] = dot_nt(low, wo_b[f]).astype(BF)


def resid_back_call(core, dm, h, gy, g2, wo_a, wo_b):
    T, D = h.shape
    F, hw, _ = wo_a.shape
    smem = pl.BlockSpec(memory_space=pltpu.SMEM)
    vmem = pl.BlockSpec(memory_space=pltpu.VMEM)
    return pl.pallas_call(
        resid_back_kernel,
        out_shape=(
            jax.ShapeDtypeStruct((T, D), F32),
            jax.ShapeDtypeStruct((T, D), BF),
            jax.ShapeDtypeStruct((2 * F, T, hw), BF),
            jax.ShapeDtypeStruct((1, D), F32),
        ),
        in_specs=[smem] + [vmem] * 6,
        out_specs=(vmem,) * 4,
        compiler_params=pltpu.CompilerParams(vmem_limit_bytes=VMEM_LIMIT),
        cost_estimate=pl.CostEstimate(
            flops=200 * F * hw * T * D, bytes_accessed=4 * T * D * F + 4 * wo_a.size, transcendentals=0
        ),
        name="resid_bwd",
    )(core, dm, h, gy, g2, wo_a, wo_b)


LANE = 256


def pack_kernel(F, C, ggu, gd, out):
    R = ggu.shape[0] // (F * C)
    J = ggu.shape[1] // LANE
    for f in range(F):
        for c in range(C):
            for j in range(J):
                out[c, (f * J + j) * R : (f * J + j + 1) * R, :] = ggu[
                    (f * C + c) * R : (f * C + c + 1) * R, j * LANE : (j + 1) * LANE
                ]
    base = F * J * R
    n = gd.shape[0] // C
    for c in range(C):
        for j in range(gd.shape[1] // LANE):
            out[c, base + j * n : base + (j + 1) * n, :] = gd[
                c * n : (c + 1) * n, j * LANE : (j + 1) * LANE
            ]


def pack_call(ggu, gd, F, C):
    rows = (ggu.size + gd.size) // (C * LANE)
    return pl.pallas_call(
        functools.partial(pack_kernel, F, C),
        out_shape=jax.ShapeDtypeStruct((C, rows, LANE), BF),
        compiler_params=pltpu.CompilerParams(vmem_limit_bytes=VMEM_LIMIT),
        cost_estimate=pl.CostEstimate(
            flops=0, bytes_accessed=4 * (ggu.size + gd.size), transcendentals=0
        ),
        name="pack_ffn",
    )(ggu, gd)


def unpack_ffn_kernel(F, R, J, f_ref, src, gate_out, up_out, down_out):
    half = J // 2
    ffl = half * LANE
    for s in range(F):
        base = pl.multiple_of((f_ref[0] ^ s) * ffl, ffl)
        for j in range(J):
            (gate_out if j < half else up_out)[:, pl.ds(base + (j % half) * LANE, LANE)] = src[
                0, (s * J + j) * R : (s * J + j + 1) * R, :
            ].astype(F32)
    n, wide = down_out.shape
    for j in range(wide // LANE):
        at = F * J * R + j * n
        down_out[:, j * LANE : (j + 1) * LANE] = src[0, at : at + n, :].astype(F32)


def unpack_ffn_call(f_idx, src, F, R, FF, D):
    C, rows, _ = src.shape
    J = 2 * FF // (F * LANE)
    n = FF // (F * C)
    row = lambda c, f: (c, 0)
    return pl.pallas_call(
        functools.partial(unpack_ffn_kernel, F, R, J),
        out_shape=(
            jax.ShapeDtypeStruct((C * R, FF), F32),
            jax.ShapeDtypeStruct((C * R, FF), F32),
            jax.ShapeDtypeStruct((C * n, D), F32),
        ),
        grid_spec=pltpu.PrefetchScalarGridSpec(
            num_scalar_prefetch=1,
            grid=(C,),
            in_specs=[pl.BlockSpec((1, rows, LANE), lambda c, f: (c, 0, 0))],
            out_specs=(
                pl.BlockSpec((R, FF), row),
                pl.BlockSpec((R, FF), row),
                pl.BlockSpec((n, D), row),
            ),
        ),
        compiler_params=pltpu.CompilerParams(vmem_limit_bytes=VMEM_LIMIT),
        cost_estimate=pl.CostEstimate(flops=0, bytes_accessed=6 * src.size, transcendentals=0),
        name="unpack_ffn",
    )(f_idx, src)


def unpack_attn_kernel(heads, hd, rows, smalls, src, q_out, kv_out, small_out, o_out):
    for h in range(heads):
        q_out[:, h * hd : (h + 1) * hd] = src[0, h * rows : (h + 1) * rows, :].astype(F32)
    for h in range(2):
        at = (heads + h) * rows
        kv_out[h, 0] = src[0, at : at + rows, :].astype(F32)
    at = (heads + 2) * rows

    @pl.when(pl.program_id(0) == 0)
    def _():
        small_out[...] = jnp.zeros_like(small_out)

    small_out[...] += src[0, at : at + smalls, :].astype(F32)
    n, wide = o_out.shape
    for j in range(wide // hd):
        o_out[:, j * hd : (j + 1) * hd] = src[
            0, at + smalls + j * n : at + smalls + (j + 1) * n, :
        ].astype(F32)


def unpack_attn_call(src, heads, hd, rows, smalls, n_o, D):
    C, total, _ = src.shape
    return pl.pallas_call(
        functools.partial(unpack_attn_kernel, heads, hd, rows, smalls),
        out_shape=(
            jax.ShapeDtypeStruct((rows, C * heads * hd), F32),
            jax.ShapeDtypeStruct((2, C, rows, hd), F32),
            jax.ShapeDtypeStruct((smalls, hd), F32),
            jax.ShapeDtypeStruct((C * n_o, D), F32),
        ),
        grid=(C,),
        in_specs=[pl.BlockSpec((1, total, hd), lambda i: (i, 0, 0))],
        out_specs=(
            pl.BlockSpec((rows, heads * hd), lambda i: (0, i)),
            pl.BlockSpec((2, 1, rows, hd), lambda i: (0, i, 0, 0)),
            pl.BlockSpec((smalls, hd), lambda i: (0, 0)),
            pl.BlockSpec((n_o, D), lambda i: (i, 0)),
        ),
        compiler_params=pltpu.CompilerParams(vmem_limit_bytes=VMEM_LIMIT),
        cost_estimate=pl.CostEstimate(flops=0, bytes_accessed=6 * src.size, transcendentals=0),
        name="unpack_attn",
    )(src)


def split_low(values):
    high = values.astype(BF)
    return high, (values - high.astype(F32)).astype(BF)


def after(value, *others):
    return lax.optimization_barrier((value,) + others)[0]


def body(
    block_input,
    cotangent,
    seq_lengths,
    block_table,
    query_proj,
    key_proj,
    value_proj,
    output_proj,
    gate_proj,
    up_proj,
    down_proj,
    attn_norm,
    ffn_norm,
    query_norm,
    key_norm,
):
    C = lax.axis_size("ctx")
    F = lax.axis_size("fsdp")
    c_idx = lax.axis_index("ctx")
    f_idx = lax.axis_index("fsdp")
    core = lax.rem(c_idx, 2)
    core_ref = core[None].astype(jnp.int32)
    T, D = block_input.shape[1:]
    S = T * C
    blocks = block_table.shape[0]
    blk = S // blocks
    hd = query_norm.shape[0] * F
    HQ = query_proj.shape[1] // hd
    KV = key_proj.shape[1] // hd
    FF = gate_proj.shape[1]
    heads = HQ // C
    rep = max(1, C // KV)
    FFl = FF // F
    R = D // (F * C)
    scale = 1.0 / math.sqrt(hd)
    length = seq_lengths.astype(jnp.int32)
    own_blocks = lax.dynamic_slice_in_dim(block_table, c_idx * (blocks // C), blocks // C)
    own_pos = (own_blocks[:, None] * blk + jnp.arange(blk, dtype=jnp.int32)[None, :]).reshape(-1)
    live = (own_pos < length[0]).astype(F32)[:, None]
    order = jnp.argsort(block_table).astype(jnp.int32)

    def gather_f(v):
        return lax.all_to_all(jnp.broadcast_to(v[None], (F,) + v.shape), "fsdp", 0, 0)

    def exchange_f(v):
        return lax.all_to_all(v, "fsdp", 0, 0)

    def exchange_c(v):
        return lax.all_to_all(v, "ctx", 0, 0)

    def to_partner(v, s):
        return lax.ppermute(v, "fsdp", [(i, i ^ s) for i in range(F)])

    def gather_x(v):
        return jnp.stack([v] + [to_partner(v, s) for s in range(1, F)])

    def exchange_x(v):
        pick = lambda s: lax.dynamic_index_in_dim(v, f_idx ^ s, 0, keepdims=False)
        return jnp.stack([pick(0)] + [to_partner(pick(s), s) for s in range(1, F)])

    def other_core(v):
        return lax.ppermute(v, "ctx", [(i, i ^ 1) for i in range(C)])

    x_all = lax.all_gather(block_input[0], "ctx", axis=0, tiled=True)
    kv_at = (c_idx // rep) * hd
    w_own = jnp.concatenate(
        [
            lax.dynamic_slice_in_dim(query_proj, c_idx * heads * hd, heads * hd, 1),
            lax.dynamic_slice_in_dim(key_proj, kv_at, hd, 1),
            lax.dynamic_slice_in_dim(value_proj, kv_at, hd, 1),
        ],
        axis=1,
    ).astype(BF)
    cols = (heads + 2) * hd
    gains_own = jnp.concatenate([attn_norm, ffn_norm, query_norm, key_norm]).astype(BF)
    gain_rows = -(-gains_own.shape[0] // (16 * cols)) * 16
    gains_own = jnp.pad(gains_own, (0, gain_rows * cols - gains_own.shape[0]))
    moved = gather_f(jnp.concatenate([w_own, gains_own.reshape(gain_rows, cols)], axis=0))
    w_heads = moved[:, : D // F].reshape(D, cols)
    gains = moved[:, D // F :].reshape(F, gain_rows * cols).astype(F32)
    g1 = gains[:, : D // F].reshape(1, D)
    g2 = gains[:, D // F : 2 * D // F].reshape(1, D)
    gq = gains[:, 2 * D // F : (2 * D + hd) // F].reshape(1, hd)
    gk = gains[:, (2 * D + hd) // F : (2 * D + 2 * hd) // F].reshape(1, hd)
    gy = (cotangent[0].astype(F32) * live).astype(BF)
    gy_all = lax.all_gather(after(gy, x_all), "fsdp", axis=0)
    wo_rows = output_proj.shape[0] // 2
    wo_half = lax.dynamic_slice_in_dim(output_proj, core * wo_rows, wo_rows, 0).astype(BF)
    wo_a = gather_f(after(wo_half, moved))
    wo_b = other_core(wo_a)
    gu_rows = D // F // 2
    half_of = lambda w: lax.dynamic_slice_in_dim(w, core * gu_rows, gu_rows, 0).astype(BF)
    wgu_half = jnp.concatenate(
        [half_of(gate_proj).reshape(gu_rows, F, FFl), half_of(up_proj).reshape(gu_rows, F, FFl)],
        axis=2,
    )
    wgu_a = exchange_f(after(jnp.swapaxes(wgu_half, 0, 1), wo_a))
    wgu_b = other_core(wgu_a)
    wd = down_proj.astype(BF)

    half = hd // 2
    frequency = THETA ** (-(jnp.arange(half).astype(F32) * 2.0 / hd))
    angles = jnp.arange(S, dtype=jnp.int32).astype(F32)[:, None] * frequency[None, :]
    cos_t, sin_t = jnp.cos(angles), jnp.sin(angles)
    cos_t = jnp.concatenate([cos_t, cos_t], -1)
    sin_t = jnp.concatenate([-sin_t, sin_t], -1)
    a_s, raw, low = qkv_call(order, after(x_all, wo_a), g1, w_heads, gq, gk, cos_t, sin_t, heads, hd, blk)
    o_st, o32, lse = attn_call(order, length, low, heads, hd, blk, scale)
    o_nat = exchange_c(after(o_st, wgu_a).reshape(C, T, heads * hd))
    x = block_input[0]
    h, m_own = resid_call(core_ref, o_nat, wo_a, wo_b, x, g2)

    m = gather_f(m_own)
    o_f = exchange_x(after(o_nat.reshape(F, C // F, T, heads * hd), m))
    hidden, dgu, dm_part = ffn_call(core_ref, m, gy_all, wgu_a, wgu_b, wd)
    dm_parts = exchange_f(dm_part)
    dh, dhb, do_nat, ffn_gain = resid_back_call(core_ref, dm_parts, h, gy, g2, wo_a, wo_b)
    m, gy_all = m.reshape(F * T, D), gy_all.reshape(F * T, D)
    hidden, dgu = hidden.reshape(F * T, FFl), dgu.reshape(F * T, 2 * FFl)

    ggu = dot_tn(m, dgu).astype(BF)
    gd = dot_tn(hidden, gy_all).astype(BF)
    packed = pack_call(ggu, gd, F, C)
    owned = lax.psum_scatter(packed.reshape(-1, LANE), "ctx", scatter_dimension=0, tiled=True)
    n_gu = F * (2 * FFl // LANE) * R

    do_st = exchange_c(do_nat).reshape(S, heads * hd)
    dhb_all = gather_x(dhb)
    owned_gu = exchange_x(owned[:n_gu].reshape(F, -1, LANE)).reshape(n_gu, LANE)
    all_ffn = lax.all_gather(jnp.concatenate([owned_gu, owned[n_gu:]], axis=0), "ctx", axis=0)
    dq, dkv = attn_back_call(order, length, low, do_st, o32, lse, heads, hd, blk, scale)
    go = jnp.einsum("sctd,stn->cdn", o_f, dhb_all, preferred_element_type=F32)
    go = go.astype(BF).reshape(C, -1, D)
    n_o = go.shape[1]
    send, dqkv, head_gains, attn_gain = head_back_call(
        order, x_all, after(dq, all_ffn), dkv, raw, w_heads, go, gq, gk, cos_t, sin_t, heads, hd, blk, C
    )
    summed = lax.psum_scatter(send.reshape(-1, D), "ctx", scatter_dimension=0, tiled=True)
    da = summed[:T].astype(F32)
    dx, _ = norm_back(x.astype(F32), g1, da)
    grad_input = (dh + dx)[None]

    grad_gate, grad_up, grad_down = unpack_ffn_call(
        f_idx[None].astype(jnp.int32), all_ffn, F, R, FF, D
    )

    per_f = lambda v: v.reshape(F, -1)
    small = jnp.concatenate(
        [
            per_f(attn_gain),
            per_f(ffn_gain),
            per_f(head_gains[0]),
            per_f(head_gains[1]),
        ],
        axis=1,
    )
    n_small = small.shape[1]
    small_rows = -(-n_small // hd)
    smalls = -(-2 * small_rows // 16) * 16

    def small_block(values):
        values = jnp.pad(values, ((0, 0), (0, small_rows * hd - n_small)))
        high, low_part = split_low(values.reshape(-1, small_rows, hd))
        both = jnp.concatenate([high, low_part], axis=1)
        return jnp.pad(both, ((0, 0), (0, smalls - 2 * small_rows), (0, 0)))

    def small_values(block):
        both = block.astype(F32)
        both = both[..., :small_rows, :] + both[..., small_rows : 2 * small_rows, :]
        return both.reshape(both.shape[:-2] + (small_rows * hd,))[..., :n_small]

    gqkv = dot_tn(a_s, dqkv).astype(BF).reshape(F, D // F, heads + 2, hd)
    gqkv = jnp.swapaxes(gqkv, 1, 2).reshape(F, -1, hd)
    parts = exchange_f(jnp.concatenate([gqkv, small_block(small)], axis=1))
    n_p = gqkv.shape[1]
    own_p = jnp.sum(parts[:, :n_p].astype(F32), axis=0).astype(BF)
    own_s = small_block(jnp.sum(small_values(parts[:, n_p:]), axis=0, keepdims=True))[0]
    own_o = jnp.swapaxes(summed[T:].reshape(n_o, D // hd, hd), 0, 1).reshape(-1, hd)
    all_attn = lax.all_gather(jnp.concatenate([own_p, own_s, own_o], axis=0), "ctx", axis=0)
    grad_query, gkv, small_sum, grad_output = unpack_attn_call(
        all_attn, heads, hd, D // F, smalls, n_o, D
    )
    gkv = jnp.sum(gkv.reshape(2, C // rep, rep, D // F, hd), axis=2)
    gkv = jnp.swapaxes(gkv, 1, 2).reshape(2, D // F, KV * hd)
    small_sum = small_values(small_sum)
    d_f, h_f = D // F, hd // F

    ffn_part = dot_nn(hidden, wd).astype(BF).reshape(F, T, D)
    ffn = jnp.sum(exchange_x(ffn_part).astype(F32), axis=0)
    block_output = ((h + ffn) * live).astype(BF)[None]
    return (
        block_output,
        grad_input,
        grad_query,
        gkv[0],
        gkv[1],
        grad_output,
        grad_gate,
        grad_up,
        grad_down,
        small_sum[:d_f],
        small_sum[d_f : 2 * d_f],
        small_sum[2 * d_f : 2 * d_f + h_f],
        small_sum[2 * d_f + h_f :],
    )


def solution(mesh):
    matrix, vector = P("fsdp", None), P("fsdp")
    rows = P("fsdp", "ctx", None)
    in_specs = (rows, rows, vector, P()) + (matrix,) * 7 + (vector,) * 4
    out_specs = (rows, rows) + (matrix,) * 7 + (vector,) * 4
    return jax.shard_map(body, mesh=mesh, in_specs=in_specs, out_specs=out_specs, check_vma=False)
```

```python
import functools
import math

import jax
import jax.numpy as jnp
from jax import lax
from jax.experimental import pallas as pl
from jax.experimental.pallas import tpu as pltpu
from jax.sharding import PartitionSpec as P

EPS = 1e-06
THETA = 1000000.0
BF = jnp.bfloat16
F32 = jnp.float32
LOG2E = math.log2(math.e)
VMEM_LIMIT = 56 * 1024 * 1024


def dot_nn(left, right):
    return lax.dot_general(left, right, (((1,), (0,)), ((), ())), preferred_element_type=F32)


def dot_nt(left, right):
    return lax.dot_general(left, right, (((1,), (1,)), ((), ())), preferred_element_type=F32)


def dot_tn(left, right):
    return lax.dot_general(left, right, (((0,), (0,)), ((), ())), preferred_element_type=F32)


def norm_back(values, gain_vec, upstream_grad):
    inverse = lax.rsqrt(jnp.mean(values * values, axis=-1, keepdims=True) + EPS)
    normed = values * inverse
    gain_terms = upstream_grad * normed
    gained = upstream_grad * gain_vec
    grad_values = inverse * (gained - normed * jnp.mean(gained * normed, axis=-1, keepdims=True))
    return (grad_values, gain_terms)


def params():
    return pltpu.CompilerParams(vmem_limit_bytes=VMEM_LIMIT)


def cost(us, moved=0):
    return pl.CostEstimate(flops=int(us * 1.15e9), bytes_accessed=int(moved), transcendentals=0)


SMEM = pl.BlockSpec(memory_space=pltpu.SMEM)
VMEM = pl.BlockSpec(memory_space=pltpu.VMEM)


def like(shape, dtype):
    return jax.ShapeDtypeStruct(tuple(shape), dtype)


def qkv_kernel(parts, heads, hd, order, *refs):
    x_refs = refs[:parts]
    gain, weight, gq, gk, cos, sin, raw_out, low_out = refs[parts:]
    x = jnp.concatenate([r[...] for r in x_refs], axis=0).astype(F32)
    a = (x * lax.rsqrt(jnp.mean(x * x, axis=-1, keepdims=True) + EPS) * gain[...]).astype(BF)
    raw = dot_nn(a, weight[...])
    c, s = cos[...], sin[...]
    for h in range(heads + 1):
        u = raw[:, h * hd : (h + 1) * hd]
        raw_out[:, h * hd : (h + 1) * hd] = u
        g = gq[...] if h < heads else gk[...]
        n = u * lax.rsqrt(jnp.mean(u * u, axis=-1, keepdims=True) + EPS) * g
        low_out[:, h * hd : (h + 1) * hd] = (n * c + pltpu.roll(n, hd // 2, axis=1) * s).astype(BF)
    low_out[:, (heads + 1) * hd :] = raw[:, (heads + 1) * hd :].astype(BF)


def block_specs(parts, blk, width):
    return [
        pl.BlockSpec((blk, width), functools.partial(lambda k, i, o: (o[parts * i + k], 0), k))
        for k in range(parts)
    ]


def qkv_call(order, x_all, gain, weight, gq, gk, cos, sin, heads, hd, blk):
    total, width = x_all.shape
    cols = weight.shape[1]
    parts = 4
    step = parts * blk
    const = lambda i, o: (0, 0)
    rows = lambda i, o: (i, 0)
    return pl.pallas_call(
        functools.partial(qkv_kernel, parts, heads, hd),
        out_shape=(like((total, (heads + 1) * hd), F32), like((total, cols), BF)),
        grid_spec=pltpu.PrefetchScalarGridSpec(
            num_scalar_prefetch=1,
            grid=(total // step,),
            in_specs=block_specs(parts, blk, width)
            + [
                pl.BlockSpec((1, width), const),
                pl.BlockSpec(weight.shape, const),
                pl.BlockSpec((1, hd), const),
                pl.BlockSpec((1, hd), const),
                pl.BlockSpec((step, hd), rows),
                pl.BlockSpec((step, hd), rows),
            ],
            out_specs=(
                pl.BlockSpec((step, (heads + 1) * hd), rows),
                pl.BlockSpec((step, cols), rows),
            ),
        ),
        compiler_params=params(),
        cost_estimate=cost(40),
        name="qkv",
    )(order, *([x_all] * parts), gain, weight, gq, gk, cos, sin)


TQ, TK = 512, 512


def stack_heads(ref, start, heads, hd):
    return jnp.concatenate(
        [ref[pl.ds(start, TQ), h * hd : (h + 1) * hd] for h in range(heads)], axis=0
    )


def attn_kernel(heads, hd, blk, scale, order, length_ref, low, o_even, o_odd, o32_out, lse_out, vext, acc):
    total = low.shape[0]
    length = length_ref[0]
    kcol, vcol = heads * hd, (heads + 1) * hd
    rows = heads * TQ
    vext[:, :hd] = low[:, vcol : vcol + hd]
    vext[:, hd:] = jnp.ones((total, hd), BF)
    full = length // TK
    ends = pl.cdiv(length, TK)

    @pl.loop(0, total // TQ)
    def _(i):
        qs = pl.multiple_of(i * TQ, TQ)
        q = stack_heads(low, qs, heads, hd)
        acc[...] = jnp.zeros_like(acc)

        def tile(j, masked):
            ks = pl.multiple_of(j * TK, TK)
            s = dot_nt(q, low[pl.ds(ks, TK), kcol : kcol + hd])
            p = jnp.exp2(s * (scale * LOG2E))
            if masked:
                kpos = ks + lax.broadcasted_iota(jnp.int32, (rows, TK), 1)
                qpos = qs + lax.broadcasted_iota(jnp.int32, (rows, TK), 0) % TQ
                p = jnp.where((kpos <= qpos) & (kpos < length), p, 0.0)
            acc[...] += dot_nn(p.astype(BF), vext[pl.ds(ks, TK), :])

        clean = jnp.minimum(qs // TK, full)

        @pl.loop(0, clean)
        def _(j):
            tile(j, False)

        @pl.loop(clean, jnp.minimum((qs + TQ - 1) // TK + 1, ends))
        def _(j):
            tile(j, True)

        total_p = acc[:, hd:]
        o = acc[:, :hd] / total_p
        lse_out[i] = jnp.log2(total_p.T[:8])
        for h in range(heads):
            cut = slice(h * hd, (h + 1) * hd)
            part = o[h * TQ : (h + 1) * TQ]
            o32_out[pl.ds(qs, TQ), cut] = part
            for b in range(TQ // blk):
                at = order[i * (TQ // blk) + b]
                low_part = part[b * blk : (b + 1) * blk].astype(BF)

                @pl.when(at % 2 == 0)
                def _():
                    o_even[at // 2, :, cut] = low_part

                @pl.when(at % 2 == 1)
                def _():
                    o_odd[at // 2, :, cut] = low_part


def attn_call(order, length, low, heads, hd, blk, scale):
    total = low.shape[0]
    half = like((total // (2 * blk), blk, heads * hd), BF)
    return pl.pallas_call(
        functools.partial(attn_kernel, heads, hd, blk, scale),
        out_shape=(
            half,
            half,
            like((total, heads * hd), F32),
            like((total // TQ, 8, heads * TQ), F32),
        ),
        in_specs=[SMEM, SMEM, VMEM],
        out_specs=(VMEM,) * 4,
        scratch_shapes=[
            pltpu.VMEM((total, 2 * hd), BF),
            pltpu.VMEM((heads * TQ, 2 * hd), F32),
        ],
        compiler_params=params(),
        cost_estimate=cost(40),
        name="attn_fwd",
    )(order, length, low)


def attn_back_kernel(
    heads, hd, blk, scale, order, length_ref, low, do_even, do_odd, o32, lse, dq_out, dkv_out,
    do_s, delta, dkv,
):
    total = low.shape[0]
    tiles = total // TQ
    length = length_ref[0]
    kcol, vcol = heads * hd, (heads + 1) * hd
    rows = heads * TQ

    @pl.loop(0, tiles)
    def _(i):
        qs = pl.multiple_of(i * TQ, TQ)
        for b in range(TQ // blk):
            at = order[i * (TQ // blk) + b]

            @pl.when(at % 2 == 0)
            def _():
                do_s[pl.ds(qs + b * blk, blk), :] = do_even[at // 2]

            @pl.when(at % 2 == 1)
            def _():
                do_s[pl.ds(qs + b * blk, blk), :] = do_odd[at // 2]

        do_t = stack_heads(do_s, qs, heads, hd).astype(F32) * stack_heads(o32, qs, heads, hd)
        delta[i] = jnp.broadcast_to(jnp.sum(do_t.T, axis=0, keepdims=True), (8, rows))
        dq_out[pl.ds(qs, TQ), :] = jnp.zeros((TQ, heads * hd), F32)

    full = length // TK

    @pl.loop(0, total // TK)
    def _(j):
        ks = pl.multiple_of(j * TK, TK)
        k = low[pl.ds(ks, TK), kcol : kcol + hd]
        v = low[pl.ds(ks, TK), vcol : vcol + hd]
        dkv[...] = jnp.zeros_like(dkv)

        def tile(i, masked):
            qs = pl.multiple_of(i * TQ, TQ)
            q = stack_heads(low, qs, heads, hd)
            do = stack_heads(do_s, qs, heads, hd)
            s = dot_nt(k, q)
            p = jnp.exp2(s * (scale * LOG2E) - lse[i][:1])
            if masked:
                kpos = ks + lax.broadcasted_iota(jnp.int32, (TK, rows), 0)
                qpos = qs + lax.broadcasted_iota(jnp.int32, (TK, rows), 1) % TQ
                p = jnp.where((kpos <= qpos) & (kpos < length), p, 0.0)
            dp = dot_nt(v, do)
            ds = (p * (dp - delta[i][:1])).astype(BF)
            dkv[:, :hd] += dot_nn(ds, q)
            dkv[:, hd:] += dot_nn(p.astype(BF), do)
            dq = dot_tn(ds, k)
            for h in range(heads):
                dq_out[pl.ds(qs, TQ), h * hd : (h + 1) * hd] += dq[h * TQ : (h + 1) * TQ]

        first = ks // TQ
        masked_end = jnp.where(j < full, (ks + TK - 1) // TQ + 1, tiles)

        @pl.loop(first, masked_end)
        def _(i):
            tile(i, True)

        @pl.loop(masked_end, tiles)
        def _(i):
            tile(i, False)

        dkv_out[pl.ds(ks, TK), :hd] = dkv[:, :hd]
        dkv_out[pl.ds(ks, TK), hd:] = dkv[:, hd:]


def attn_back_call(order, length, low, do_even, do_odd, o32, lse, heads, hd, blk, scale):
    total = low.shape[0]
    return pl.pallas_call(
        functools.partial(attn_back_kernel, heads, hd, blk, scale),
        out_shape=(like((total, heads * hd), F32), like((total, 2 * hd), F32)),
        in_specs=[SMEM, SMEM] + [VMEM] * 5,
        out_specs=(VMEM, VMEM),
        scratch_shapes=[
            pltpu.VMEM((total, heads * hd), BF),
            pltpu.VMEM((total // TQ, 8, heads * TQ), F32),
            pltpu.VMEM((TK, 2 * hd), F32),
        ],
        compiler_params=params(),
        cost_estimate=cost(300),
        name="attn_bwd",
    )(order, length, low, do_even, do_odd, o32, lse)


def split_low(values):
    high = values.astype(BF)
    return high, (values - high.astype(F32)).astype(BF)


def head_back_kernel(parts, blk, heads, hd, F, scale, order, f_ref, *refs):
    x_refs = refs[:parts]
    dq, dkv, raw, weight, go, gain, gq, gk, fg0, fg1, cos, sin = refs[parts : parts + 12]
    send_out = refs[parts + 12]
    grad_outs = refs[parts + 13 : parts + 13 + F]
    grad_acc, gain_acc, attn_acc = refs[parts + 13 + F :]
    i = pl.program_id(0)

    @pl.when(i == 0)
    def _():
        grad_acc[...] = jnp.zeros_like(grad_acc)
        gain_acc[...] = jnp.zeros_like(gain_acc)
        attn_acc[...] = jnp.zeros_like(attn_acc)
        rows_own = send_out.shape[1] - go.shape[1]
        for c in range(go.shape[0]):
            send_out[c, rows_own:, :] = go[c]

    c, s = cos[...] * scale, sin[...] * scale
    pieces = []
    for h in range(heads + 1):
        cut = slice(h * hd, (h + 1) * hd)
        g_rot = dq[:, cut] if h < heads else dkv[:, :hd]
        e = g_rot * c + pltpu.roll(g_rot * s, hd // 2, axis=1)
        dv, terms = norm_back(raw[:, cut], gq[...] if h < heads else gk[...], e)
        pieces.append(dv.astype(BF))
        row = 0 if h < heads else 1
        gain_acc[row : row + 1, :] += jnp.sum(terms, axis=0, keepdims=True)
    pieces.append(dkv[:, hd:].astype(BF))
    dqkv = jnp.concatenate(pieces, axis=1)
    da = dot_nt(dqkv, weight[...])
    per = (send_out.shape[1] - go.shape[1]) // blk
    normed_parts = []
    for k in range(parts):
        x = x_refs[k][...].astype(F32)
        part = da[k * blk : (k + 1) * blk]
        normed = x * lax.rsqrt(jnp.mean(x * x, axis=-1, keepdims=True) + EPS)
        normed_parts.append((normed * gain[...]).astype(BF))
        attn_acc[...] += jnp.sum(part * normed, axis=0, keepdims=True)
        at = order[parts * i + k]
        send_out[at // per, pl.ds(pl.multiple_of((at % per) * blk, blk), blk), :] = part.astype(BF)
    grad_acc[...] += dot_tn(jnp.concatenate(normed_parts, axis=0), dqkv)

    @pl.when(i == pl.num_programs(0) - 1)
    def _():
        n = grad_acc.shape[0] // F
        for s_ in range(F):
            f = f_ref[0] ^ s_
            at = pl.multiple_of(f * n, n)
            out = grad_outs[s_]
            for b in range(heads + 2):
                out[b * n : (b + 1) * n, :] = grad_acc[
                    pl.ds(at, n), b * hd : (b + 1) * hd
                ].astype(BF)
            base = (heads + 2) * n
            rows = []
            for r in range(n // hd):
                rows.append(attn_acc[:, pl.ds(pl.multiple_of(at + r * hd, hd), hd)])
            for r in range(n // hd):
                lane = pl.ds(pl.multiple_of(at + r * hd, hd), hd)
                rows.append(fg0[:, lane] + fg1[:, lane])
            rows += [gain_acc[0:1, :], gain_acc[1:2, :]]
            rows += [jnp.zeros((1, hd), F32)] * (8 - len(rows))
            high, low = split_low(jnp.concatenate(rows, axis=0))
            out[base : base + 16, :] = jnp.concatenate([high, low], axis=0)


def head_back_call(
    order, f_idx, x_all, dq, dkv, raw, weight, go, gain, gq, gk, fgains, cos, sin, heads, hd, blk, F
):
    total = dq.shape[0]
    width, cols = weight.shape
    parts = 4
    step = parts * blk
    ctx = go.shape[0]
    const = lambda i, o: (0, 0)
    const3 = lambda i, o: (0, 0, 0)
    rows = lambda i, o: (i, 0)
    send = (ctx, total // ctx + go.shape[1], width)
    grad = ((heads + 2) * (width // F) + 16, hd)
    return pl.pallas_call(
        functools.partial(head_back_kernel, parts, blk, heads, hd, F, hd**-0.5),
        out_shape=(like(send, BF),) + (like(grad, BF),) * F,
        grid_spec=pltpu.PrefetchScalarGridSpec(
            num_scalar_prefetch=1,
            grid=(total // step,),
            in_specs=[SMEM]
            + block_specs(parts, blk, width)
            + [
                pl.BlockSpec((step, heads * hd), rows),
                pl.BlockSpec((step, 2 * hd), rows),
                pl.BlockSpec((step, (heads + 1) * hd), rows),
                pl.BlockSpec(weight.shape, const),
                pl.BlockSpec(go.shape, const3),
                pl.BlockSpec((1, width), const),
                pl.BlockSpec((1, hd), const),
                pl.BlockSpec((1, hd), const),
                pl.BlockSpec((1, width), const),
                pl.BlockSpec((1, width), const),
                pl.BlockSpec((step, hd), rows),
                pl.BlockSpec((step, hd), rows),
            ],
            out_specs=(pl.BlockSpec(send, const3),) + (pl.BlockSpec(grad, const),) * F,
            scratch_shapes=[
                pltpu.VMEM((width, cols), F32),
                pltpu.VMEM((8, hd), F32),
                pltpu.VMEM((1, width), F32),
            ],
        ),
        compiler_params=params(),
        cost_estimate=cost(60),
        name="head_bwd",
    )(
        order, f_idx, *([x_all] * parts), dq, dkv, raw, weight, go, gain, gq, gk, *fgains, cos, sin
    )


def heads_at(c_ref, f, part):
    return 2 * f + ((c_ref[0] % 2) ^ part)


def resid_kernel(F, f_ref, c_ref, o, wo_a, wo_b, x, g2, h_out, m_out, *o_outs):
    n = wo_a.shape[1] // 2
    half = wo_a.shape[2]
    left, right = x[:, :half].astype(F32), x[:, half:].astype(F32)
    for part, wo in enumerate((wo_a, wo_b)):
        for f in range(F):
            of = o[heads_at(c_ref, f, part)]
            left = left + dot_nn(of, wo[f, :n])
            right = right + dot_nn(of, wo[f, n : 2 * n])
    h = jnp.concatenate([left, right], axis=1)
    h_out[...] = h
    m_out[...] = (h * lax.rsqrt(jnp.mean(h * h, axis=-1, keepdims=True) + EPS) * g2[...]).astype(BF)
    for s in range(F):
        for r in range(2):
            o_outs[s][r] = o[(f_ref[0] ^ s) * 2 + r]


def wo_specs(wo_a, wo_b):
    const3 = lambda i: (0, 0, 0)
    return [pl.BlockSpec(wo_b.shape, const3), pl.BlockSpec(wo_b.shape, const3)]


def resid_call(half, f_idx, c_idx, o, wo_a, wo_b, x, g2):
    C, T, hw = o.shape
    D = x.shape[1]
    F = wo_b.shape[0]
    part = like((2, T, hw), BF)
    const = lambda i: (0, 0)
    const3 = lambda i: (0, 0, 0)
    return pl.pallas_call(
        functools.partial(resid_kernel, F),
        out_shape=(like((T, D), F32), like((T, D), BF)) + (part,) * F,
        grid=(1,),
        in_specs=[SMEM, SMEM, pl.BlockSpec(o.shape, const3)]
        + wo_specs(wo_a, wo_b)
        + [pl.BlockSpec((T, D), lambda i: (half, 0)), pl.BlockSpec(g2.shape, const)],
        out_specs=(pl.BlockSpec((T, D), const),) * 2 + (pl.BlockSpec(part.shape, const3),) * F,
        compiler_params=params(),
        cost_estimate=cost(10),
        name="resid",
    )(f_idx, c_idx, o, wo_a, wo_b, x, g2)


def ffn_kernel(F, *refs):
    ms, gys = refs[1 : 1 + F], refs[1 + F : 1 + 2 * F]
    wgu, wd, hid_out, dgu_out = refs[1 + 2 * F : 5 + 2 * F]
    dm_outs = refs[5 + 2 * F :]
    ffl = wd.shape[0]
    T = ms[0].shape[0]
    m = jnp.concatenate([r[...] for r in ms], axis=0)
    gy = jnp.concatenate([r[...] for r in gys], axis=0)
    gu = dot_nn(m, wgu[...])
    dhid = dot_nt(gy, wd[...])
    gate, up = gu[:, :ffl], gu[:, ffl:]
    sig = 1.0 / (1.0 + jnp.exp(-gate))
    silu = gate * sig
    hid_out[...] = (silu * up).astype(BF)
    dgu = jnp.concatenate(
        [(dhid * up * (sig + silu * (1.0 - sig))).astype(BF), (dhid * silu).astype(BF)], axis=1
    )
    dgu_out[...] = dgu
    dm = dot_nt(dgu, wgu[...]).astype(BF)
    for s in range(F):
        dm_outs[s][...] = dm[s * T : (s + 1) * T]


def gy_spec(T, D, half):
    return pl.BlockSpec((T, D), lambda i, f: (half, 0))


def ffn_call(half, f_idx, ms, gys, wgu, wd):
    F = len(ms)
    T, D = ms[0].shape
    ffl = wd.shape[0]
    const = lambda i, f: (0, 0)
    return pl.pallas_call(
        functools.partial(ffn_kernel, F),
        out_shape=(like((F * T, ffl), BF), like((F * T, 2 * ffl), BF)) + (like((T, D), BF),) * F,
        grid_spec=pltpu.PrefetchScalarGridSpec(
            num_scalar_prefetch=1,
            grid=(1,),
            in_specs=[pl.BlockSpec((T, D), const)] * F
            + [gy_spec(T, D, half)] * F
            + [pl.BlockSpec(wgu.shape, const), pl.BlockSpec(wd.shape, const)],
            out_specs=(
                pl.BlockSpec((F * T, ffl), const),
                pl.BlockSpec((F * T, 2 * ffl), const),
            )
            + (pl.BlockSpec((T, D), const),) * F,
        ),
        compiler_params=params(),
        cost_estimate=cost(10),
        name="ffn",
    )(f_idx, *ms, *gys, wgu, wd)


def resid_back_kernel(F, c_ref, *refs):
    dms = refs[:F]
    wo_a, wo_b, h, gy, g2, dh_out, dhb_out, do_out, gain_out = refs[F:]
    total = dms[0][...].astype(F32)
    for s in range(1, F):
        total = total + dms[s][...].astype(F32)
    dv, terms = norm_back(h[...], g2[...], total)
    gain_out[...] = jnp.sum(terms, axis=0, keepdims=True)
    dh = gy[...].astype(F32) + dv
    dh_out[...] = dh
    low = dh.astype(BF)
    dhb_out[...] = low
    n = wo_a.shape[1] // 2
    half = wo_a.shape[2]
    for part, wo in enumerate((wo_a, wo_b)):
        for f in range(F):
            do = dot_nt(low[:, :half], wo[f, :n]) + dot_nt(low[:, half:], wo[f, n : 2 * n])
            do_out[heads_at(c_ref, f, part)] = do.astype(BF)


def resid_back_call(half, c_idx, dms, h, gy, g2, wo_a, wo_b):
    F = len(dms)
    T, D = h.shape
    hw = wo_b.shape[1] // 2
    const = lambda i: (0, 0)
    return pl.pallas_call(
        functools.partial(resid_back_kernel, F),
        out_shape=(
            like((T, D), F32),
            like((T, D), BF),
            like((2 * F, T, hw), BF),
            like((1, D), F32),
        ),
        grid=(1,),
        in_specs=[SMEM]
        + [pl.BlockSpec((T, D), const)] * F
        + wo_specs(wo_a, wo_b)
        + [
            pl.BlockSpec((T, D), const),
            pl.BlockSpec((T, D), lambda i: (half, 0)),
            pl.BlockSpec(g2.shape, const),
        ],
        out_specs=(
            pl.BlockSpec((T, D), const),
            pl.BlockSpec((T, D), const),
            pl.BlockSpec((2 * F, T, hw), lambda i: (0, 0, 0)),
            pl.BlockSpec((1, D), const),
        ),
        compiler_params=params(),
        cost_estimate=cost(10),
        name="resid_bwd",
    )(c_idx, *dms, wo_a, wo_b, h, gy, g2)


def rows_kernel(c_ref, a, b, out):
    n = a.shape[1]
    for part, src in enumerate((a, b)):
        for f in range(src.shape[0]):
            at = pl.multiple_of(heads_at(c_ref, f, part) * n, n)
            out[pl.ds(at, n), :] = src[f]


def rows_call(c_idx, a, b):
    F, n, wide = a.shape
    return pl.pallas_call(
        rows_kernel,
        out_shape=like((2 * F * n, wide), BF),
        in_specs=[SMEM, VMEM, VMEM],
        out_specs=VMEM,
        compiler_params=params(),
        cost_estimate=cost(4),
        name="weight_rows",
    )(c_idx, a, b)


LANE = 256


def wgrad_kernel(F, C, f_ref, *refs):
    ms, gys = refs[: 2 * F], refs[2 * F : 4 * F]
    hid0, hid1, dgu0, dgu1, out, dgu, gd = refs[4 * F :]
    D = ms[0].shape[1]
    n = D // F
    R = n // C
    J = dgu0.shape[1] // LANE
    half = dgu0.shape[0]
    dgu[:half, :] = dgu0[...]
    dgu[half:, :] = dgu1[...]
    for s in range(F):
        lane = pl.ds(pl.multiple_of((f_ref[0] ^ s) * n, n), n)
        lhs = jnp.concatenate([r[:, lane] for r in ms], axis=0)
        res = dot_tn(lhs, dgu[...]).astype(BF)
        for c in range(C):
            for j in range(J):
                out[c, (s * J + j) * R : (s * J + j + 1) * R, :] = res[
                    c * R : (c + 1) * R, j * LANE : (j + 1) * LANE
                ]
    hid = jnp.concatenate([hid0[...], hid1[...]], axis=0)
    gy = jnp.concatenate([r[...] for r in gys], axis=0)
    gd[...] = dot_tn(hid, gy).astype(BF)
    base = F * J * R
    n = gd.shape[0] // C
    for c in range(C):
        for j in range(D // LANE):
            out[c, base + j * n : base + (j + 1) * n, :] = gd[
                c * n : (c + 1) * n, j * LANE : (j + 1) * LANE
            ]


def wgrad_call(f_idx, ms, gys, hiddens, dgus, C):
    F = len(ms) // 2
    T, D = ms[0].shape
    rows, ffl = hiddens[0].shape
    total = 3 * D * ffl // (C * LANE)
    const = lambda i, f: (0, 0)
    return pl.pallas_call(
        functools.partial(wgrad_kernel, F, C),
        out_shape=like((C, total, LANE), BF),
        grid_spec=pltpu.PrefetchScalarGridSpec(
            num_scalar_prefetch=1,
            grid=(1,),
            in_specs=[pl.BlockSpec((T, D), const)] * (2 * F)
            + [gy_spec(T, D, half) for half in range(2) for s in range(F)]
            + [pl.BlockSpec((rows, ffl), const)] * 2
            + [pl.BlockSpec((rows, 2 * ffl), const)] * 2,
            out_specs=pl.BlockSpec((C, total, LANE), lambda i, f: (0, 0, 0)),
            scratch_shapes=[pltpu.VMEM((2 * rows, 2 * ffl), BF), pltpu.VMEM((ffl, D), BF)],
        ),
        compiler_params=params(),
        cost_estimate=cost(15),
        name="wgrad",
    )(f_idx, *ms, *gys, *gys, *hiddens, *dgus)


def ffn_out_kernel(F, hid0, hid1, wd, *outs):
    T = hid0.shape[0] // F
    for half, hid in enumerate((hid0, hid1)):
        res = dot_nn(hid[...], wd[...]).astype(BF)
        for s in range(F):
            outs[s][half * T : (half + 1) * T, :] = res[s * T : (s + 1) * T]


def ffn_out_call(hiddens, wd, F):
    rows = hiddens[0].shape[0]
    D = wd.shape[1]
    return pl.pallas_call(
        functools.partial(ffn_out_kernel, F),
        out_shape=(like((2 * rows // F, D), BF),) * F,
        in_specs=[VMEM] * 3,
        out_specs=(VMEM,) * F,
        compiler_params=params(),
        cost_estimate=cost(5),
        name="ffn_out",
    )(*hiddens, wd)


def go_kernel(parts, *refs):
    os, ds = refs[:parts], refs[parts : 2 * parts]
    out = refs[2 * parts]
    low = jnp.concatenate([r[...] for r in ds], axis=0)
    rows = [
        dot_tn(jnp.concatenate([r[p] for r in os], axis=0), low).astype(BF)
        for p in range(os[0].shape[0])
    ]
    wide = jnp.concatenate(rows, axis=0)
    C, n, _ = out.shape
    for c in range(C):
        out[c] = wide[c * n : (c + 1) * n]


def go_call(os, ds, C):
    per, _, hw = os[0].shape
    D = ds[0].shape[1]
    return pl.pallas_call(
        functools.partial(go_kernel, len(os)),
        out_shape=like((C, per * hw // C, D), BF),
        in_specs=[VMEM] * (2 * len(os)),
        out_specs=VMEM,
        compiler_params=params(),
        cost_estimate=cost(5),
        name="wgrad_out",
    )(*os, *ds)


def combine_kernel(F, body_rows, *refs):
    out = refs[F]
    total = refs[0][:body_rows, :].astype(F32)
    for s in range(1, F):
        total = total + refs[s][:body_rows, :].astype(F32)
    out[:body_rows, :] = total.astype(BF)
    small = jnp.zeros((8, out.shape[1]), F32)
    for s in range(F):
        both = refs[s][body_rows:, :].astype(F32)
        small = small + both[:8] + both[8:]
    high, low = split_low(small)
    out[body_rows:, :] = jnp.concatenate([high, low], axis=0)


def combine_call(parts):
    rows, hd = parts[0].shape
    return pl.pallas_call(
        functools.partial(combine_kernel, len(parts), rows - 16),
        out_shape=like((rows, hd), BF),
        in_specs=[VMEM] * len(parts),
        out_specs=VMEM,
        compiler_params=params(),
        cost_estimate=cost(2),
        name="combine",
    )(*parts)


def unpack_ffn_kernel(F, R, J, f_ref, src, gate_out, up_out, down_out):
    half = J // 2
    ffl = half * LANE
    for s in range(F):
        base = pl.multiple_of((f_ref[0] ^ s) * ffl, ffl)
        for j in range(J):
            (gate_out if j < half else up_out)[:, pl.ds(base + (j % half) * LANE, LANE)] = src[
                0, (s * J + j) * R : (s * J + j + 1) * R, :
            ].astype(F32)
    n, wide = down_out.shape
    for j in range(wide // LANE):
        at = F * J * R + j * n
        down_out[:, j * LANE : (j + 1) * LANE] = src[0, at : at + n, :].astype(F32)


def unpack_ffn_call(f_idx, src, F, R, FF, D):
    C, rows, _ = src.shape
    J = 2 * FF // (F * LANE)
    n = FF // (F * C)
    row = lambda c, f: (c, 0)
    return pl.pallas_call(
        functools.partial(unpack_ffn_kernel, F, R, J),
        out_shape=(like((C * R, FF), F32), like((C * R, FF), F32), like((C * n, D), F32)),
        grid_spec=pltpu.PrefetchScalarGridSpec(
            num_scalar_prefetch=1,
            grid=(C,),
            in_specs=[pl.BlockSpec((1, rows, LANE), lambda c, f: (c, 0, 0))],
            out_specs=(
                pl.BlockSpec((R, FF), row),
                pl.BlockSpec((R, FF), row),
                pl.BlockSpec((n, D), row),
            ),
        ),
        compiler_params=params(),
        cost_estimate=cost(8),
        name="unpack_ffn",
    )(f_idx, src)


def join_kernel(p, o, out):
    n, hd = p.shape
    out[:n, :] = p[...]
    rows, wide = o.shape
    for j in range(wide // hd):
        out[n + j * rows : n + (j + 1) * rows, :] = o[:, j * hd : (j + 1) * hd]


def join_call(p, summed, n_o):
    n, hd = p.shape
    total, D = summed.shape
    rows = n + n_o * D // hd
    return pl.pallas_call(
        join_kernel,
        out_shape=like((rows, hd), BF),
        grid=(1,),
        in_specs=[
            pl.BlockSpec((n, hd), lambda i: (0, 0)),
            pl.BlockSpec((n_o, D), lambda i: (total // n_o - 1, 0)),
        ],
        out_specs=pl.BlockSpec((rows, hd), lambda i: (0, 0)),
        compiler_params=params(),
        cost_estimate=cost(2),
        name="join",
    )(p, summed)


def unpack_attn_kernel(heads, hd, rep, src, q_out, k_out, v_out, o_out, small_out):
    C = src.shape[0]
    rows = q_out.shape[0]
    n = o_out.shape[0] // C
    small = jnp.zeros((8, hd), F32)
    for c in range(C):
        for h in range(heads):
            at = (c * heads + h) * hd
            q_out[:, at : at + hd] = src[c, h * rows : (h + 1) * rows, :].astype(F32)
        lane = slice((c // rep) * hd, (c // rep + 1) * hd)
        for h, out in ((heads, k_out), (heads + 1, v_out)):
            value = src[c, h * rows : (h + 1) * rows, :].astype(F32)
            if c % rep == 0:
                out[:, lane] = value
            else:
                out[:, lane] += value
        at = (heads + 2) * rows
        both = src[c, at : at + 16, :].astype(F32)
        small = small + both[:8] + both[8:]
        for j in range(o_out.shape[1] // hd):
            o_out[c * n : (c + 1) * n, j * hd : (j + 1) * hd] = src[
                c, at + 16 + j * n : at + 16 + (j + 1) * n, :
            ].astype(F32)
    small_out[...] = small


def unpack_attn_call(src, heads, hd, rep, rows, n_o, D):
    C = src.shape[0]
    return pl.pallas_call(
        functools.partial(unpack_attn_kernel, heads, hd, rep),
        out_shape=(
            like((rows, C * heads * hd), F32),
            like((rows, C * hd // rep), F32),
            like((rows, C * hd // rep), F32),
            like((C * n_o, D), F32),
            like((8, hd), F32),
        ),
        in_specs=[VMEM],
        out_specs=(VMEM,) * 5,
        compiler_params=params(),
        cost_estimate=cost(5),
        name="unpack_attn",
    )(src)


def after(value, *others):
    return lax.optimization_barrier((value,) + others)[0]


def body(
    block_input,
    cotangent,
    seq_lengths,
    block_table,
    query_proj,
    key_proj,
    value_proj,
    output_proj,
    gate_proj,
    up_proj,
    down_proj,
    attn_norm,
    ffn_norm,
    query_norm,
    key_norm,
):
    C = lax.axis_size("ctx")
    F = lax.axis_size("fsdp")
    c_at = lax.axis_index("ctx")
    f_at = lax.axis_index("fsdp")
    core = lax.rem(c_at, 2)
    c_idx, f_idx = c_at[None].astype(jnp.int32), f_at[None].astype(jnp.int32)
    T, D = block_input.shape[1:]
    S = T * C
    blocks = block_table.shape[0]
    blk = S // blocks
    hd = query_norm.shape[0] * F
    HQ = query_proj.shape[1] // hd
    KV = key_proj.shape[1] // hd
    FF = gate_proj.shape[1]
    heads = HQ // C
    rep = max(1, C // KV)
    FFl = FF // F
    R = D // (F * C)
    scale = 1.0 / math.sqrt(hd)
    length = seq_lengths.astype(jnp.int32)
    own_blocks = lax.dynamic_slice_in_dim(block_table, c_at * (blocks // C), blocks // C)
    own_pos = (own_blocks[:, None] * blk + jnp.arange(blk, dtype=jnp.int32)[None, :]).reshape(-1)
    live = (own_pos < length[0]).astype(F32)[:, None]
    order = jnp.argsort(block_table).astype(jnp.int32)

    def gather_f(v):
        return lax.all_to_all(jnp.broadcast_to(v[None], (F,) + v.shape), "fsdp", 0, 0)

    def exchange_c(v):
        return lax.all_to_all(v, "ctx", 0, 0)

    def to_partner(v, s):
        return lax.ppermute(v, "fsdp", [(i, i ^ s) for i in range(F)])

    def gather_x(v):
        return [v] + [to_partner(v, s) for s in range(1, F)]

    def exchange_x(vs):
        return [vs[0]] + [to_partner(vs[s], s) for s in range(1, F)]

    def other_core(v):
        return lax.ppermute(v, "ctx", [(i, i ^ 1) for i in range(C)])

    def gather_c(v):
        parts = [v] + [
            lax.ppermute(v, "ctx", [(i, i ^ (2 * k)) for i in range(C)]) for k in range(1, C // 2)
        ]
        return [p for v in parts for p in (v, other_core(v))]

    x_all = lax.all_gather(block_input[0], "ctx", axis=0, tiled=True)
    kv_at = (c_at // rep) * hd
    cols = (heads + 2) * hd
    w_own = jnp.concatenate(
        [
            lax.dynamic_slice_in_dim(query_proj, c_at * heads * hd, heads * hd, 1),
            lax.dynamic_slice_in_dim(key_proj, kv_at, hd, 1),
            lax.dynamic_slice_in_dim(value_proj, kv_at, hd, 1),
        ],
        axis=1,
    ).astype(BF)
    gains_own = jnp.concatenate([attn_norm, ffn_norm, query_norm, key_norm]).astype(BF)
    lanes = D // 2
    w_own = jnp.pad(w_own, ((0, 0), (0, lanes - cols)))
    gain_rows = -(-gains_own.shape[0] // (16 * lanes)) * 16
    gains_own = jnp.pad(gains_own, (0, gain_rows * lanes - gains_own.shape[0]))
    wo_rows = output_proj.shape[0] // 2
    wo_half = lax.dynamic_slice_in_dim(output_proj, core * wo_rows, wo_rows, 0).astype(BF)
    n_wo = 2 * wo_rows
    moved = gather_f(
        jnp.concatenate(
            [wo_half[:, :lanes], wo_half[:, lanes:], w_own, gains_own.reshape(gain_rows, lanes)],
            axis=0,
        )
    )
    w_heads = moved[:, n_wo : n_wo + D // F, :cols].reshape(D, cols)
    gains = moved[:, n_wo + D // F :].reshape(F, gain_rows * lanes).astype(F32)
    g1 = gains[:, : D // F].reshape(1, D)
    g2 = gains[:, D // F : 2 * D // F].reshape(1, D)
    gq = gains[:, 2 * D // F : (2 * D + hd) // F].reshape(1, hd)
    gk = gains[:, (2 * D + hd) // F : (2 * D + 2 * hd) // F].reshape(1, hd)
    wo_a = moved[:, :n_wo]
    wo_b = other_core(wo_a)
    gu_rows = D // F // 2
    half_of = lambda w: lax.dynamic_slice_in_dim(w, core * gu_rows, gu_rows, 0).astype(BF)
    wgu_half = jnp.concatenate(
        [half_of(gate_proj).reshape(gu_rows, F, FFl), half_of(up_proj).reshape(gu_rows, F, FFl)],
        axis=2,
    )
    wgu_a = lax.all_to_all(after(jnp.swapaxes(wgu_half, 0, 1), moved), "fsdp", 0, 0)
    wd = down_proj.astype(BF)
    gy = (cotangent[0].astype(F32) * live).astype(BF)
    gys = gather_x(after(gy, wgu_a))

    half = hd // 2
    frequency = THETA ** (-(jnp.arange(half).astype(F32) * 2.0 / hd))
    angles = jnp.arange(S, dtype=jnp.int32).astype(F32)[:, None] * frequency[None, :]
    cos_t, sin_t = jnp.cos(angles), jnp.sin(angles)
    cos_t = jnp.concatenate([cos_t, cos_t], -1)
    sin_t = jnp.concatenate([-sin_t, sin_t], -1)
    raw, low = qkv_call(order, x_all, g1, w_heads, gq, gk, cos_t, sin_t, heads, hd, blk)
    o_even, o_odd, o32, lse = attn_call(order, length, low, heads, hd, blk, scale)


    x = block_input[0]
    o_nat = [exchange_c(after(o_even, wgu_a))]
    o_nat.append(exchange_c(after(o_odd, o_nat[0])))
    hs, ms, os, hiddens, dgus, dhs, dhbs, dos, fgains = [], [], [], [], [], [], [], [], []
    for b in range(2):
        o_b = o_nat[b] if b == 0 else after(o_nat[b], *gys)
        h, m_own, *o_parts = resid_call(b, f_idx, c_idx, o_b, wo_a, wo_b, x, g2)
        hs.append(h)
        os.append(o_parts)
        ms.append(gather_x(m_own))
    dms = []
    wgu_a = after(wgu_a, hs[0])
    wgu = rows_call(c_idx, wgu_a, other_core(wgu_a))
    for b in range(2):
        hidden, dgu, *dm_parts = ffn_call(b, f_idx, ms[b], gys, wgu, wd)
        hiddens.append(hidden)
        dgus.append(dgu)
        dms.append(exchange_x(dm_parts))
    hiddens[1] = after(hiddens[1], *dms[0])
    packed = wgrad_call(f_idx, ms[0] + ms[1], gys, hiddens, dgus, C)
    hs[1] = after(hs[1], packed)
    for b in range(2):
        dh, dhb, do_nat, fgain = resid_back_call(b, c_idx, dms[b], hs[b], gy, g2, wo_a, wo_b)
        dhs.append(dh)
        dhbs.append(dhb)
        fgains.append(fgain)
        dos.append(exchange_c(do_nat))

    owned = lax.psum_scatter(packed.reshape(-1, LANE), "ctx", scatter_dimension=0, tiled=True)
    owned = after(owned, dos[1])
    n_s = 2 * FFl // LANE * R
    owned_gu = exchange_x([owned[s * n_s : (s + 1) * n_s] for s in range(F)])
    all_ffn = lax.all_gather(jnp.concatenate(owned_gu + [owned[F * n_s :]], axis=0), "ctx", axis=0)
    grad_gate, grad_up, grad_down = unpack_ffn_call(f_idx, all_ffn, F, R, FF, D)

    ffn_parts = exchange_x([after(v, *owned_gu) for v in ffn_out_call(hiddens, wd, F)])
    ffn = sum(p.astype(F32) for p in ffn_parts)
    block_output = ((jnp.concatenate(hs, axis=0) + ffn) * live).astype(BF)[None]

    dq, dkv = attn_back_call(order, length, low, dos[0], dos[1], o32, lse, heads, hd, blk, scale)
    o_f = [p for parts in os for p in exchange_x([after(v, dhbs[1]) for v in parts])]
    dhb_f = [p for v in dhbs for p in gather_x(v)]
    go = go_call(o_f, dhb_f, C)
    n_o = go.shape[1]
    send, *grad_parts = head_back_call(
        order, f_idx, x_all, after(dq, *ffn_parts), dkv, raw, w_heads, go, g1, gq, gk, fgains, cos_t, sin_t,
        heads, hd, blk, F,
    )
    summed = lax.psum_scatter(after(send, all_ffn).reshape(-1, D), "ctx", scatter_dimension=0, tiled=True)
    dx, _ = norm_back(x.astype(F32), g1, summed[:T].astype(F32))
    grad_input = (jnp.concatenate(dhs, axis=0) + dx)[None]

    own_p = combine_call(exchange_x(grad_parts))
    joined = lax.all_gather(join_call(own_p, summed, n_o), "ctx", axis=0)
    grad_query, grad_key, grad_value, grad_output, small = unpack_attn_call(
        joined, heads, hd, rep, D // F, n_o, D
    )
    n_r = D // F // hd
    own_gain = lambda r: lax.dynamic_slice_in_dim(small[2 * n_r + r], f_at * (hd // F), hd // F)

    return (
        block_output,
        grad_input,
        grad_query,
        grad_key,
        grad_value,
        grad_output,
        grad_gate,
        grad_up,
        grad_down,
        small[:n_r].reshape(-1),
        small[n_r : 2 * n_r].reshape(-1),
        own_gain(0),
        own_gain(1),
    )


def solution(mesh):
    matrix, vector = P("fsdp", None), P("fsdp")
    rows = P("fsdp", "ctx", None)
    in_specs = (rows, rows, vector, P()) + (matrix,) * 7 + (vector,) * 4
    out_specs = (rows, rows) + (matrix,) * 7 + (vector,) * 4
    return jax.shard_map(body, mesh=mesh, in_specs=in_specs, out_specs=out_specs, check_vma=False)
```

```python
import functools
import math

import jax
import jax.numpy as jnp
from jax import lax
from jax.experimental import pallas as pl
from jax.experimental.pallas import tpu as pltpu
from jax.sharding import PartitionSpec as P

EPS = 1e-06
THETA = 1000000.0
BF = jnp.bfloat16
F32 = jnp.float32
LOG2E = math.log2(math.e)


def dot_nn(left, right):
    return lax.dot_general(left, right, (((1,), (0,)), ((), ())), preferred_element_type=F32)


def dot_nt(left, right):
    return lax.dot_general(left, right, (((1,), (1,)), ((), ())), preferred_element_type=F32)


def dot_tn(left, right):
    return lax.dot_general(left, right, (((0,), (0,)), ((), ())), preferred_element_type=F32)


def norm_back(values, gain_vec, upstream_grad):
    inverse = lax.rsqrt(jnp.mean(values * values, axis=-1, keepdims=True) + EPS)
    normed = values * inverse
    gain_terms = upstream_grad * normed
    gained = upstream_grad * gain_vec
    grad_values = inverse * (gained - normed * jnp.mean(gained * normed, axis=-1, keepdims=True))
    return (grad_values, gain_terms)


def params(mib=56):
    return pltpu.CompilerParams(vmem_limit_bytes=mib * 1024 * 1024)


def cost(us, moved=0):
    return pl.CostEstimate(flops=int(us * 1.15e9), bytes_accessed=int(moved), transcendentals=0)


SMEM = pl.BlockSpec(memory_space=pltpu.SMEM)
VMEM = pl.BlockSpec(memory_space=pltpu.VMEM)


def like(shape, dtype):
    return jax.ShapeDtypeStruct(tuple(shape), dtype)


def own_columns(weight, cols):
    F, rows, lanes = weight.shape
    return weight[...].reshape(F * rows, lanes)[:, :cols]


def weight_spec(moved, width):
    F, _, lanes = moved.shape
    return pl.BlockSpec((F, width // F, lanes), lambda i, o: (0, 2, 0))


def qkv_kernel(parts, heads, hd, order, *refs):
    x_refs = refs[:parts]
    gain, weight, gq, gk, cos, sin, raw_out, low_out = refs[parts:]
    x = jnp.concatenate([r[...] for r in x_refs], axis=0).astype(F32)
    a = (x * lax.rsqrt(jnp.mean(x * x, axis=-1, keepdims=True) + EPS) * gain[...]).astype(BF)
    raw = dot_nn(a, own_columns(weight, (heads + 2) * hd))
    c, s = cos[...], sin[...]
    for h in range(heads + 1):
        u = raw[:, h * hd : (h + 1) * hd]
        raw_out[:, h * hd : (h + 1) * hd] = u
        g = gq[...] if h < heads else gk[...]
        n = u * lax.rsqrt(jnp.mean(u * u, axis=-1, keepdims=True) + EPS) * g
        low_out[:, h * hd : (h + 1) * hd] = (n * c + pltpu.roll(n, hd // 2, axis=1) * s).astype(BF)
    low_out[:, (heads + 1) * hd :] = raw[:, (heads + 1) * hd :].astype(BF)


def block_specs(parts, blk, width):
    return [
        pl.BlockSpec((blk, width), functools.partial(lambda k, i, o: (o[parts * i + k], 0), k))
        for k in range(parts)
    ]


def qkv_call(order, x_all, gain, weight, gq, gk, cos, sin, heads, hd, blk):
    total, width = x_all.shape
    cols = (heads + 2) * hd
    parts = 4
    step = parts * blk
    const = lambda i, o: (0, 0)
    rows = lambda i, o: (i, 0)
    return pl.pallas_call(
        functools.partial(qkv_kernel, parts, heads, hd),
        out_shape=(like((total, (heads + 1) * hd), F32), like((total, cols), BF)),
        grid_spec=pltpu.PrefetchScalarGridSpec(
            num_scalar_prefetch=1,
            grid=(total // step,),
            in_specs=block_specs(parts, blk, width)
            + [
                pl.BlockSpec((1, width), const),
                weight_spec(weight, width),
                pl.BlockSpec((1, hd), const),
                pl.BlockSpec((1, hd), const),
                pl.BlockSpec((step, hd), rows),
                pl.BlockSpec((step, hd), rows),
            ],
            out_specs=(
                pl.BlockSpec((step, (heads + 1) * hd), rows),
                pl.BlockSpec((step, cols), rows),
            ),
        ),
        compiler_params=params(),
        cost_estimate=cost(40),
        name="qkv",
    )(order, *([x_all] * parts), gain, weight, gq, gk, cos, sin)


TQ, TK = 512, 512


def stack_heads(ref, start, heads, hd):
    return jnp.concatenate(
        [ref[pl.ds(start, TQ), h * hd : (h + 1) * hd] for h in range(heads)], axis=0
    )


def attn_kernel(heads, hd, blk, scale, order, length_ref, low, o_even, o_odd, o32_out, lse_out, vext, acc):
    total = low.shape[0]
    length = length_ref[0]
    kcol, vcol = heads * hd, (heads + 1) * hd
    rows = heads * TQ
    vext[:, :hd] = low[:, vcol : vcol + hd]
    vext[:, hd:] = jnp.ones((total, hd), BF)
    full = length // TK
    ends = pl.cdiv(length, TK)

    @pl.loop(0, total // TQ)
    def _(i):
        qs = pl.multiple_of(i * TQ, TQ)
        q = stack_heads(low, qs, heads, hd)
        acc[...] = jnp.zeros_like(acc)

        def tile(j, masked):
            ks = pl.multiple_of(j * TK, TK)
            s = dot_nt(q, low[pl.ds(ks, TK), kcol : kcol + hd])
            p = jnp.exp2(s * (scale * LOG2E))
            if masked:
                kpos = ks + lax.broadcasted_iota(jnp.int32, (rows, TK), 1)
                qpos = qs + lax.broadcasted_iota(jnp.int32, (rows, TK), 0) % TQ
                p = jnp.where((kpos <= qpos) & (kpos < length), p, 0.0)
            acc[...] += dot_nn(p.astype(BF), vext[pl.ds(ks, TK), :])

        clean = jnp.minimum(qs // TK, full)

        @pl.loop(0, clean)
        def _(j):
            tile(j, False)

        @pl.loop(clean, jnp.minimum((qs + TQ - 1) // TK + 1, ends))
        def _(j):
            tile(j, True)

        total_p = acc[:, hd:]
        o = acc[:, :hd] / total_p
        lse_out[i] = jnp.log2(total_p.T[:8])
        for h in range(heads):
            cut = slice(h * hd, (h + 1) * hd)
            part = o[h * TQ : (h + 1) * TQ]
            o32_out[pl.ds(qs, TQ), cut] = part
            for b in range(TQ // blk):
                at = order[i * (TQ // blk) + b]
                low_part = part[b * blk : (b + 1) * blk].astype(BF)

                @pl.when(at % 2 == 0)
                def _():
                    o_even[at // 2, :, cut] = low_part

                @pl.when(at % 2 == 1)
                def _():
                    o_odd[at // 2, :, cut] = low_part


def attn_call(order, length, low, heads, hd, blk, scale):
    total = low.shape[0]
    half = like((total // (2 * blk), blk, heads * hd), BF)
    return pl.pallas_call(
        functools.partial(attn_kernel, heads, hd, blk, scale),
        out_shape=(
            half,
            half,
            like((total, heads * hd), F32),
            like((total // TQ, 8, heads * TQ), F32),
        ),
        in_specs=[SMEM, SMEM, VMEM],
        out_specs=(VMEM,) * 4,
        scratch_shapes=[
            pltpu.VMEM((total, 2 * hd), BF),
            pltpu.VMEM((heads * TQ, 2 * hd), F32),
        ],
        compiler_params=params(),
        cost_estimate=cost(40),
        name="attn_fwd",
    )(order, length, low)


def attn_back_kernel(
    heads, hd, blk, scale, order, length_ref, low, do_even, do_odd, o32, lse, dq_out, dkv_out,
    do_s, delta, dkv,
):
    total = low.shape[0]
    tiles = total // TQ
    length = length_ref[0]
    kcol, vcol = heads * hd, (heads + 1) * hd
    rows = heads * TQ

    @pl.loop(0, tiles)
    def _(i):
        qs = pl.multiple_of(i * TQ, TQ)
        for b in range(TQ // blk):
            at = order[i * (TQ // blk) + b]

            @pl.when(at % 2 == 0)
            def _():
                do_s[pl.ds(qs + b * blk, blk), :] = do_even[at // 2]

            @pl.when(at % 2 == 1)
            def _():
                do_s[pl.ds(qs + b * blk, blk), :] = do_odd[at // 2]

        do_t = stack_heads(do_s, qs, heads, hd).astype(F32) * stack_heads(o32, qs, heads, hd)
        delta[i] = jnp.broadcast_to(jnp.sum(do_t.T, axis=0, keepdims=True), (8, rows))
        dq_out[pl.ds(qs, TQ), :] = jnp.zeros((TQ, heads * hd), F32)

    full = length // TK

    @pl.loop(0, total // TK)
    def _(j):
        ks = pl.multiple_of(j * TK, TK)
        k = low[pl.ds(ks, TK), kcol : kcol + hd]
        v = low[pl.ds(ks, TK), vcol : vcol + hd]
        dkv[...] = jnp.zeros_like(dkv)

        def tile(i, masked):
            qs = pl.multiple_of(i * TQ, TQ)
            q = stack_heads(low, qs, heads, hd)
            do = stack_heads(do_s, qs, heads, hd)
            s = dot_nt(k, q)
            p = jnp.exp2(s * (scale * LOG2E) - lse[i][:1])
            if masked:
                kpos = ks + lax.broadcasted_iota(jnp.int32, (TK, rows), 0)
                qpos = qs + lax.broadcasted_iota(jnp.int32, (TK, rows), 1) % TQ
                p = jnp.where((kpos <= qpos) & (kpos < length), p, 0.0)
            dp = dot_nt(v, do)
            ds = (p * (dp - delta[i][:1])).astype(BF)
            dkv[:, :hd] += dot_nn(ds, q)
            dkv[:, hd:] += dot_nn(p.astype(BF), do)
            dq = dot_tn(ds, k)
            for h in range(heads):
                dq_out[pl.ds(qs, TQ), h * hd : (h + 1) * hd] += dq[h * TQ : (h + 1) * TQ]

        first = ks // TQ
        masked_end = jnp.where(j < full, (ks + TK - 1) // TQ + 1, tiles)

        @pl.loop(first, masked_end)
        def _(i):
            tile(i, True)

        @pl.loop(masked_end, tiles)
        def _(i):
            tile(i, False)

        dkv_out[pl.ds(ks, TK), :hd] = dkv[:, :hd]
        dkv_out[pl.ds(ks, TK), hd:] = dkv[:, hd:]


def attn_back_call(order, length, low, do_even, do_odd, o32, lse, heads, hd, blk, scale):
    total = low.shape[0]
    return pl.pallas_call(
        functools.partial(attn_back_kernel, heads, hd, blk, scale),
        out_shape=(like((total, heads * hd), F32), like((total, 2 * hd), F32)),
        in_specs=[SMEM, SMEM] + [VMEM] * 5,
        out_specs=(VMEM, VMEM),
        scratch_shapes=[
            pltpu.VMEM((total, heads * hd), BF),
            pltpu.VMEM((total // TQ, 8, heads * TQ), F32),
            pltpu.VMEM((TK, 2 * hd), F32),
        ],
        compiler_params=params(),
        cost_estimate=cost(300),
        name="attn_bwd",
    )(order, length, low, do_even, do_odd, o32, lse)


def split_low(values):
    high = values.astype(BF)
    return high, (values - high.astype(F32)).astype(BF)


def head_back_kernel(parts, blk, heads, hd, F, scale, order, f_ref, *refs):
    x_refs = refs[:parts]
    dq, dkv, raw, weight, go, gain, gq, gk, fg0, fg1, cos, sin = refs[parts : parts + 12]
    send_out = refs[parts + 12]
    grad_outs = refs[parts + 13 : parts + 13 + F]
    grad_acc, gain_acc, attn_acc = refs[parts + 13 + F :]
    i = pl.program_id(0)

    @pl.when(i == 0)
    def _():
        grad_acc[...] = jnp.zeros_like(grad_acc)
        gain_acc[...] = jnp.zeros_like(gain_acc)
        attn_acc[...] = jnp.zeros_like(attn_acc)
        rows_own = send_out.shape[1] - go.shape[1]
        for c in range(go.shape[0]):
            send_out[c, rows_own:, :] = go[c]

    c, s = cos[...] * scale, sin[...] * scale
    pieces = []
    for h in range(heads + 1):
        cut = slice(h * hd, (h + 1) * hd)
        g_rot = dq[:, cut] if h < heads else dkv[:, :hd]
        e = g_rot * c + pltpu.roll(g_rot * s, hd // 2, axis=1)
        dv, terms = norm_back(raw[:, cut], gq[...] if h < heads else gk[...], e)
        pieces.append(dv.astype(BF))
        row = 0 if h < heads else 1
        gain_acc[row : row + 1, :] += jnp.sum(terms, axis=0, keepdims=True)
    pieces.append(dkv[:, hd:].astype(BF))
    dqkv = jnp.concatenate(pieces, axis=1)
    da = dot_nt(dqkv, own_columns(weight, (heads + 2) * hd))
    per = (send_out.shape[1] - go.shape[1]) // blk
    normed_parts = []
    for k in range(parts):
        x = x_refs[k][...].astype(F32)
        part = da[k * blk : (k + 1) * blk]
        normed = x * lax.rsqrt(jnp.mean(x * x, axis=-1, keepdims=True) + EPS)
        normed_parts.append((normed * gain[...]).astype(BF))
        attn_acc[...] += jnp.sum(part * normed, axis=0, keepdims=True)
        at = order[parts * i + k]
        send_out[at // per, pl.ds(pl.multiple_of((at % per) * blk, blk), blk), :] = part.astype(BF)
    grad_acc[...] += dot_tn(jnp.concatenate(normed_parts, axis=0), dqkv)

    @pl.when(i == pl.num_programs(0) - 1)
    def _():
        n = grad_acc.shape[0] // F
        for s_ in range(F):
            f = f_ref[0] ^ s_
            at = pl.multiple_of(f * n, n)
            out = grad_outs[s_]
            for b in range(heads + 2):
                out[b * n : (b + 1) * n, :] = grad_acc[
                    pl.ds(at, n), b * hd : (b + 1) * hd
                ].astype(BF)
            base = (heads + 2) * n
            rows = []
            for r in range(n // hd):
                rows.append(attn_acc[:, pl.ds(pl.multiple_of(at + r * hd, hd), hd)])
            for r in range(n // hd):
                lane = pl.ds(pl.multiple_of(at + r * hd, hd), hd)
                rows.append(fg0[:, lane] + fg1[:, lane])
            rows += [gain_acc[0:1, :], gain_acc[1:2, :]]
            rows += [jnp.zeros((1, hd), F32)] * (8 - len(rows))
            high, low = split_low(jnp.concatenate(rows, axis=0))
            out[base : base + 16, :] = jnp.concatenate([high, low], axis=0)


def head_back_call(
    order, f_idx, x_all, dq, dkv, raw, weight, go, gain, gq, gk, fgains, cos, sin, heads, hd, blk, F
):
    total = dq.shape[0]
    width, cols = x_all.shape[1], (heads + 2) * hd
    parts = 4
    step = parts * blk
    ctx = go.shape[0]
    const = lambda i, o: (0, 0)
    const3 = lambda i, o: (0, 0, 0)
    rows = lambda i, o: (i, 0)
    send = (ctx, total // ctx + go.shape[1], width)
    grad = ((heads + 2) * (width // F) + 16, hd)
    return pl.pallas_call(
        functools.partial(head_back_kernel, parts, blk, heads, hd, F, hd**-0.5),
        out_shape=(like(send, BF),) + (like(grad, BF),) * F,
        grid_spec=pltpu.PrefetchScalarGridSpec(
            num_scalar_prefetch=1,
            grid=(total // step,),
            in_specs=[SMEM]
            + block_specs(parts, blk, width)
            + [
                pl.BlockSpec((step, heads * hd), rows),
                pl.BlockSpec((step, 2 * hd), rows),
                pl.BlockSpec((step, (heads + 1) * hd), rows),
                weight_spec(weight, width),
                pl.BlockSpec(go.shape, const3),
                pl.BlockSpec((1, width), const),
                pl.BlockSpec((1, hd), const),
                pl.BlockSpec((1, hd), const),
                pl.BlockSpec((1, width), const),
                pl.BlockSpec((1, width), const),
                pl.BlockSpec((step, hd), rows),
                pl.BlockSpec((step, hd), rows),
            ],
            out_specs=(pl.BlockSpec(send, const3),) + (pl.BlockSpec(grad, const),) * F,
            scratch_shapes=[
                pltpu.VMEM((width, cols), F32),
                pltpu.VMEM((8, hd), F32),
                pltpu.VMEM((1, width), F32),
            ],
        ),
        compiler_params=params(),
        cost_estimate=cost(60),
        name="head_bwd",
    )(
        order, f_idx, *([x_all] * parts), dq, dkv, raw, weight, go, gain, gq, gk, *fgains, cos, sin
    )


def heads_at(c_ref, f, part):
    return 2 * f + ((c_ref[0] % 2) ^ part)


def resid_kernel(F, f_ref, c_ref, o, wo_a, wo_b, x, g2, h_out, m_out, *o_outs):
    n = wo_a.shape[1] // 2
    half = wo_a.shape[2]
    left, right = x[:, :half].astype(F32), x[:, half:].astype(F32)
    for part, wo in enumerate((wo_a, wo_b)):
        for f in range(F):
            of = o[heads_at(c_ref, f, part)]
            left = left + dot_nn(of, wo[f, :n])
            right = right + dot_nn(of, wo[f, n : 2 * n])
    h = jnp.concatenate([left, right], axis=1)
    h_out[...] = h
    m_out[...] = (h * lax.rsqrt(jnp.mean(h * h, axis=-1, keepdims=True) + EPS) * g2[...]).astype(BF)
    for s in range(F):
        for r in range(2):
            o_outs[s][r] = o[(f_ref[0] ^ s) * 2 + r]


def wo_specs(wo_a, wo_b):
    const3 = lambda i: (0, 0, 0)
    return [pl.BlockSpec(wo_b.shape, const3), pl.BlockSpec(wo_b.shape, const3)]


def resid_call(half, f_idx, c_idx, o, wo_a, wo_b, x, g2):
    C, T, hw = o.shape
    D = x.shape[1]
    F = wo_b.shape[0]
    part = like((2, T, hw), BF)
    const = lambda i: (0, 0)
    const3 = lambda i: (0, 0, 0)
    return pl.pallas_call(
        functools.partial(resid_kernel, F),
        out_shape=(like((T, D), F32), like((T, D), BF)) + (part,) * F,
        grid=(1,),
        in_specs=[SMEM, SMEM, pl.BlockSpec(o.shape, const3)]
        + wo_specs(wo_a, wo_b)
        + [pl.BlockSpec((T, D), lambda i: (half, 0)), pl.BlockSpec(g2.shape, const)],
        out_specs=(pl.BlockSpec((T, D), const),) * 2 + (pl.BlockSpec(part.shape, const3),) * F,
        compiler_params=params(),
        cost_estimate=cost(10),
        name="resid",
    )(f_idx, c_idx, o, wo_a, wo_b, x, g2)


def ffn_kernel(F, *refs):
    c_ref = refs[1]
    ms, gys = refs[2 : 2 + F], refs[2 + F : 2 + 2 * F]
    wgu_a, wgu_b, wd, hid_out, dgu_out = refs[2 + 2 * F : 7 + 2 * F]
    dm_outs, wgu = refs[7 + 2 * F : -1], refs[-1]
    n = wgu_a.shape[1]
    for part, src in enumerate((wgu_a, wgu_b)):
        for f in range(F):
            at = pl.multiple_of(heads_at(c_ref, f, part) * n, n)
            wgu[pl.ds(at, n), :] = src[f]
    ffl = wd.shape[0]
    T = ms[0].shape[0]
    m = jnp.concatenate([r[...] for r in ms], axis=0)
    gy = jnp.concatenate([r[...] for r in gys], axis=0)
    gu = dot_nn(m, wgu[...])
    dhid = dot_nt(gy, wd[...])
    gate, up = gu[:, :ffl], gu[:, ffl:]
    sig = 1.0 / (1.0 + jnp.exp(-gate))
    silu = gate * sig
    hid_out[...] = (silu * up).astype(BF)
    dgu = jnp.concatenate(
        [(dhid * up * (sig + silu * (1.0 - sig))).astype(BF), (dhid * silu).astype(BF)], axis=1
    )
    dgu_out[...] = dgu
    dm = dot_nt(dgu, wgu[...]).astype(BF)
    for s in range(F):
        dm_outs[s][...] = dm[s * T : (s + 1) * T]


def gy_spec(T, D, half):
    return pl.BlockSpec((T, D), lambda i, f: (half, 0))


def ffn_call(half, f_idx, c_idx, ms, gys, wgu_a, wgu_b, wd):
    F = len(ms)
    T, D = ms[0].shape
    ffl = wd.shape[0]
    const = lambda i, f: (0, 0)
    return pl.pallas_call(
        functools.partial(ffn_kernel, F),
        out_shape=(like((F * T, ffl), BF), like((F * T, 2 * ffl), BF)) + (like((T, D), BF),) * F,
        grid_spec=pltpu.PrefetchScalarGridSpec(
            num_scalar_prefetch=1,
            grid=(1,),
            in_specs=[SMEM]
            + [pl.BlockSpec((T, D), const)] * F
            + [gy_spec(T, D, half)] * F
            + [pl.BlockSpec(wgu_a.shape, lambda i, f: (0, 0, 0))] * 2
            + [pl.BlockSpec(wd.shape, const)],
            out_specs=(
                pl.BlockSpec((F * T, ffl), const),
                pl.BlockSpec((F * T, 2 * ffl), const),
            )
            + (pl.BlockSpec((T, D), const),) * F,
            scratch_shapes=[pltpu.VMEM((D, wgu_a.shape[2]), BF)],
        ),
        compiler_params=params(),
        cost_estimate=cost(10),
        name="ffn",
    )(f_idx, c_idx, *ms, *gys, wgu_a, wgu_b, wd)


def resid_back_kernel(F, c_ref, *refs):
    dms = refs[:F]
    wo_a, wo_b, h, gy, g2, dh_out, dhb_out, do_out, gain_out = refs[F:]
    total = dms[0][...].astype(F32)
    for s in range(1, F):
        total = total + dms[s][...].astype(F32)
    dv, terms = norm_back(h[...], g2[...], total)
    gain_out[...] = jnp.sum(terms, axis=0, keepdims=True)
    dh = gy[...].astype(F32) + dv
    dh_out[...] = dh
    low = dh.astype(BF)
    dhb_out[...] = low
    n = wo_a.shape[1] // 2
    half = wo_a.shape[2]
    for part, wo in enumerate((wo_a, wo_b)):
        for f in range(F):
            do = dot_nt(low[:, :half], wo[f, :n]) + dot_nt(low[:, half:], wo[f, n : 2 * n])
            do_out[heads_at(c_ref, f, part)] = do.astype(BF)


def resid_back_call(half, c_idx, dms, h, gy, g2, wo_a, wo_b):
    F = len(dms)
    T, D = h.shape
    hw = wo_b.shape[1] // 2
    const = lambda i: (0, 0)
    return pl.pallas_call(
        functools.partial(resid_back_kernel, F),
        out_shape=(
            like((T, D), F32),
            like((T, D), BF),
            like((2 * F, T, hw), BF),
            like((1, D), F32),
        ),
        grid=(1,),
        in_specs=[SMEM]
        + [pl.BlockSpec((T, D), const)] * F
        + wo_specs(wo_a, wo_b)
        + [
            pl.BlockSpec((T, D), const),
            pl.BlockSpec((T, D), lambda i: (half, 0)),
            pl.BlockSpec(g2.shape, const),
        ],
        out_specs=(
            pl.BlockSpec((T, D), const),
            pl.BlockSpec((T, D), const),
            pl.BlockSpec((2 * F, T, hw), lambda i: (0, 0, 0)),
            pl.BlockSpec((1, D), const),
        ),
        compiler_params=params(),
        cost_estimate=cost(10),
        name="resid_bwd",
    )(c_idx, *dms, wo_a, wo_b, h, gy, g2)


LANE = 256


def wgrad_kernel(F, C, f_ref, *refs):
    ms, gys = refs[: 2 * F], refs[2 * F : 4 * F]
    hid0, hid1, dgu0, dgu1, out, gd = refs[4 * F :]
    D = ms[0].shape[1]
    n = D // F
    R = n // C
    J = dgu0.shape[1] // LANE
    for s in range(F):
        lane = pl.ds(pl.multiple_of((f_ref[0] ^ s) * n, n), n)
        lhs = [jnp.concatenate([r[:, lane] for r in ms[b * F : (b + 1) * F]], axis=0) for b in (0, 1)]
        res = (dot_tn(lhs[0], dgu0[...]) + dot_tn(lhs[1], dgu1[...])).astype(BF)
        for c in range(C):
            for j in range(J):
                out[c, (s * J + j) * R : (s * J + j + 1) * R, :] = res[
                    c * R : (c + 1) * R, j * LANE : (j + 1) * LANE
                ]
    hid = jnp.concatenate([hid0[...], hid1[...]], axis=0)
    gy = jnp.concatenate([r[...] for r in gys], axis=0)
    gd[...] = dot_tn(hid, gy).astype(BF)
    base = F * J * R
    n = gd.shape[0] // C
    for c in range(C):
        for j in range(D // LANE):
            out[c, base + j * n : base + (j + 1) * n, :] = gd[
                c * n : (c + 1) * n, j * LANE : (j + 1) * LANE
            ]


def wgrad_call(f_idx, ms, gys, hiddens, dgus, C):
    F = len(ms) // 2
    T, D = ms[0].shape
    rows, ffl = hiddens[0].shape
    total = 3 * D * ffl // (C * LANE)
    const = lambda i, f: (0, 0)
    return pl.pallas_call(
        functools.partial(wgrad_kernel, F, C),
        out_shape=like((C, total, LANE), BF),
        grid_spec=pltpu.PrefetchScalarGridSpec(
            num_scalar_prefetch=1,
            grid=(1,),
            in_specs=[pl.BlockSpec((T, D), const)] * (2 * F)
            + [gy_spec(T, D, half) for half in range(2) for s in range(F)]
            + [pl.BlockSpec((rows, ffl), const)] * 2
            + [pl.BlockSpec((rows, 2 * ffl), const)] * 2,
            out_specs=pl.BlockSpec((C, total, LANE), lambda i, f: (0, 0, 0)),
            scratch_shapes=[pltpu.VMEM((ffl, D), BF)],
        ),
        compiler_params=params(),
        cost_estimate=cost(15),
        name="wgrad",
    )(f_idx, *ms, *gys, *gys, *hiddens, *dgus)


def ffn_out_kernel(F, hid0, hid1, wd, *outs):
    T = hid0.shape[0] // F
    for half, hid in enumerate((hid0, hid1)):
        res = dot_nn(hid[...], wd[...]).astype(BF)
        for s in range(F):
            outs[s][half * T : (half + 1) * T, :] = res[s * T : (s + 1) * T]


def ffn_out_call(hiddens, wd, F):
    rows = hiddens[0].shape[0]
    D = wd.shape[1]
    return pl.pallas_call(
        functools.partial(ffn_out_kernel, F),
        out_shape=(like((2 * rows // F, D), BF),) * F,
        in_specs=[VMEM] * 3,
        out_specs=(VMEM,) * F,
        compiler_params=params(),
        cost_estimate=cost(5),
        name="ffn_out",
    )(*hiddens, wd)


def go_kernel(parts, *refs):
    os, ds = refs[:parts], refs[parts : 2 * parts]
    out = refs[2 * parts]
    low = jnp.concatenate([r[...] for r in ds], axis=0)
    rows = [
        dot_tn(jnp.concatenate([r[p] for r in os], axis=0), low).astype(BF)
        for p in range(os[0].shape[0])
    ]
    wide = jnp.concatenate(rows, axis=0)
    C, n, _ = out.shape
    for c in range(C):
        out[c] = wide[c * n : (c + 1) * n]


def go_call(os, ds, C):
    per, _, hw = os[0].shape
    D = ds[0].shape[1]
    return pl.pallas_call(
        functools.partial(go_kernel, len(os)),
        out_shape=like((C, per * hw // C, D), BF),
        in_specs=[VMEM] * (2 * len(os)),
        out_specs=VMEM,
        compiler_params=params(),
        cost_estimate=cost(5),
        name="wgrad_out",
    )(*os, *ds)


def combine_kernel(F, body_rows, *refs):
    out = refs[F]
    total = refs[0][:body_rows, :].astype(F32)
    for s in range(1, F):
        total = total + refs[s][:body_rows, :].astype(F32)
    out[:body_rows, :] = total.astype(BF)
    small = jnp.zeros((8, out.shape[1]), F32)
    for s in range(F):
        both = refs[s][body_rows:, :].astype(F32)
        small = small + both[:8] + both[8:]
    high, low = split_low(small)
    out[body_rows:, :] = jnp.concatenate([high, low], axis=0)


def combine_call(parts):
    rows, hd = parts[0].shape
    return pl.pallas_call(
        functools.partial(combine_kernel, len(parts), rows - 16),
        out_shape=like((rows, hd), BF),
        in_specs=[VMEM] * len(parts),
        out_specs=VMEM,
        compiler_params=params(8),
        cost_estimate=cost(2),
        name="combine",
    )(*parts)


def unpack_ffn_kernel(F, R, J, f_ref, src, gate_out, up_out, down_out):
    half = J // 2
    ffl = half * LANE
    for s in range(F):
        base = pl.multiple_of((f_ref[0] ^ s) * ffl, ffl)
        for j in range(J):
            (gate_out if j < half else up_out)[:, pl.ds(base + (j % half) * LANE, LANE)] = src[
                0, (s * J + j) * R : (s * J + j + 1) * R, :
            ].astype(F32)
    n, wide = down_out.shape
    for j in range(wide // LANE):
        at = F * J * R + j * n
        down_out[:, j * LANE : (j + 1) * LANE] = src[0, at : at + n, :].astype(F32)


def unpack_ffn_call(f_idx, src, F, R, FF, D):
    C, rows, _ = src.shape
    J = 2 * FF // (F * LANE)
    n = FF // (F * C)
    row = lambda c, f: (c, 0)
    return pl.pallas_call(
        functools.partial(unpack_ffn_kernel, F, R, J),
        out_shape=(like((C * R, FF), F32), like((C * R, FF), F32), like((C * n, D), F32)),
        grid_spec=pltpu.PrefetchScalarGridSpec(
            num_scalar_prefetch=1,
            grid=(C,),
            in_specs=[pl.BlockSpec((1, rows, LANE), lambda c, f: (c, 0, 0))],
            out_specs=(
                pl.BlockSpec((R, FF), row),
                pl.BlockSpec((R, FF), row),
                pl.BlockSpec((n, D), row),
            ),
        ),
        compiler_params=params(16),
        cost_estimate=cost(8),
        name="unpack_ffn",
    )(f_idx, src)


def join_kernel(p, o, out):
    n, hd = p.shape
    out[:n, :] = p[...]
    rows, wide = o.shape
    for j in range(wide // hd):
        out[n + j * rows : n + (j + 1) * rows, :] = o[:, j * hd : (j + 1) * hd]


def join_call(p, summed, n_o):
    n, hd = p.shape
    total, D = summed.shape
    rows = n + n_o * D // hd
    return pl.pallas_call(
        join_kernel,
        out_shape=like((rows, hd), BF),
        grid=(1,),
        in_specs=[
            pl.BlockSpec((n, hd), lambda i: (0, 0)),
            pl.BlockSpec((n_o, D), lambda i: (total // n_o - 1, 0)),
        ],
        out_specs=pl.BlockSpec((rows, hd), lambda i: (0, 0)),
        compiler_params=params(8),
        cost_estimate=cost(2),
        name="join",
    )(p, summed)


def unpack_attn_kernel(heads, hd, rep, src, q_out, k_out, v_out, o_out, small_out):
    C = src.shape[0]
    rows = q_out.shape[0]
    n = o_out.shape[0] // C
    small = jnp.zeros((8, hd), F32)
    for c in range(C):
        for h in range(heads):
            at = (c * heads + h) * hd
            q_out[:, at : at + hd] = src[c, h * rows : (h + 1) * rows, :].astype(F32)
        lane = slice((c // rep) * hd, (c // rep + 1) * hd)
        for h, out in ((heads, k_out), (heads + 1, v_out)):
            value = src[c, h * rows : (h + 1) * rows, :].astype(F32)
            if c % rep == 0:
                out[:, lane] = value
            else:
                out[:, lane] += value
        at = (heads + 2) * rows
        both = src[c, at : at + 16, :].astype(F32)
        small = small + both[:8] + both[8:]
        for j in range(o_out.shape[1] // hd):
            o_out[c * n : (c + 1) * n, j * hd : (j + 1) * hd] = src[
                c, at + 16 + j * n : at + 16 + (j + 1) * n, :
            ].astype(F32)
    small_out[...] = small


def unpack_attn_call(src, heads, hd, rep, rows, n_o, D):
    C = src.shape[0]
    return pl.pallas_call(
        functools.partial(unpack_attn_kernel, heads, hd, rep),
        out_shape=(
            like((rows, C * heads * hd), F32),
            like((rows, C * hd // rep), F32),
            like((rows, C * hd // rep), F32),
            like((C * n_o, D), F32),
            like((8, hd), F32),
        ),
        in_specs=[VMEM],
        out_specs=(VMEM,) * 5,
        compiler_params=params(20),
        cost_estimate=cost(5),
        name="unpack_attn",
    )(src)


def after(value, *others):
    return lax.optimization_barrier((value,) + others)[0]


def body(
    block_input,
    cotangent,
    seq_lengths,
    block_table,
    query_proj,
    key_proj,
    value_proj,
    output_proj,
    gate_proj,
    up_proj,
    down_proj,
    attn_norm,
    ffn_norm,
    query_norm,
    key_norm,
):
    C = lax.axis_size("ctx")
    F = lax.axis_size("fsdp")
    c_at = lax.axis_index("ctx")
    f_at = lax.axis_index("fsdp")
    core = lax.rem(c_at, 2)
    c_idx, f_idx = c_at[None].astype(jnp.int32), f_at[None].astype(jnp.int32)
    T, D = block_input.shape[1:]
    S = T * C
    blocks = block_table.shape[0]
    blk = S // blocks
    hd = query_norm.shape[0] * F
    HQ = query_proj.shape[1] // hd
    KV = key_proj.shape[1] // hd
    FF = gate_proj.shape[1]
    heads = HQ // C
    rep = max(1, C // KV)
    FFl = FF // F
    R = D // (F * C)
    scale = 1.0 / math.sqrt(hd)
    length = seq_lengths.astype(jnp.int32)
    own_blocks = lax.dynamic_slice_in_dim(block_table, c_at * (blocks // C), blocks // C)
    own_pos = (own_blocks[:, None] * blk + jnp.arange(blk, dtype=jnp.int32)[None, :]).reshape(-1)
    live = (own_pos < length[0]).astype(F32)[:, None]
    order = jnp.argsort(block_table).astype(jnp.int32)

    def gather_f(v):
        return lax.all_to_all(jnp.broadcast_to(v[None], (F,) + v.shape), "fsdp", 0, 0)

    def exchange_c(v):
        return lax.all_to_all(v, "ctx", 0, 0)

    def to_partner(v, s):
        return lax.ppermute(v, "fsdp", [(i, i ^ s) for i in range(F)])

    def gather_x(v):
        return [v] + [to_partner(v, s) for s in range(1, F)]

    def exchange_x(vs):
        return [vs[0]] + [to_partner(vs[s], s) for s in range(1, F)]

    def other_core(v):
        return lax.ppermute(v, "ctx", [(i, i ^ 1) for i in range(C)])

    def gather_c(v):
        parts = [v] + [
            lax.ppermute(v, "ctx", [(i, i ^ (2 * k)) for i in range(C)]) for k in range(1, C // 2)
        ]
        return [p for v in parts for p in (v, other_core(v))]

    x_all = lax.all_gather(block_input[0], "ctx", axis=0, tiled=True)
    kv_at = (c_at // rep) * hd
    cols = (heads + 2) * hd
    w_own = jnp.concatenate(
        [
            lax.dynamic_slice_in_dim(query_proj, c_at * heads * hd, heads * hd, 1),
            lax.dynamic_slice_in_dim(key_proj, kv_at, hd, 1),
            lax.dynamic_slice_in_dim(value_proj, kv_at, hd, 1),
        ],
        axis=1,
    ).astype(BF)
    gains_own = jnp.concatenate([attn_norm, ffn_norm, query_norm, key_norm]).astype(BF)
    lanes = D // 2
    w_own = jnp.pad(w_own, ((0, 0), (0, lanes - cols)))
    gain_rows = -(-gains_own.shape[0] // (16 * lanes)) * 16
    gains_own = jnp.pad(gains_own, (0, gain_rows * lanes - gains_own.shape[0]))
    wo_rows = output_proj.shape[0] // 2
    wo_half = lax.dynamic_slice_in_dim(output_proj, core * wo_rows, wo_rows, 0).astype(BF)
    n_wo = 2 * wo_rows
    moved = gather_f(
        jnp.concatenate(
            [wo_half[:, :lanes], wo_half[:, lanes:], w_own, gains_own.reshape(gain_rows, lanes)],
            axis=0,
        )
    )
    gains = moved[:, n_wo + D // F :].reshape(F, gain_rows * lanes).astype(F32)
    g1 = gains[:, : D // F].reshape(1, D)
    g2 = gains[:, D // F : 2 * D // F].reshape(1, D)
    gq = gains[:, 2 * D // F : (2 * D + hd) // F].reshape(1, hd)
    gk = gains[:, (2 * D + hd) // F : (2 * D + 2 * hd) // F].reshape(1, hd)
    wo_a = moved
    wo_b = other_core(moved[:, :n_wo])
    gu_rows = D // F // 2
    half_of = lambda w: lax.dynamic_slice_in_dim(w, core * gu_rows, gu_rows, 0).astype(BF)
    wgu_half = jnp.concatenate(
        [half_of(gate_proj).reshape(gu_rows, F, FFl), half_of(up_proj).reshape(gu_rows, F, FFl)],
        axis=2,
    )
    wgu_a = lax.all_to_all(after(jnp.swapaxes(wgu_half, 0, 1), moved), "fsdp", 0, 0)
    wd = down_proj.astype(BF)
    gy = (cotangent[0].astype(F32) * live).astype(BF)
    gys = gather_x(after(gy, wgu_a))

    half = hd // 2
    frequency = THETA ** (-(jnp.arange(half).astype(F32) * 2.0 / hd))
    angles = jnp.arange(S, dtype=jnp.int32).astype(F32)[:, None] * frequency[None, :]
    cos_t, sin_t = jnp.cos(angles), jnp.sin(angles)
    cos_t = jnp.concatenate([cos_t, cos_t], -1)
    sin_t = jnp.concatenate([-sin_t, sin_t], -1)
    raw, low = qkv_call(order, x_all, g1, moved, gq, gk, cos_t, sin_t, heads, hd, blk)
    o_even, o_odd, o32, lse = attn_call(order, length, low, heads, hd, blk, scale)


    x = block_input[0]
    o_nat = [exchange_c(after(o_even, wgu_a))]
    o_nat.append(exchange_c(after(o_odd, o_nat[0])))
    hs, ms, os, hiddens, dgus, dhs, dhbs, dos, fgains = [], [], [], [], [], [], [], [], []
    for b in range(2):
        o_b = o_nat[b] if b == 0 else after(o_nat[b], *gys)
        h, m_own, *o_parts = resid_call(b, f_idx, c_idx, o_b, wo_a, wo_b, x, g2)
        hs.append(h)
        os.append(o_parts)
        ms.append(gather_x(m_own))
    dms = []
    wgu_a = after(wgu_a, hs[0])
    wgu_b = other_core(wgu_a)
    for b in range(2):
        hidden, dgu, *dm_parts = ffn_call(b, f_idx, c_idx, ms[b], gys, wgu_a, wgu_b, wd)
        hiddens.append(hidden)
        dgus.append(dgu)
        dms.append(exchange_x(dm_parts))
    hiddens[1] = after(hiddens[1], *dms[0])
    packed = wgrad_call(f_idx, ms[0] + ms[1], gys, hiddens, dgus, C)
    hs[1] = after(hs[1], packed)
    for b in range(2):
        dh, dhb, do_nat, fgain = resid_back_call(b, c_idx, dms[b], hs[b], gy, g2, wo_a, wo_b)
        dhs.append(dh)
        dhbs.append(dhb)
        fgains.append(fgain)
        dos.append(exchange_c(do_nat))

    owned = lax.psum_scatter(packed.reshape(-1, LANE), "ctx", scatter_dimension=0, tiled=True)
    owned = after(owned, dos[1])
    n_s = 2 * FFl // LANE * R
    owned_gu = exchange_x([owned[s * n_s : (s + 1) * n_s] for s in range(F)])
    all_ffn = lax.all_gather(jnp.concatenate(owned_gu + [owned[F * n_s :]], axis=0), "ctx", axis=0)
    grad_gate, grad_up, grad_down = unpack_ffn_call(f_idx, all_ffn, F, R, FF, D)

    ffn_parts = exchange_x([after(v, *owned_gu) for v in ffn_out_call(hiddens, wd, F)])
    ffn = sum(p.astype(F32) for p in ffn_parts)
    block_output = ((jnp.concatenate(hs, axis=0) + ffn) * live).astype(BF)[None]

    dq, dkv = attn_back_call(order, length, low, dos[0], dos[1], o32, lse, heads, hd, blk, scale)
    o_f = [p for parts in os for p in exchange_x([after(v, dhbs[1]) for v in parts])]
    dhb_f = [p for v in dhbs for p in gather_x(v)]
    go = go_call(o_f, dhb_f, C)
    n_o = go.shape[1]
    send, *grad_parts = head_back_call(
        order, f_idx, x_all, after(dq, *ffn_parts), dkv, raw, moved, go, g1, gq, gk, fgains, cos_t, sin_t,
        heads, hd, blk, F,
    )
    summed = lax.psum_scatter(after(send, all_ffn).reshape(-1, D), "ctx", scatter_dimension=0, tiled=True)
    dx, _ = norm_back(x.astype(F32), g1, summed[:T].astype(F32))
    grad_input = (jnp.concatenate(dhs, axis=0) + dx)[None]

    own_p = combine_call(exchange_x(grad_parts))
    joined = lax.all_gather(join_call(own_p, summed, n_o), "ctx", axis=0)
    grad_query, grad_key, grad_value, grad_output, small = unpack_attn_call(
        joined, heads, hd, rep, D // F, n_o, D
    )
    n_r = D // F // hd
    own_gain = lambda r: lax.dynamic_slice_in_dim(small[2 * n_r + r], f_at * (hd // F), hd // F)

    return (
        block_output,
        grad_input,
        grad_query,
        grad_key,
        grad_value,
        grad_output,
        grad_gate,
        grad_up,
        grad_down,
        small[:n_r].reshape(-1),
        small[n_r : 2 * n_r].reshape(-1),
        own_gain(0),
        own_gain(1),
    )


def solution(mesh):
    matrix, vector = P("fsdp", None), P("fsdp")
    rows = P("fsdp", "ctx", None)
    in_specs = (rows, rows, vector, P()) + (matrix,) * 7 + (vector,) * 4
    out_specs = (rows, rows) + (matrix,) * 7 + (vector,) * 4
    return jax.shard_map(body, mesh=mesh, in_specs=in_specs, out_specs=out_specs, check_vma=False)
```

```python
import functools
import math

import jax
import jax.numpy as jnp
from jax import lax
from jax.experimental import pallas as pl
from jax.experimental.pallas import tpu as pltpu
from jax.sharding import PartitionSpec as P

EPS = 1e-06
THETA = 1000000.0
BF = jnp.bfloat16
F32 = jnp.float32
LOG2E = math.log2(math.e)


def dot_nn(left, right):
    return lax.dot_general(left, right, (((1,), (0,)), ((), ())), preferred_element_type=F32)


def dot_nt(left, right):
    return lax.dot_general(left, right, (((1,), (1,)), ((), ())), preferred_element_type=F32)


def dot_tn(left, right):
    return lax.dot_general(left, right, (((0,), (0,)), ((), ())), preferred_element_type=F32)


def norm_back(values, gain_vec, upstream_grad):
    inverse = lax.rsqrt(jnp.mean(values * values, axis=-1, keepdims=True) + EPS)
    normed = values * inverse
    gain_terms = upstream_grad * normed
    gained = upstream_grad * gain_vec
    grad_values = inverse * (gained - normed * jnp.mean(gained * normed, axis=-1, keepdims=True))
    return (grad_values, gain_terms)


def params(mib=56):
    return pltpu.CompilerParams(vmem_limit_bytes=mib * 1024 * 1024)


def cost(us, moved=0):
    return pl.CostEstimate(flops=int(us * 1.15e9), bytes_accessed=int(moved), transcendentals=0)


SMEM = pl.BlockSpec(memory_space=pltpu.SMEM)
VMEM = pl.BlockSpec(memory_space=pltpu.VMEM)


def like(shape, dtype):
    return jax.ShapeDtypeStruct(tuple(shape), dtype)


def own_columns(weight, cols):
    F, rows, lanes = weight.shape
    return weight[...].reshape(F * rows, lanes)[:, :cols]


def weight_spec(moved, width):
    F, _, lanes = moved.shape
    return pl.BlockSpec((F, width // F, lanes), lambda i, o: (0, 2, 0))


def qkv_kernel(parts, heads, hd, order, *refs):
    x_refs = refs[:parts]
    gain, weight, gq, gk, cos, sin, raw_out, low_out = refs[parts:]
    x = jnp.concatenate([r[...] for r in x_refs], axis=0).astype(F32)
    a = (x * lax.rsqrt(jnp.mean(x * x, axis=-1, keepdims=True) + EPS) * gain[...]).astype(BF)
    raw = dot_nn(a, own_columns(weight, (heads + 2) * hd))
    c, s = cos[...], sin[...]
    for h in range(heads + 1):
        u = raw[:, h * hd : (h + 1) * hd]
        raw_out[:, h * hd : (h + 1) * hd] = u
        g = gq[...] if h < heads else gk[...]
        n = u * lax.rsqrt(jnp.mean(u * u, axis=-1, keepdims=True) + EPS) * g
        low_out[:, h * hd : (h + 1) * hd] = (n * c + pltpu.roll(n, hd // 2, axis=1) * s).astype(BF)
    low_out[:, (heads + 1) * hd :] = raw[:, (heads + 1) * hd :].astype(BF)


def block_specs(parts, blk, width):
    return [
        pl.BlockSpec((blk, width), functools.partial(lambda k, i, o: (o[parts * i + k], 0), k))
        for k in range(parts)
    ]


def qkv_call(order, x_all, gain, weight, gq, gk, cos, sin, heads, hd, blk):
    total, width = x_all.shape
    cols = (heads + 2) * hd
    parts = 2
    step = parts * blk
    const = lambda i, o: (0, 0)
    rows = lambda i, o: (i, 0)
    return pl.pallas_call(
        functools.partial(qkv_kernel, parts, heads, hd),
        out_shape=(like((total, (heads + 1) * hd), F32), like((total, cols), BF)),
        grid_spec=pltpu.PrefetchScalarGridSpec(
            num_scalar_prefetch=1,
            grid=(total // step,),
            in_specs=block_specs(parts, blk, width)
            + [
                pl.BlockSpec((1, width), const),
                weight_spec(weight, width),
                pl.BlockSpec((1, hd), const),
                pl.BlockSpec((1, hd), const),
                pl.BlockSpec((step, hd), rows),
                pl.BlockSpec((step, hd), rows),
            ],
            out_specs=(
                pl.BlockSpec((step, (heads + 1) * hd), rows),
                pl.BlockSpec((step, cols), rows),
            ),
        ),
        compiler_params=params(),
        cost_estimate=cost(40),
        name="qkv",
    )(order, *([x_all] * parts), gain, weight, gq, gk, cos, sin)


TQ, TK = 512, 512


def stack_heads(ref, start, heads, hd):
    return jnp.concatenate(
        [ref[pl.ds(start, TQ), h * hd : (h + 1) * hd] for h in range(heads)], axis=0
    )


def attn_kernel(heads, hd, blk, scale, order, length_ref, low, o_even, o_odd, o32_out, lse_out, vext, acc):
    total = low.shape[0]
    length = length_ref[0]
    kcol, vcol = heads * hd, (heads + 1) * hd
    rows = heads * TQ
    vext[:, :hd] = low[:, vcol : vcol + hd]
    vext[:, hd:] = jnp.ones((total, hd), BF)
    full = length // TK
    ends = pl.cdiv(length, TK)

    @pl.loop(0, total // TQ)
    def _(i):
        qs = pl.multiple_of(i * TQ, TQ)
        q = stack_heads(low, qs, heads, hd)
        acc[...] = jnp.zeros_like(acc)

        def tile(j, masked):
            ks = pl.multiple_of(j * TK, TK)
            s = dot_nt(q, low[pl.ds(ks, TK), kcol : kcol + hd])
            p = jnp.exp2(s * (scale * LOG2E))
            if masked:
                kpos = ks + lax.broadcasted_iota(jnp.int32, (rows, TK), 1)
                qpos = qs + lax.broadcasted_iota(jnp.int32, (rows, TK), 0) % TQ
                p = jnp.where((kpos <= qpos) & (kpos < length), p, 0.0)
            acc[...] += dot_nn(p.astype(BF), vext[pl.ds(ks, TK), :])

        clean = jnp.minimum(qs // TK, full)

        @pl.loop(0, clean)
        def _(j):
            tile(j, False)

        @pl.loop(clean, jnp.minimum((qs + TQ - 1) // TK + 1, ends))
        def _(j):
            tile(j, True)

        total_p = acc[:, hd:]
        o = acc[:, :hd] / total_p
        lse_out[i] = jnp.log2(total_p.T[:8])
        for h in range(heads):
            cut = slice(h * hd, (h + 1) * hd)
            part = o[h * TQ : (h + 1) * TQ]
            o32_out[pl.ds(qs, TQ), cut] = part
            for b in range(TQ // blk):
                at = order[i * (TQ // blk) + b]
                low_part = part[b * blk : (b + 1) * blk].astype(BF)

                @pl.when(at % 2 == 0)
                def _():
                    o_even[at // 2, :, cut] = low_part

                @pl.when(at % 2 == 1)
                def _():
                    o_odd[at // 2, :, cut] = low_part


def attn_call(order, length, low, heads, hd, blk, scale):
    total = low.shape[0]
    half = like((total // (2 * blk), blk, heads * hd), BF)
    return pl.pallas_call(
        functools.partial(attn_kernel, heads, hd, blk, scale),
        out_shape=(
            half,
            half,
            like((total, heads * hd), F32),
            like((total // TQ, 8, heads * TQ), F32),
        ),
        in_specs=[SMEM, SMEM, VMEM],
        out_specs=(VMEM,) * 4,
        scratch_shapes=[
            pltpu.VMEM((total, 2 * hd), BF),
            pltpu.VMEM((heads * TQ, 2 * hd), F32),
        ],
        compiler_params=params(),
        cost_estimate=cost(40),
        name="attn_fwd",
    )(order, length, low)


def attn_back_kernel(
    heads, hd, blk, scale, order, length_ref, low, do_even, do_odd, o32, lse, dq_out, dkv_out,
    do_s, delta, dkv,
):
    total = low.shape[0]
    tiles = total // TQ
    length = length_ref[0]
    kcol, vcol = heads * hd, (heads + 1) * hd
    rows = heads * TQ

    @pl.loop(0, tiles)
    def _(i):
        qs = pl.multiple_of(i * TQ, TQ)
        for b in range(TQ // blk):
            at = order[i * (TQ // blk) + b]

            @pl.when(at % 2 == 0)
            def _():
                do_s[pl.ds(qs + b * blk, blk), :] = do_even[at // 2]

            @pl.when(at % 2 == 1)
            def _():
                do_s[pl.ds(qs + b * blk, blk), :] = do_odd[at // 2]

        do_t = stack_heads(do_s, qs, heads, hd).astype(F32) * stack_heads(o32, qs, heads, hd)
        delta[i] = jnp.broadcast_to(jnp.sum(do_t.T, axis=0, keepdims=True), (8, rows))
        dq_out[pl.ds(qs, TQ), :] = jnp.zeros((TQ, heads * hd), F32)

    full = length // TK

    @pl.loop(0, total // TK)
    def _(j):
        ks = pl.multiple_of(j * TK, TK)
        k = low[pl.ds(ks, TK), kcol : kcol + hd]
        v = low[pl.ds(ks, TK), vcol : vcol + hd]
        dkv[...] = jnp.zeros_like(dkv)

        def tile(i, masked):
            qs = pl.multiple_of(i * TQ, TQ)
            q = stack_heads(low, qs, heads, hd)
            do = stack_heads(do_s, qs, heads, hd)
            s = dot_nt(k, q)
            p = jnp.exp2(s * (scale * LOG2E) - lse[i][:1])
            if masked:
                kpos = ks + lax.broadcasted_iota(jnp.int32, (TK, rows), 0)
                qpos = qs + lax.broadcasted_iota(jnp.int32, (TK, rows), 1) % TQ
                p = jnp.where((kpos <= qpos) & (kpos < length), p, 0.0)
            dp = dot_nt(v, do)
            ds = (p * (dp - delta[i][:1])).astype(BF)
            dkv[:, :hd] += dot_nn(ds, q)
            dkv[:, hd:] += dot_nn(p.astype(BF), do)
            dq = dot_tn(ds, k)
            for h in range(heads):
                dq_out[pl.ds(qs, TQ), h * hd : (h + 1) * hd] += dq[h * TQ : (h + 1) * TQ]

        first = ks // TQ
        masked_end = jnp.where(j < full, (ks + TK - 1) // TQ + 1, tiles)

        @pl.loop(first, masked_end)
        def _(i):
            tile(i, True)

        @pl.loop(masked_end, tiles)
        def _(i):
            tile(i, False)

        dkv_out[pl.ds(ks, TK), :hd] = dkv[:, :hd]
        dkv_out[pl.ds(ks, TK), hd:] = dkv[:, hd:]


def attn_back_call(order, length, low, do_even, do_odd, o32, lse, heads, hd, blk, scale):
    total = low.shape[0]
    return pl.pallas_call(
        functools.partial(attn_back_kernel, heads, hd, blk, scale),
        out_shape=(like((total, heads * hd), F32), like((total, 2 * hd), F32)),
        in_specs=[SMEM, SMEM] + [VMEM] * 5,
        out_specs=(VMEM, VMEM),
        scratch_shapes=[
            pltpu.VMEM((total, heads * hd), BF),
            pltpu.VMEM((total // TQ, 8, heads * TQ), F32),
            pltpu.VMEM((TK, 2 * hd), F32),
        ],
        compiler_params=params(),
        cost_estimate=cost(300),
        name="attn_bwd",
    )(order, length, low, do_even, do_odd, o32, lse)


def split_low(values):
    high = values.astype(BF)
    return high, (values - high.astype(F32)).astype(BF)


def head_back_kernel(parts, blk, heads, hd, F, scale, order, f_ref, *refs):
    x_refs = refs[:parts]
    dq, dkv, raw, weight, go, gain, gq, gk, fg0, fg1, cos, sin = refs[parts : parts + 12]
    send_out = refs[parts + 12]
    grad_outs = refs[parts + 13 : parts + 13 + F]
    grad_acc, gain_acc, attn_acc = refs[parts + 13 + F :]
    i = pl.program_id(0)

    @pl.when(i == 0)
    def _():
        grad_acc[...] = jnp.zeros_like(grad_acc)
        gain_acc[...] = jnp.zeros_like(gain_acc)
        attn_acc[...] = jnp.zeros_like(attn_acc)
        rows_own = send_out.shape[1] - go.shape[1]
        for c in range(go.shape[0]):
            send_out[c, rows_own:, :] = go[c]

    c, s = cos[...] * scale, sin[...] * scale
    pieces = []
    for h in range(heads + 1):
        cut = slice(h * hd, (h + 1) * hd)
        g_rot = dq[:, cut] if h < heads else dkv[:, :hd]
        e = g_rot * c + pltpu.roll(g_rot * s, hd // 2, axis=1)
        dv, terms = norm_back(raw[:, cut], gq[...] if h < heads else gk[...], e)
        pieces.append(dv.astype(BF))
        row = 0 if h < heads else 1
        gain_acc[row : row + 1, :] += jnp.sum(terms, axis=0, keepdims=True)
    pieces.append(dkv[:, hd:].astype(BF))
    dqkv = jnp.concatenate(pieces, axis=1)
    da = dot_nt(dqkv, own_columns(weight, (heads + 2) * hd))
    per = (send_out.shape[1] - go.shape[1]) // blk
    normed_parts = []
    for k in range(parts):
        x = x_refs[k][...].astype(F32)
        part = da[k * blk : (k + 1) * blk]
        normed = x * lax.rsqrt(jnp.mean(x * x, axis=-1, keepdims=True) + EPS)
        normed_parts.append((normed * gain[...]).astype(BF))
        attn_acc[...] += jnp.sum(part * normed, axis=0, keepdims=True)
        at = order[parts * i + k]
        send_out[at // per, pl.ds(pl.multiple_of((at % per) * blk, blk), blk), :] = part.astype(BF)
    grad_acc[...] += dot_tn(jnp.concatenate(normed_parts, axis=0), dqkv)

    @pl.when(i == pl.num_programs(0) - 1)
    def _():
        n = grad_acc.shape[0] // F
        for s_ in range(F):
            f = f_ref[0] ^ s_
            at = pl.multiple_of(f * n, n)
            out = grad_outs[s_]
            for b in range(heads + 2):
                out[b * n : (b + 1) * n, :] = grad_acc[
                    pl.ds(at, n), b * hd : (b + 1) * hd
                ].astype(BF)
            base = (heads + 2) * n
            rows = []
            for r in range(n // hd):
                rows.append(attn_acc[:, pl.ds(pl.multiple_of(at + r * hd, hd), hd)])
            for r in range(n // hd):
                lane = pl.ds(pl.multiple_of(at + r * hd, hd), hd)
                rows.append(fg0[:, lane] + fg1[:, lane])
            rows += [gain_acc[0:1, :], gain_acc[1:2, :]]
            rows += [jnp.zeros((1, hd), F32)] * (8 - len(rows))
            high, low = split_low(jnp.concatenate(rows, axis=0))
            out[base : base + 16, :] = jnp.concatenate([high, low], axis=0)


def head_back_call(
    order, f_idx, x_all, dq, dkv, raw, weight, go, gain, gq, gk, fgains, cos, sin, heads, hd, blk, F
):
    total = dq.shape[0]
    width, cols = x_all.shape[1], (heads + 2) * hd
    parts = 4
    step = parts * blk
    ctx = go.shape[0]
    const = lambda i, o: (0, 0)
    const3 = lambda i, o: (0, 0, 0)
    rows = lambda i, o: (i, 0)
    send = (ctx, total // ctx + go.shape[1], width)
    grad = ((heads + 2) * (width // F) + 16, hd)
    return pl.pallas_call(
        functools.partial(head_back_kernel, parts, blk, heads, hd, F, hd**-0.5),
        out_shape=(like(send, BF),) + (like(grad, BF),) * F,
        grid_spec=pltpu.PrefetchScalarGridSpec(
            num_scalar_prefetch=1,
            grid=(total // step,),
            in_specs=[SMEM]
            + block_specs(parts, blk, width)
            + [
                pl.BlockSpec((step, heads * hd), rows),
                pl.BlockSpec((step, 2 * hd), rows),
                pl.BlockSpec((step, (heads + 1) * hd), rows),
                weight_spec(weight, width),
                pl.BlockSpec(go.shape, const3),
                pl.BlockSpec((1, width), const),
                pl.BlockSpec((1, hd), const),
                pl.BlockSpec((1, hd), const),
                pl.BlockSpec((1, width), const),
                pl.BlockSpec((1, width), const),
                pl.BlockSpec((step, hd), rows),
                pl.BlockSpec((step, hd), rows),
            ],
            out_specs=(pl.BlockSpec(send, const3),) + (pl.BlockSpec(grad, const),) * F,
            scratch_shapes=[
                pltpu.VMEM((width, cols), F32),
                pltpu.VMEM((8, hd), F32),
                pltpu.VMEM((1, width), F32),
            ],
        ),
        compiler_params=params(),
        cost_estimate=cost(60),
        name="head_bwd",
    )(
        order, f_idx, *([x_all] * parts), dq, dkv, raw, weight, go, gain, gq, gk, *fgains, cos, sin
    )


def heads_at(c_ref, f, part):
    return 2 * f + ((c_ref[0] % 2) ^ part)


def resid_kernel(F, f_ref, c_ref, o, wo_a, wo_b, x, g2, h_out, m_out, *o_outs):
    n = wo_a.shape[1] // 2
    half = wo_a.shape[2]
    left, right = x[:, :half].astype(F32), x[:, half:].astype(F32)
    for part, wo in enumerate((wo_a, wo_b)):
        for f in range(F):
            of = o[heads_at(c_ref, f, part)]
            left = left + dot_nn(of, wo[f, :n])
            right = right + dot_nn(of, wo[f, n : 2 * n])
    h = jnp.concatenate([left, right], axis=1)
    h_out[...] = h
    m_out[...] = (h * lax.rsqrt(jnp.mean(h * h, axis=-1, keepdims=True) + EPS) * g2[...]).astype(BF)
    for s in range(F):
        for r in range(2):
            o_outs[s][r] = o[(f_ref[0] ^ s) * 2 + r]


def wo_specs(wo_a, wo_b):
    const3 = lambda i: (0, 0, 0)
    return [pl.BlockSpec(wo_b.shape, const3), pl.BlockSpec(wo_b.shape, const3)]


def resid_call(half, f_idx, c_idx, o, wo_a, wo_b, x, g2):
    C, T, hw = o.shape
    D = x.shape[1]
    F = wo_b.shape[0]
    part = like((2, T, hw), BF)
    const = lambda i: (0, 0)
    const3 = lambda i: (0, 0, 0)
    return pl.pallas_call(
        functools.partial(resid_kernel, F),
        out_shape=(like((T, D), F32), like((T, D), BF)) + (part,) * F,
        grid=(1,),
        in_specs=[SMEM, SMEM, pl.BlockSpec(o.shape, const3)]
        + wo_specs(wo_a, wo_b)
        + [pl.BlockSpec((T, D), lambda i: (half, 0)), pl.BlockSpec(g2.shape, const)],
        out_specs=(pl.BlockSpec((T, D), const),) * 2 + (pl.BlockSpec(part.shape, const3),) * F,
        compiler_params=params(),
        cost_estimate=cost(10),
        name="resid",
    )(f_idx, c_idx, o, wo_a, wo_b, x, g2)


def ffn_kernel(F, *refs):
    c_ref = refs[1]
    ms, gys = refs[2 : 2 + F], refs[2 + F : 2 + 2 * F]
    wgu_a, wgu_b, wd, hid_out, dgu_out = refs[2 + 2 * F : 7 + 2 * F]
    dm_outs, wgu = refs[7 + 2 * F : -1], refs[-1]
    n = wgu_a.shape[1]
    for part, src in enumerate((wgu_a, wgu_b)):
        for f in range(F):
            at = pl.multiple_of(heads_at(c_ref, f, part) * n, n)
            wgu[pl.ds(at, n), :] = src[f]
    ffl = wd.shape[0]
    T = ms[0].shape[0]
    m = jnp.concatenate([r[...] for r in ms], axis=0)
    gy = jnp.concatenate([r[...] for r in gys], axis=0)
    gu = dot_nn(m, wgu[...])
    dhid = dot_nt(gy, wd[...])
    gate, up = gu[:, :ffl], gu[:, ffl:]
    sig = 1.0 / (1.0 + jnp.exp(-gate))
    silu = gate * sig
    hid_out[...] = (silu * up).astype(BF)
    dgu = jnp.concatenate(
        [(dhid * up * (sig + silu * (1.0 - sig))).astype(BF), (dhid * silu).astype(BF)], axis=1
    )
    dgu_out[...] = dgu
    dm = dot_nt(dgu, wgu[...]).astype(BF)
    for s in range(F):
        dm_outs[s][...] = dm[s * T : (s + 1) * T]


def gy_spec(T, D, half):
    return pl.BlockSpec((T, D), lambda i, f: (half, 0))


def ffn_call(half, f_idx, c_idx, ms, gys, wgu_a, wgu_b, wd):
    F = len(ms)
    T, D = ms[0].shape
    ffl = wd.shape[0]
    const = lambda i, f: (0, 0)
    return pl.pallas_call(
        functools.partial(ffn_kernel, F),
        out_shape=(like((F * T, ffl), BF), like((F * T, 2 * ffl), BF)) + (like((T, D), BF),) * F,
        grid_spec=pltpu.PrefetchScalarGridSpec(
            num_scalar_prefetch=1,
            grid=(1,),
            in_specs=[SMEM]
            + [pl.BlockSpec((T, D), const)] * F
            + [gy_spec(T, D, half)] * F
            + [pl.BlockSpec(wgu_a.shape, lambda i, f: (0, 0, 0))] * 2
            + [pl.BlockSpec(wd.shape, const)],
            out_specs=(
                pl.BlockSpec((F * T, ffl), const),
                pl.BlockSpec((F * T, 2 * ffl), const),
            )
            + (pl.BlockSpec((T, D), const),) * F,
            scratch_shapes=[pltpu.VMEM((D, wgu_a.shape[2]), BF)],
        ),
        compiler_params=params(),
        cost_estimate=cost(10),
        name="ffn",
    )(f_idx, c_idx, *ms, *gys, wgu_a, wgu_b, wd)


def resid_back_kernel(F, c_ref, *refs):
    dms = refs[:F]
    wo_a, wo_b, h, gy, g2, dh_out, dhb_out, do_out, gain_out = refs[F:]
    total = dms[0][...].astype(F32)
    for s in range(1, F):
        total = total + dms[s][...].astype(F32)
    dv, terms = norm_back(h[...], g2[...], total)
    gain_out[...] = jnp.sum(terms, axis=0, keepdims=True)
    dh = gy[...].astype(F32) + dv
    dh_out[...] = dh
    low = dh.astype(BF)
    dhb_out[...] = low
    n = wo_a.shape[1] // 2
    half = wo_a.shape[2]
    for part, wo in enumerate((wo_a, wo_b)):
        for f in range(F):
            do = dot_nt(low[:, :half], wo[f, :n]) + dot_nt(low[:, half:], wo[f, n : 2 * n])
            do_out[heads_at(c_ref, f, part)] = do.astype(BF)


def resid_back_call(half, c_idx, dms, h, gy, g2, wo_a, wo_b):
    F = len(dms)
    T, D = h.shape
    hw = wo_b.shape[1] // 2
    const = lambda i: (0, 0)
    return pl.pallas_call(
        functools.partial(resid_back_kernel, F),
        out_shape=(
            like((T, D), F32),
            like((T, D), BF),
            like((2 * F, T, hw), BF),
            like((1, D), F32),
        ),
        grid=(1,),
        in_specs=[SMEM]
        + [pl.BlockSpec((T, D), const)] * F
        + wo_specs(wo_a, wo_b)
        + [
            pl.BlockSpec((T, D), const),
            pl.BlockSpec((T, D), lambda i: (half, 0)),
            pl.BlockSpec(g2.shape, const),
        ],
        out_specs=(
            pl.BlockSpec((T, D), const),
            pl.BlockSpec((T, D), const),
            pl.BlockSpec((2 * F, T, hw), lambda i: (0, 0, 0)),
            pl.BlockSpec((1, D), const),
        ),
        compiler_params=params(),
        cost_estimate=cost(10),
        name="resid_bwd",
    )(c_idx, *dms, wo_a, wo_b, h, gy, g2)


LANE = 256


def wgrad_kernel(F, C, f_ref, *refs):
    ms, gys = refs[: 2 * F], refs[2 * F : 4 * F]
    hid0, hid1, dgu0, dgu1, out, gd = refs[4 * F :]
    D = ms[0].shape[1]
    n = D // F
    R = n // C
    J = dgu0.shape[1] // LANE
    for s in range(F):
        lane = pl.ds(pl.multiple_of((f_ref[0] ^ s) * n, n), n)
        lhs = [jnp.concatenate([r[:, lane] for r in ms[b * F : (b + 1) * F]], axis=0) for b in (0, 1)]
        res = (dot_tn(lhs[0], dgu0[...]) + dot_tn(lhs[1], dgu1[...])).astype(BF)
        for c in range(C):
            for j in range(J):
                out[c, (s * J + j) * R : (s * J + j + 1) * R, :] = res[
                    c * R : (c + 1) * R, j * LANE : (j + 1) * LANE
                ]
    hid = jnp.concatenate([hid0[...], hid1[...]], axis=0)
    gy = jnp.concatenate([r[...] for r in gys], axis=0)
    gd[...] = dot_tn(hid, gy).astype(BF)
    base = F * J * R
    n = gd.shape[0] // C
    for c in range(C):
        for j in range(D // LANE):
            out[c, base + j * n : base + (j + 1) * n, :] = gd[
                c * n : (c + 1) * n, j * LANE : (j + 1) * LANE
            ]


def wgrad_call(f_idx, ms, gys, hiddens, dgus, C):
    F = len(ms) // 2
    T, D = ms[0].shape
    rows, ffl = hiddens[0].shape
    total = 3 * D * ffl // (C * LANE)
    const = lambda i, f: (0, 0)
    return pl.pallas_call(
        functools.partial(wgrad_kernel, F, C),
        out_shape=like((C, total, LANE), BF),
        grid_spec=pltpu.PrefetchScalarGridSpec(
            num_scalar_prefetch=1,
            grid=(1,),
            in_specs=[pl.BlockSpec((T, D), const)] * (2 * F)
            + [gy_spec(T, D, half) for half in range(2) for s in range(F)]
            + [pl.BlockSpec((rows, ffl), const)] * 2
            + [pl.BlockSpec((rows, 2 * ffl), const)] * 2,
            out_specs=pl.BlockSpec((C, total, LANE), lambda i, f: (0, 0, 0)),
            scratch_shapes=[pltpu.VMEM((ffl, D), BF)],
        ),
        compiler_params=params(),
        cost_estimate=cost(15),
        name="wgrad",
    )(f_idx, *ms, *gys, *gys, *hiddens, *dgus)


def ffn_out_kernel(F, hid0, hid1, wd, *outs):
    T = hid0.shape[0] // F
    for half, hid in enumerate((hid0, hid1)):
        res = dot_nn(hid[...], wd[...]).astype(BF)
        for s in range(F):
            outs[s][half * T : (half + 1) * T, :] = res[s * T : (s + 1) * T]


def ffn_out_call(hiddens, wd, F):
    rows = hiddens[0].shape[0]
    D = wd.shape[1]
    return pl.pallas_call(
        functools.partial(ffn_out_kernel, F),
        out_shape=(like((2 * rows // F, D), BF),) * F,
        in_specs=[VMEM] * 3,
        out_specs=(VMEM,) * F,
        compiler_params=params(),
        cost_estimate=cost(5),
        name="ffn_out",
    )(*hiddens, wd)


def go_kernel(parts, *refs):
    os, ds = refs[:parts], refs[parts : 2 * parts]
    out = refs[2 * parts]
    low = jnp.concatenate([r[...] for r in ds], axis=0)
    rows = [
        dot_tn(jnp.concatenate([r[p] for r in os], axis=0), low).astype(BF)
        for p in range(os[0].shape[0])
    ]
    wide = jnp.concatenate(rows, axis=0)
    C, n, _ = out.shape
    for c in range(C):
        out[c] = wide[c * n : (c + 1) * n]


def go_call(os, ds, C):
    per, _, hw = os[0].shape
    D = ds[0].shape[1]
    return pl.pallas_call(
        functools.partial(go_kernel, len(os)),
        out_shape=like((C, per * hw // C, D), BF),
        in_specs=[VMEM] * (2 * len(os)),
        out_specs=VMEM,
        compiler_params=params(),
        cost_estimate=cost(5),
        name="wgrad_out",
    )(*os, *ds)


def combine_kernel(F, body_rows, *refs):
    out = refs[F]
    total = refs[0][:body_rows, :].astype(F32)
    for s in range(1, F):
        total = total + refs[s][:body_rows, :].astype(F32)
    out[:body_rows, :] = total.astype(BF)
    small = jnp.zeros((8, out.shape[1]), F32)
    for s in range(F):
        both = refs[s][body_rows:, :].astype(F32)
        small = small + both[:8] + both[8:]
    high, low = split_low(small)
    out[body_rows:, :] = jnp.concatenate([high, low], axis=0)


def combine_call(parts):
    rows, hd = parts[0].shape
    return pl.pallas_call(
        functools.partial(combine_kernel, len(parts), rows - 16),
        out_shape=like((rows, hd), BF),
        in_specs=[VMEM] * len(parts),
        out_specs=VMEM,
        compiler_params=params(8),
        cost_estimate=cost(2),
        name="combine",
    )(*parts)


def unpack_ffn_kernel(F, R, J, f_ref, src, gate_out, up_out, down_out):
    half = J // 2
    ffl = half * LANE
    for s in range(F):
        base = pl.multiple_of((f_ref[0] ^ s) * ffl, ffl)
        for j in range(J):
            (gate_out if j < half else up_out)[:, pl.ds(base + (j % half) * LANE, LANE)] = src[
                0, (s * J + j) * R : (s * J + j + 1) * R, :
            ].astype(F32)
    n, wide = down_out.shape
    for j in range(wide // LANE):
        at = F * J * R + j * n
        down_out[:, j * LANE : (j + 1) * LANE] = src[0, at : at + n, :].astype(F32)


def unpack_ffn_call(f_idx, src, F, R, FF, D):
    C, rows, _ = src.shape
    J = 2 * FF // (F * LANE)
    n = FF // (F * C)
    row = lambda c, f: (c, 0)
    return pl.pallas_call(
        functools.partial(unpack_ffn_kernel, F, R, J),
        out_shape=(like((C * R, FF), F32), like((C * R, FF), F32), like((C * n, D), F32)),
        grid_spec=pltpu.PrefetchScalarGridSpec(
            num_scalar_prefetch=1,
            grid=(C,),
            in_specs=[pl.BlockSpec((1, rows, LANE), lambda c, f: (c, 0, 0))],
            out_specs=(
                pl.BlockSpec((R, FF), row),
                pl.BlockSpec((R, FF), row),
                pl.BlockSpec((n, D), row),
            ),
        ),
        compiler_params=params(16),
        cost_estimate=cost(8),
        name="unpack_ffn",
    )(f_idx, src)


def join_kernel(p, o, out):
    n, hd = p.shape
    out[:n, :] = p[...]
    rows, wide = o.shape
    for j in range(wide // hd):
        out[n + j * rows : n + (j + 1) * rows, :] = o[:, j * hd : (j + 1) * hd]


def join_call(p, summed, n_o):
    n, hd = p.shape
    total, D = summed.shape
    rows = n + n_o * D // hd
    return pl.pallas_call(
        join_kernel,
        out_shape=like((rows, hd), BF),
        grid=(1,),
        in_specs=[
            pl.BlockSpec((n, hd), lambda i: (0, 0)),
            pl.BlockSpec((n_o, D), lambda i: (total // n_o - 1, 0)),
        ],
        out_specs=pl.BlockSpec((rows, hd), lambda i: (0, 0)),
        compiler_params=params(8),
        cost_estimate=cost(2),
        name="join",
    )(p, summed)


def unpack_attn_kernel(heads, hd, rep, src, q_out, k_out, v_out, o_out, small_out):
    C = src.shape[0]
    rows = q_out.shape[0]
    n = o_out.shape[0] // C
    small = jnp.zeros((8, hd), F32)
    for c in range(C):
        for h in range(heads):
            at = (c * heads + h) * hd
            q_out[:, at : at + hd] = src[c, h * rows : (h + 1) * rows, :].astype(F32)
        lane = slice((c // rep) * hd, (c // rep + 1) * hd)
        for h, out in ((heads, k_out), (heads + 1, v_out)):
            value = src[c, h * rows : (h + 1) * rows, :].astype(F32)
            if c % rep == 0:
                out[:, lane] = value
            else:
                out[:, lane] += value
        at = (heads + 2) * rows
        both = src[c, at : at + 16, :].astype(F32)
        small = small + both[:8] + both[8:]
        for j in range(o_out.shape[1] // hd):
            o_out[c * n : (c + 1) * n, j * hd : (j + 1) * hd] = src[
                c, at + 16 + j * n : at + 16 + (j + 1) * n, :
            ].astype(F32)
    small_out[...] = small


def unpack_attn_call(src, heads, hd, rep, rows, n_o, D):
    C = src.shape[0]
    return pl.pallas_call(
        functools.partial(unpack_attn_kernel, heads, hd, rep),
        out_shape=(
            like((rows, C * heads * hd), F32),
            like((rows, C * hd // rep), F32),
            like((rows, C * hd // rep), F32),
            like((C * n_o, D), F32),
            like((8, hd), F32),
        ),
        in_specs=[VMEM],
        out_specs=(VMEM,) * 5,
        compiler_params=params(20),
        cost_estimate=cost(5),
        name="unpack_attn",
    )(src)


def after(value, *others):
    return lax.optimization_barrier((value,) + others)[0]


def body(
    block_input,
    cotangent,
    seq_lengths,
    block_table,
    query_proj,
    key_proj,
    value_proj,
    output_proj,
    gate_proj,
    up_proj,
    down_proj,
    attn_norm,
    ffn_norm,
    query_norm,
    key_norm,
):
    C = lax.axis_size("ctx")
    F = lax.axis_size("fsdp")
    c_at = lax.axis_index("ctx")
    f_at = lax.axis_index("fsdp")
    core = lax.rem(c_at, 2)
    c_idx, f_idx = c_at[None].astype(jnp.int32), f_at[None].astype(jnp.int32)
    T, D = block_input.shape[1:]
    S = T * C
    blocks = block_table.shape[0]
    blk = S // blocks
    hd = query_norm.shape[0] * F
    HQ = query_proj.shape[1] // hd
    KV = key_proj.shape[1] // hd
    FF = gate_proj.shape[1]
    heads = HQ // C
    rep = max(1, C // KV)
    FFl = FF // F
    R = D // (F * C)
    scale = 1.0 / math.sqrt(hd)
    length = seq_lengths.astype(jnp.int32)
    own_blocks = lax.dynamic_slice_in_dim(block_table, c_at * (blocks // C), blocks // C)
    own_pos = (own_blocks[:, None] * blk + jnp.arange(blk, dtype=jnp.int32)[None, :]).reshape(-1)
    live = (own_pos < length[0]).astype(F32)[:, None]
    order = jnp.argsort(block_table).astype(jnp.int32)

    def gather_f(v):
        return lax.all_to_all(jnp.broadcast_to(v[None], (F,) + v.shape), "fsdp", 0, 0)

    def exchange_c(v):
        return lax.all_to_all(v, "ctx", 0, 0)

    def to_partner(v, s):
        return lax.ppermute(v, "fsdp", [(i, i ^ s) for i in range(F)])

    def gather_x(v):
        return [v] + [to_partner(v, s) for s in range(1, F)]

    def exchange_x(vs):
        return [vs[0]] + [to_partner(vs[s], s) for s in range(1, F)]

    def other_core(v):
        return lax.ppermute(v, "ctx", [(i, i ^ 1) for i in range(C)])

    def gather_c(v):
        parts = [v] + [
            lax.ppermute(v, "ctx", [(i, i ^ (2 * k)) for i in range(C)]) for k in range(1, C // 2)
        ]
        return [p for v in parts for p in (v, other_core(v))]

    x_all = lax.all_gather(block_input[0], "ctx", axis=0, tiled=True)
    kv_at = (c_at // rep) * hd
    cols = (heads + 2) * hd
    w_own = jnp.concatenate(
        [
            lax.dynamic_slice_in_dim(query_proj, c_at * heads * hd, heads * hd, 1),
            lax.dynamic_slice_in_dim(key_proj, kv_at, hd, 1),
            lax.dynamic_slice_in_dim(value_proj, kv_at, hd, 1),
        ],
        axis=1,
    ).astype(BF)
    gains_own = jnp.concatenate([attn_norm, ffn_norm, query_norm, key_norm]).astype(BF)
    lanes = D // 2
    w_own = jnp.pad(w_own, ((0, 0), (0, lanes - cols)))
    gain_rows = -(-gains_own.shape[0] // (16 * lanes)) * 16
    gains_own = jnp.pad(gains_own, (0, gain_rows * lanes - gains_own.shape[0]))
    wo_rows = output_proj.shape[0] // 2
    wo_half = lax.dynamic_slice_in_dim(output_proj, core * wo_rows, wo_rows, 0).astype(BF)
    n_wo = 2 * wo_rows
    moved = gather_f(
        jnp.concatenate(
            [wo_half[:, :lanes], wo_half[:, lanes:], w_own, gains_own.reshape(gain_rows, lanes)],
            axis=0,
        )
    )
    gains = moved[:, n_wo + D // F :].reshape(F, gain_rows * lanes).astype(F32)
    g1 = gains[:, : D // F].reshape(1, D)
    g2 = gains[:, D // F : 2 * D // F].reshape(1, D)
    gq = gains[:, 2 * D // F : (2 * D + hd) // F].reshape(1, hd)
    gk = gains[:, (2 * D + hd) // F : (2 * D + 2 * hd) // F].reshape(1, hd)
    wo_a = moved
    wo_b = other_core(moved[:, :n_wo])
    gu_rows = D // F // 2
    half_of = lambda w: lax.dynamic_slice_in_dim(w, core * gu_rows, gu_rows, 0).astype(BF)
    wgu_half = jnp.concatenate(
        [half_of(gate_proj).reshape(gu_rows, F, FFl), half_of(up_proj).reshape(gu_rows, F, FFl)],
        axis=2,
    )
    wgu_a = lax.all_to_all(after(jnp.swapaxes(wgu_half, 0, 1), moved), "fsdp", 0, 0)
    wd = down_proj.astype(BF)
    gy = (cotangent[0].astype(F32) * live).astype(BF)
    gys = gather_x(after(gy, wgu_a))

    half = hd // 2
    frequency = THETA ** (-(jnp.arange(half).astype(F32) * 2.0 / hd))
    angles = jnp.arange(S, dtype=jnp.int32).astype(F32)[:, None] * frequency[None, :]
    cos_t, sin_t = jnp.cos(angles), jnp.sin(angles)
    cos_t = jnp.concatenate([cos_t, cos_t], -1)
    sin_t = jnp.concatenate([-sin_t, sin_t], -1)
    raw, low = qkv_call(order, x_all, g1, moved, gq, gk, cos_t, sin_t, heads, hd, blk)
    o_even, o_odd, o32, lse = attn_call(order, length, low, heads, hd, blk, scale)


    x = block_input[0]
    o_nat = [exchange_c(after(o_even, wgu_a))]
    o_nat.append(exchange_c(after(o_odd, o_nat[0])))
    hs, ms, os, hiddens, dgus, dhs, dhbs, dos, fgains = [], [], [], [], [], [], [], [], []
    for b in range(2):
        o_b = o_nat[b] if b == 0 else after(o_nat[b], *gys)
        h, m_own, *o_parts = resid_call(b, f_idx, c_idx, o_b, wo_a, wo_b, x, g2)
        hs.append(h)
        os.append(o_parts)
        ms.append(gather_x(m_own))
    dms = []
    wgu_a = after(wgu_a, hs[0])
    wgu_b = other_core(wgu_a)
    for b in range(2):
        hidden, dgu, *dm_parts = ffn_call(b, f_idx, c_idx, ms[b], gys, wgu_a, wgu_b, wd)
        hiddens.append(hidden)
        dgus.append(dgu)
        dms.append(exchange_x(dm_parts))
    hiddens[1] = after(hiddens[1], *dms[0])
    packed = wgrad_call(f_idx, ms[0] + ms[1], gys, hiddens, dgus, C)
    hs[1] = after(hs[1], packed)
    for b in range(2):
        dh, dhb, do_nat, fgain = resid_back_call(b, c_idx, dms[b], hs[b], gy, g2, wo_a, wo_b)
        dhs.append(dh)
        dhbs.append(dhb)
        fgains.append(fgain)
        dos.append(exchange_c(do_nat))

    owned = lax.psum_scatter(packed.reshape(-1, LANE), "ctx", scatter_dimension=0, tiled=True)
    owned = after(owned, dos[1])
    n_s = 2 * FFl // LANE * R
    owned_gu = exchange_x([owned[s * n_s : (s + 1) * n_s] for s in range(F)])
    all_ffn = lax.all_gather(jnp.concatenate(owned_gu + [owned[F * n_s :]], axis=0), "ctx", axis=0)
    grad_gate, grad_up, grad_down = unpack_ffn_call(f_idx, all_ffn, F, R, FF, D)

    ffn_parts = exchange_x([after(v, *owned_gu) for v in ffn_out_call(hiddens, wd, F)])
    ffn = sum(p.astype(F32) for p in ffn_parts)
    block_output = ((jnp.concatenate(hs, axis=0) + ffn) * live).astype(BF)[None]

    dq, dkv = attn_back_call(order, length, low, dos[0], dos[1], o32, lse, heads, hd, blk, scale)
    o_f = [p for parts in os for p in exchange_x([after(v, dhbs[1]) for v in parts])]
    dhb_f = [p for v in dhbs for p in gather_x(v)]
    go = go_call(o_f, dhb_f, C)
    n_o = go.shape[1]
    send, *grad_parts = head_back_call(
        order, f_idx, x_all, after(dq, *ffn_parts), dkv, raw, moved, go, g1, gq, gk, fgains, cos_t, sin_t,
        heads, hd, blk, F,
    )
    summed = lax.psum_scatter(after(send, all_ffn).reshape(-1, D), "ctx", scatter_dimension=0, tiled=True)
    dx, _ = norm_back(x.astype(F32), g1, summed[:T].astype(F32))
    grad_input = (jnp.concatenate(dhs, axis=0) + dx)[None]

    own_p = combine_call(exchange_x(grad_parts))
    joined = lax.all_gather(join_call(own_p, summed, n_o), "ctx", axis=0)
    grad_query, grad_key, grad_value, grad_output, small = unpack_attn_call(
        joined, heads, hd, rep, D // F, n_o, D
    )
    n_r = D // F // hd
    own_gain = lambda r: lax.dynamic_slice_in_dim(small[2 * n_r + r], f_at * (hd // F), hd // F)

    return (
        block_output,
        grad_input,
        grad_query,
        grad_key,
        grad_value,
        grad_output,
        grad_gate,
        grad_up,
        grad_down,
        small[:n_r].reshape(-1),
        small[n_r : 2 * n_r].reshape(-1),
        own_gain(0),
        own_gain(1),
    )


def solution(mesh):
    matrix, vector = P("fsdp", None), P("fsdp")
    rows = P("fsdp", "ctx", None)
    in_specs = (rows, rows, vector, P()) + (matrix,) * 7 + (vector,) * 4
    out_specs = (rows, rows) + (matrix,) * 7 + (vector,) * 4
    return jax.shard_map(body, mesh=mesh, in_specs=in_specs, out_specs=out_specs, check_vma=False)
```

```python
import functools
import math

import jax
import jax.numpy as jnp
from jax import lax
from jax.experimental import pallas as pl
from jax.experimental.pallas import tpu as pltpu
from jax.sharding import PartitionSpec as P

EPS = 1e-06
THETA = 1000000.0
BF = jnp.bfloat16
F32 = jnp.float32
LOG2E = math.log2(math.e)


def dot_nn(left, right):
    return lax.dot_general(left, right, (((1,), (0,)), ((), ())), preferred_element_type=F32)


def dot_nt(left, right):
    return lax.dot_general(left, right, (((1,), (1,)), ((), ())), preferred_element_type=F32)


def dot_tn(left, right):
    return lax.dot_general(left, right, (((0,), (0,)), ((), ())), preferred_element_type=F32)


def norm_back(values, gain_vec, upstream_grad):
    inverse = lax.rsqrt(jnp.mean(values * values, axis=-1, keepdims=True) + EPS)
    normed = values * inverse
    gain_terms = upstream_grad * normed
    gained = upstream_grad * gain_vec
    grad_values = inverse * (gained - normed * jnp.mean(gained * normed, axis=-1, keepdims=True))
    return (grad_values, gain_terms)


def params(mib=56):
    return pltpu.CompilerParams(vmem_limit_bytes=mib * 1024 * 1024)


def cost(us, moved=0):
    return pl.CostEstimate(flops=int(us * 1.15e9), bytes_accessed=int(moved), transcendentals=0)


SMEM = pl.BlockSpec(memory_space=pltpu.SMEM)
VMEM = pl.BlockSpec(memory_space=pltpu.VMEM)


def like(shape, dtype):
    return jax.ShapeDtypeStruct(tuple(shape), dtype)


def own_columns(weight, cols):
    F, rows, lanes = weight.shape
    return weight[...].reshape(F * rows, lanes)[:, :cols]


def weight_spec(moved, width):
    F, _, lanes = moved.shape
    return pl.BlockSpec((F, width // F, lanes), lambda i, o: (0, 2, 0))


def qkv_kernel(parts, heads, hd, order, *refs):
    x_refs = refs[:parts]
    gain, weight, gq, gk, cos, sin, raw_out, low_out = refs[parts:]
    x = jnp.concatenate([r[...] for r in x_refs], axis=0).astype(F32)
    a = (x * lax.rsqrt(jnp.mean(x * x, axis=-1, keepdims=True) + EPS) * gain[...]).astype(BF)
    raw = dot_nn(a, own_columns(weight, (heads + 2) * hd))
    c, s = cos[...], sin[...]
    for h in range(heads + 1):
        u = raw[:, h * hd : (h + 1) * hd]
        raw_out[:, h * hd : (h + 1) * hd] = u
        g = gq[...] if h < heads else gk[...]
        n = u * lax.rsqrt(jnp.mean(u * u, axis=-1, keepdims=True) + EPS) * g
        low_out[:, h * hd : (h + 1) * hd] = (n * c + pltpu.roll(n, hd // 2, axis=1) * s).astype(BF)
    low_out[:, (heads + 1) * hd :] = raw[:, (heads + 1) * hd :].astype(BF)


def block_specs(parts, blk, width):
    return [
        pl.BlockSpec((blk, width), functools.partial(lambda k, i, o: (o[parts * i + k], 0), k))
        for k in range(parts)
    ]


def qkv_call(order, x_all, gain, weight, gq, gk, cos, sin, heads, hd, blk):
    total, width = x_all.shape
    cols = (heads + 2) * hd
    parts = 2
    step = parts * blk
    const = lambda i, o: (0, 0)
    rows = lambda i, o: (i, 0)
    return pl.pallas_call(
        functools.partial(qkv_kernel, parts, heads, hd),
        out_shape=(like((total, (heads + 1) * hd), F32), like((total, cols), BF)),
        grid_spec=pltpu.PrefetchScalarGridSpec(
            num_scalar_prefetch=1,
            grid=(total // step,),
            in_specs=block_specs(parts, blk, width)
            + [
                pl.BlockSpec((1, width), const),
                weight_spec(weight, width),
                pl.BlockSpec((1, hd), const),
                pl.BlockSpec((1, hd), const),
                pl.BlockSpec((step, hd), rows),
                pl.BlockSpec((step, hd), rows),
            ],
            out_specs=(
                pl.BlockSpec((step, (heads + 1) * hd), rows),
                pl.BlockSpec((step, cols), rows),
            ),
        ),
        compiler_params=params(),
        cost_estimate=cost(40),
        name="qkv",
    )(order, *([x_all] * parts), gain, weight, gq, gk, cos, sin)


TQ, TK = 512, 512


def stack_heads(ref, start, heads, hd):
    return jnp.concatenate(
        [ref[pl.ds(start, TQ), h * hd : (h + 1) * hd] for h in range(heads)], axis=0
    )


def attn_kernel(heads, hd, blk, scale, order, length_ref, low, o_even, o_odd, o32_out, lse_out, vext, acc):
    total = low.shape[0]
    length = length_ref[0]
    kcol, vcol = heads * hd, (heads + 1) * hd
    rows = heads * TQ
    vext[:, :hd] = low[:, vcol : vcol + hd]
    vext[:, hd:] = jnp.ones((total, hd), BF)
    full = length // TK
    ends = pl.cdiv(length, TK)

    @pl.loop(0, total // TQ)
    def _(i):
        qs = pl.multiple_of(i * TQ, TQ)
        q = stack_heads(low, qs, heads, hd)
        acc[...] = jnp.zeros_like(acc)

        def tile(j, masked):
            ks = pl.multiple_of(j * TK, TK)
            s = dot_nt(q, low[pl.ds(ks, TK), kcol : kcol + hd])
            p = jnp.exp2(s * (scale * LOG2E))
            if masked:
                kpos = ks + lax.broadcasted_iota(jnp.int32, (rows, TK), 1)
                qpos = qs + lax.broadcasted_iota(jnp.int32, (rows, TK), 0) % TQ
                p = jnp.where((kpos <= qpos) & (kpos < length), p, 0.0)
            acc[...] += dot_nn(p.astype(BF), vext[pl.ds(ks, TK), :])

        clean = jnp.minimum(qs // TK, full)

        @pl.loop(0, clean)
        def _(j):
            tile(j, False)

        @pl.loop(clean, jnp.minimum((qs + TQ - 1) // TK + 1, ends))
        def _(j):
            tile(j, True)

        total_p = acc[:, hd:]
        o = acc[:, :hd] / total_p
        lse_out[i] = jnp.log2(total_p.T[:8])
        for h in range(heads):
            cut = slice(h * hd, (h + 1) * hd)
            part = o[h * TQ : (h + 1) * TQ]
            o32_out[pl.ds(qs, TQ), cut] = part
            for b in range(TQ // blk):
                at = order[i * (TQ // blk) + b]
                low_part = part[b * blk : (b + 1) * blk].astype(BF)

                @pl.when(at % 2 == 0)
                def _():
                    o_even[at // 2, :, cut] = low_part

                @pl.when(at % 2 == 1)
                def _():
                    o_odd[at // 2, :, cut] = low_part


def attn_call(order, length, low, heads, hd, blk, scale):
    total = low.shape[0]
    half = like((total // (2 * blk), blk, heads * hd), BF)
    return pl.pallas_call(
        functools.partial(attn_kernel, heads, hd, blk, scale),
        out_shape=(
            half,
            half,
            like((total, heads * hd), F32),
            like((total // TQ, 8, heads * TQ), F32),
        ),
        in_specs=[SMEM, SMEM, VMEM],
        out_specs=(VMEM,) * 4,
        scratch_shapes=[
            pltpu.VMEM((total, 2 * hd), BF),
            pltpu.VMEM((heads * TQ, 2 * hd), F32),
        ],
        compiler_params=params(),
        cost_estimate=cost(40),
        name="attn_fwd",
    )(order, length, low)


def attn_back_kernel(
    heads, hd, blk, scale, order, length_ref, low, do_even, do_odd, o32, lse, dq_out, dkv_out,
    do_s, delta, dkv,
):
    total = low.shape[0]
    tiles = total // TQ
    length = length_ref[0]
    kcol, vcol = heads * hd, (heads + 1) * hd
    rows = heads * TQ

    @pl.loop(0, tiles)
    def _(i):
        qs = pl.multiple_of(i * TQ, TQ)
        for b in range(TQ // blk):
            at = order[i * (TQ // blk) + b]

            @pl.when(at % 2 == 0)
            def _():
                do_s[pl.ds(qs + b * blk, blk), :] = do_even[at // 2]

            @pl.when(at % 2 == 1)
            def _():
                do_s[pl.ds(qs + b * blk, blk), :] = do_odd[at // 2]

        do_t = stack_heads(do_s, qs, heads, hd).astype(F32) * stack_heads(o32, qs, heads, hd)
        delta[i] = jnp.broadcast_to(jnp.sum(do_t.T, axis=0, keepdims=True), (8, rows))
        dq_out[pl.ds(qs, TQ), :] = jnp.zeros((TQ, heads * hd), F32)

    full = length // TK

    @pl.loop(0, total // TK)
    def _(j):
        ks = pl.multiple_of(j * TK, TK)
        k = low[pl.ds(ks, TK), kcol : kcol + hd]
        v = low[pl.ds(ks, TK), vcol : vcol + hd]
        dkv[...] = jnp.zeros_like(dkv)

        def tile(i, masked):
            qs = pl.multiple_of(i * TQ, TQ)
            q = stack_heads(low, qs, heads, hd)
            do = stack_heads(do_s, qs, heads, hd)
            s = dot_nt(k, q)
            p = jnp.exp2(s * (scale * LOG2E) - lse[i][:1])
            if masked:
                kpos = ks + lax.broadcasted_iota(jnp.int32, (TK, rows), 0)
                qpos = qs + lax.broadcasted_iota(jnp.int32, (TK, rows), 1) % TQ
                p = jnp.where((kpos <= qpos) & (kpos < length), p, 0.0)
            dp = dot_nt(v, do)
            ds = (p * (dp - delta[i][:1])).astype(BF)
            dkv[:, :hd] += dot_nn(ds, q)
            dkv[:, hd:] += dot_nn(p.astype(BF), do)
            dq = dot_tn(ds, k)
            for h in range(heads):
                dq_out[pl.ds(qs, TQ), h * hd : (h + 1) * hd] += dq[h * TQ : (h + 1) * TQ]

        first = ks // TQ
        masked_end = jnp.where(j < full, (ks + TK - 1) // TQ + 1, tiles)

        @pl.loop(first, masked_end)
        def _(i):
            tile(i, True)

        @pl.loop(masked_end, tiles)
        def _(i):
            tile(i, False)

        dkv_out[pl.ds(ks, TK), :hd] = dkv[:, :hd]
        dkv_out[pl.ds(ks, TK), hd:] = dkv[:, hd:]


def attn_back_call(order, length, low, do_even, do_odd, o32, lse, heads, hd, blk, scale):
    total = low.shape[0]
    return pl.pallas_call(
        functools.partial(attn_back_kernel, heads, hd, blk, scale),
        out_shape=(like((total, heads * hd), F32), like((total, 2 * hd), F32)),
        in_specs=[SMEM, SMEM] + [VMEM] * 5,
        out_specs=(VMEM, VMEM),
        scratch_shapes=[
            pltpu.VMEM((total, heads * hd), BF),
            pltpu.VMEM((total // TQ, 8, heads * TQ), F32),
            pltpu.VMEM((TK, 2 * hd), F32),
        ],
        compiler_params=params(),
        cost_estimate=cost(300),
        name="attn_bwd",
    )(order, length, low, do_even, do_odd, o32, lse)


def split_low(values):
    high = values.astype(BF)
    return high, (values - high.astype(F32)).astype(BF)


def head_back_kernel(parts, blk, heads, hd, F, scale, order, f_ref, *refs):
    x_refs = refs[:parts]
    dq, dkv, raw, weight, go, gain, gq, gk, fg0, fg1, cos, sin = refs[parts : parts + 12]
    send_out = refs[parts + 12]
    grad_outs = refs[parts + 13 : parts + 13 + F]
    grad_acc, gain_acc, attn_acc = refs[parts + 13 + F :]
    i = pl.program_id(0)

    @pl.when(i == 0)
    def _():
        grad_acc[...] = jnp.zeros_like(grad_acc)
        gain_acc[...] = jnp.zeros_like(gain_acc)
        attn_acc[...] = jnp.zeros_like(attn_acc)
        rows_own = send_out.shape[1] - go.shape[1]
        for c in range(go.shape[0]):
            send_out[c, rows_own:, :] = go[c]

    c, s = cos[...] * scale, sin[...] * scale
    pieces = []
    for h in range(heads + 1):
        cut = slice(h * hd, (h + 1) * hd)
        g_rot = dq[:, cut] if h < heads else dkv[:, :hd]
        e = g_rot * c + pltpu.roll(g_rot * s, hd // 2, axis=1)
        dv, terms = norm_back(raw[:, cut], gq[...] if h < heads else gk[...], e)
        pieces.append(dv.astype(BF))
        row = 0 if h < heads else 1
        gain_acc[row : row + 1, :] += jnp.sum(terms, axis=0, keepdims=True)
    pieces.append(dkv[:, hd:].astype(BF))
    dqkv = jnp.concatenate(pieces, axis=1)
    da = dot_nt(dqkv, own_columns(weight, (heads + 2) * hd))
    per = (send_out.shape[1] - go.shape[1]) // blk
    normed_parts = []
    for k in range(parts):
        x = x_refs[k][...].astype(F32)
        part = da[k * blk : (k + 1) * blk]
        normed = x * lax.rsqrt(jnp.mean(x * x, axis=-1, keepdims=True) + EPS)
        normed_parts.append((normed * gain[...]).astype(BF))
        attn_acc[...] += jnp.sum(part * normed, axis=0, keepdims=True)
        at = order[parts * i + k]
        send_out[at // per, pl.ds(pl.multiple_of((at % per) * blk, blk), blk), :] = part.astype(BF)
    grad_acc[...] += dot_tn(jnp.concatenate(normed_parts, axis=0), dqkv)

    @pl.when(i == pl.num_programs(0) - 1)
    def _():
        n = grad_acc.shape[0] // F
        for s_ in range(F):
            f = f_ref[0] ^ s_
            at = pl.multiple_of(f * n, n)
            out = grad_outs[s_]
            for b in range(heads + 2):
                out[b * n : (b + 1) * n, :] = grad_acc[
                    pl.ds(at, n), b * hd : (b + 1) * hd
                ].astype(BF)
            base = (heads + 2) * n
            rows = []
            for r in range(n // hd):
                rows.append(attn_acc[:, pl.ds(pl.multiple_of(at + r * hd, hd), hd)])
            for r in range(n // hd):
                lane = pl.ds(pl.multiple_of(at + r * hd, hd), hd)
                rows.append(fg0[:, lane] + fg1[:, lane])
            rows += [gain_acc[0:1, :], gain_acc[1:2, :]]
            rows += [jnp.zeros((1, hd), F32)] * (8 - len(rows))
            high, low = split_low(jnp.concatenate(rows, axis=0))
            out[base : base + 16, :] = jnp.concatenate([high, low], axis=0)


def head_back_call(
    order, f_idx, x_all, dq, dkv, raw, weight, go, gain, gq, gk, fgains, cos, sin, heads, hd, blk, F
):
    total = dq.shape[0]
    width, cols = x_all.shape[1], (heads + 2) * hd
    parts = 2
    step = parts * blk
    ctx = go.shape[0]
    const = lambda i, o: (0, 0)
    const3 = lambda i, o: (0, 0, 0)
    rows = lambda i, o: (i, 0)
    send = (ctx, total // ctx + go.shape[1], width)
    grad = ((heads + 2) * (width // F) + 16, hd)
    return pl.pallas_call(
        functools.partial(head_back_kernel, parts, blk, heads, hd, F, hd**-0.5),
        out_shape=(like(send, BF),) + (like(grad, BF),) * F,
        grid_spec=pltpu.PrefetchScalarGridSpec(
            num_scalar_prefetch=1,
            grid=(total // step,),
            in_specs=[SMEM]
            + block_specs(parts, blk, width)
            + [
                pl.BlockSpec((step, heads * hd), rows),
                pl.BlockSpec((step, 2 * hd), rows),
                pl.BlockSpec((step, (heads + 1) * hd), rows),
                weight_spec(weight, width),
                pl.BlockSpec(go.shape, const3),
                pl.BlockSpec((1, width), const),
                pl.BlockSpec((1, hd), const),
                pl.BlockSpec((1, hd), const),
                pl.BlockSpec((1, width), const),
                pl.BlockSpec((1, width), const),
                pl.BlockSpec((step, hd), rows),
                pl.BlockSpec((step, hd), rows),
            ],
            out_specs=(pl.BlockSpec(send, const3),) + (pl.BlockSpec(grad, const),) * F,
            scratch_shapes=[
                pltpu.VMEM((width, cols), F32),
                pltpu.VMEM((8, hd), F32),
                pltpu.VMEM((1, width), F32),
            ],
        ),
        compiler_params=params(),
        cost_estimate=cost(60),
        name="head_bwd",
    )(
        order, f_idx, *([x_all] * parts), dq, dkv, raw, weight, go, gain, gq, gk, *fgains, cos, sin
    )


def heads_at(c_ref, f, part):
    return 2 * f + ((c_ref[0] % 2) ^ part)


def resid_kernel(F, f_ref, c_ref, o, wo_a, wo_b, x, g2, h_out, m_out, *o_outs):
    n = wo_a.shape[1] // 2
    half = wo_a.shape[2]
    left, right = x[:, :half].astype(F32), x[:, half:].astype(F32)
    for part, wo in enumerate((wo_a, wo_b)):
        for f in range(F):
            of = o[heads_at(c_ref, f, part)]
            left = left + dot_nn(of, wo[f, :n])
            right = right + dot_nn(of, wo[f, n : 2 * n])
    h = jnp.concatenate([left, right], axis=1)
    h_out[...] = h
    m_out[...] = (h * lax.rsqrt(jnp.mean(h * h, axis=-1, keepdims=True) + EPS) * g2[...]).astype(BF)
    for s in range(F):
        for r in range(2):
            o_outs[s][r] = o[(f_ref[0] ^ s) * 2 + r]


def wo_specs(wo_a, wo_b):
    const3 = lambda i: (0, 0, 0)
    return [pl.BlockSpec(wo_b.shape, const3), pl.BlockSpec(wo_b.shape, const3)]


def resid_call(half, f_idx, c_idx, o, wo_a, wo_b, x, g2):
    C, T, hw = o.shape
    D = x.shape[1]
    F = wo_b.shape[0]
    part = like((2, T, hw), BF)
    const = lambda i: (0, 0)
    const3 = lambda i: (0, 0, 0)
    return pl.pallas_call(
        functools.partial(resid_kernel, F),
        out_shape=(like((T, D), F32), like((T, D), BF)) + (part,) * F,
        grid=(1,),
        in_specs=[SMEM, SMEM, pl.BlockSpec(o.shape, const3)]
        + wo_specs(wo_a, wo_b)
        + [pl.BlockSpec((T, D), lambda i: (half, 0)), pl.BlockSpec(g2.shape, const)],
        out_specs=(pl.BlockSpec((T, D), const),) * 2 + (pl.BlockSpec(part.shape, const3),) * F,
        compiler_params=params(),
        cost_estimate=cost(10),
        name="resid",
    )(f_idx, c_idx, o, wo_a, wo_b, x, g2)


def ffn_kernel(F, *refs):
    c_ref = refs[1]
    ms, gys = refs[2 : 2 + F], refs[2 + F : 2 + 2 * F]
    wgu_a, wgu_b, wd, hid_out, dgu_out = refs[2 + 2 * F : 7 + 2 * F]
    dm_outs, wgu = refs[7 + 2 * F : -1], refs[-1]
    n = wgu_a.shape[1]
    for part, src in enumerate((wgu_a, wgu_b)):
        for f in range(F):
            at = pl.multiple_of(heads_at(c_ref, f, part) * n, n)
            wgu[pl.ds(at, n), :] = src[f]
    ffl = wd.shape[0]
    T = ms[0].shape[0]
    m = jnp.concatenate([r[...] for r in ms], axis=0)
    gy = jnp.concatenate([r[...] for r in gys], axis=0)
    gu = dot_nn(m, wgu[...])
    dhid = dot_nt(gy, wd[...])
    gate, up = gu[:, :ffl], gu[:, ffl:]
    sig = 1.0 / (1.0 + jnp.exp(-gate))
    silu = gate * sig
    hid_out[...] = (silu * up).astype(BF)
    dgu = jnp.concatenate(
        [(dhid * up * (sig + silu * (1.0 - sig))).astype(BF), (dhid * silu).astype(BF)], axis=1
    )
    dgu_out[...] = dgu
    dm = dot_nt(dgu, wgu[...]).astype(BF)
    for s in range(F):
        dm_outs[s][...] = dm[s * T : (s + 1) * T]


def gy_spec(T, D, half):
    return pl.BlockSpec((T, D), lambda i, f: (half, 0))


def ffn_call(half, f_idx, c_idx, ms, gys, wgu_a, wgu_b, wd):
    F = len(ms)
    T, D = ms[0].shape
    ffl = wd.shape[0]
    const = lambda i, f: (0, 0)
    return pl.pallas_call(
        functools.partial(ffn_kernel, F),
        out_shape=(like((F * T, ffl), BF), like((F * T, 2 * ffl), BF)) + (like((T, D), BF),) * F,
        grid_spec=pltpu.PrefetchScalarGridSpec(
            num_scalar_prefetch=1,
            grid=(1,),
            in_specs=[SMEM]
            + [pl.BlockSpec((T, D), const)] * F
            + [gy_spec(T, D, half)] * F
            + [pl.BlockSpec(wgu_a.shape, lambda i, f: (0, 0, 0))] * 2
            + [pl.BlockSpec(wd.shape, const)],
            out_specs=(
                pl.BlockSpec((F * T, ffl), const),
                pl.BlockSpec((F * T, 2 * ffl), const),
            )
            + (pl.BlockSpec((T, D), const),) * F,
            scratch_shapes=[pltpu.VMEM((D, wgu_a.shape[2]), BF)],
        ),
        compiler_params=params(),
        cost_estimate=cost(10),
        name="ffn",
    )(f_idx, c_idx, *ms, *gys, wgu_a, wgu_b, wd)


def resid_back_kernel(F, c_ref, *refs):
    dms = refs[:F]
    wo_a, wo_b, h, gy, g2, dh_out, dhb_out, do_out, gain_out = refs[F:]
    total = dms[0][...].astype(F32)
    for s in range(1, F):
        total = total + dms[s][...].astype(F32)
    dv, terms = norm_back(h[...], g2[...], total)
    gain_out[...] = jnp.sum(terms, axis=0, keepdims=True)
    dh = gy[...].astype(F32) + dv
    dh_out[...] = dh
    low = dh.astype(BF)
    dhb_out[...] = low
    n = wo_a.shape[1] // 2
    half = wo_a.shape[2]
    for part, wo in enumerate((wo_a, wo_b)):
        for f in range(F):
            do = dot_nt(low[:, :half], wo[f, :n]) + dot_nt(low[:, half:], wo[f, n : 2 * n])
            do_out[heads_at(c_ref, f, part)] = do.astype(BF)


def resid_back_call(half, c_idx, dms, h, gy, g2, wo_a, wo_b):
    F = len(dms)
    T, D = h.shape
    hw = wo_b.shape[1] // 2
    const = lambda i: (0, 0)
    return pl.pallas_call(
        functools.partial(resid_back_kernel, F),
        out_shape=(
            like((T, D), F32),
            like((T, D), BF),
            like((2 * F, T, hw), BF),
            like((1, D), F32),
        ),
        grid=(1,),
        in_specs=[SMEM]
        + [pl.BlockSpec((T, D), const)] * F
        + wo_specs(wo_a, wo_b)
        + [
            pl.BlockSpec((T, D), const),
            pl.BlockSpec((T, D), lambda i: (half, 0)),
            pl.BlockSpec(g2.shape, const),
        ],
        out_specs=(
            pl.BlockSpec((T, D), const),
            pl.BlockSpec((T, D), const),
            pl.BlockSpec((2 * F, T, hw), lambda i: (0, 0, 0)),
            pl.BlockSpec((1, D), const),
        ),
        compiler_params=params(),
        cost_estimate=cost(10),
        name="resid_bwd",
    )(c_idx, *dms, wo_a, wo_b, h, gy, g2)


LANE = 256


def wgrad_kernel(F, C, f_ref, *refs):
    ms, gys = refs[: 2 * F], refs[2 * F : 4 * F]
    hid0, hid1, dgu0, dgu1, out, gd = refs[4 * F :]
    D = ms[0].shape[1]
    n = D // F
    R = n // C
    J = dgu0.shape[1] // LANE
    for s in range(F):
        lane = pl.ds(pl.multiple_of((f_ref[0] ^ s) * n, n), n)
        lhs = [jnp.concatenate([r[:, lane] for r in ms[b * F : (b + 1) * F]], axis=0) for b in (0, 1)]
        res = (dot_tn(lhs[0], dgu0[...]) + dot_tn(lhs[1], dgu1[...])).astype(BF)
        for c in range(C):
            for j in range(J):
                out[c, (s * J + j) * R : (s * J + j + 1) * R, :] = res[
                    c * R : (c + 1) * R, j * LANE : (j + 1) * LANE
                ]
    hid = jnp.concatenate([hid0[...], hid1[...]], axis=0)
    gy = jnp.concatenate([r[...] for r in gys], axis=0)
    gd[...] = dot_tn(hid, gy).astype(BF)
    base = F * J * R
    n = gd.shape[0] // C
    for c in range(C):
        for j in range(D // LANE):
            out[c, base + j * n : base + (j + 1) * n, :] = gd[
                c * n : (c + 1) * n, j * LANE : (j + 1) * LANE
            ]


def wgrad_call(f_idx, ms, gys, hiddens, dgus, C):
    F = len(ms) // 2
    T, D = ms[0].shape
    rows, ffl = hiddens[0].shape
    total = 3 * D * ffl // (C * LANE)
    const = lambda i, f: (0, 0)
    return pl.pallas_call(
        functools.partial(wgrad_kernel, F, C),
        out_shape=like((C, total, LANE), BF),
        grid_spec=pltpu.PrefetchScalarGridSpec(
            num_scalar_prefetch=1,
            grid=(1,),
            in_specs=[pl.BlockSpec((T, D), const)] * (2 * F)
            + [gy_spec(T, D, half) for half in range(2) for s in range(F)]
            + [pl.BlockSpec((rows, ffl), const)] * 2
            + [pl.BlockSpec((rows, 2 * ffl), const)] * 2,
            out_specs=pl.BlockSpec((C, total, LANE), lambda i, f: (0, 0, 0)),
            scratch_shapes=[pltpu.VMEM((ffl, D), BF)],
        ),
        compiler_params=params(),
        cost_estimate=cost(15),
        name="wgrad",
    )(f_idx, *ms, *gys, *gys, *hiddens, *dgus)


def ffn_out_kernel(F, hid0, hid1, wd, *outs):
    T = hid0.shape[0] // F
    for half, hid in enumerate((hid0, hid1)):
        res = dot_nn(hid[...], wd[...]).astype(BF)
        for s in range(F):
            outs[s][half * T : (half + 1) * T, :] = res[s * T : (s + 1) * T]


def ffn_out_call(hiddens, wd, F):
    rows = hiddens[0].shape[0]
    D = wd.shape[1]
    return pl.pallas_call(
        functools.partial(ffn_out_kernel, F),
        out_shape=(like((2 * rows // F, D), BF),) * F,
        in_specs=[VMEM] * 3,
        out_specs=(VMEM,) * F,
        compiler_params=params(),
        cost_estimate=cost(5),
        name="ffn_out",
    )(*hiddens, wd)


def go_kernel(parts, *refs):
    os, ds = refs[:parts], refs[parts : 2 * parts]
    out = refs[2 * parts]
    low = jnp.concatenate([r[...] for r in ds], axis=0)
    rows = [
        dot_tn(jnp.concatenate([r[p] for r in os], axis=0), low).astype(BF)
        for p in range(os[0].shape[0])
    ]
    wide = jnp.concatenate(rows, axis=0)
    C, n, _ = out.shape
    for c in range(C):
        out[c] = wide[c * n : (c + 1) * n]


def go_call(os, ds, C):
    per, _, hw = os[0].shape
    D = ds[0].shape[1]
    return pl.pallas_call(
        functools.partial(go_kernel, len(os)),
        out_shape=like((C, per * hw // C, D), BF),
        in_specs=[VMEM] * (2 * len(os)),
        out_specs=VMEM,
        compiler_params=params(),
        cost_estimate=cost(5),
        name="wgrad_out",
    )(*os, *ds)


def combine_kernel(F, body_rows, *refs):
    out = refs[F]
    total = refs[0][:body_rows, :].astype(F32)
    for s in range(1, F):
        total = total + refs[s][:body_rows, :].astype(F32)
    out[:body_rows, :] = total.astype(BF)
    small = jnp.zeros((8, out.shape[1]), F32)
    for s in range(F):
        both = refs[s][body_rows:, :].astype(F32)
        small = small + both[:8] + both[8:]
    high, low = split_low(small)
    out[body_rows:, :] = jnp.concatenate([high, low], axis=0)


def combine_call(parts):
    rows, hd = parts[0].shape
    return pl.pallas_call(
        functools.partial(combine_kernel, len(parts), rows - 16),
        out_shape=like((rows, hd), BF),
        in_specs=[VMEM] * len(parts),
        out_specs=VMEM,
        compiler_params=params(8),
        cost_estimate=cost(2),
        name="combine",
    )(*parts)


def unpack_ffn_kernel(F, R, J, f_ref, src, gate_out, up_out, down_out):
    half = J // 2
    ffl = half * LANE
    for s in range(F):
        base = pl.multiple_of((f_ref[0] ^ s) * ffl, ffl)
        for j in range(J):
            (gate_out if j < half else up_out)[:, pl.ds(base + (j % half) * LANE, LANE)] = src[
                0, (s * J + j) * R : (s * J + j + 1) * R, :
            ].astype(F32)
    n, wide = down_out.shape
    for j in range(wide // LANE):
        at = F * J * R + j * n
        down_out[:, j * LANE : (j + 1) * LANE] = src[0, at : at + n, :].astype(F32)


def unpack_ffn_call(f_idx, src, F, R, FF, D):
    C, rows, _ = src.shape
    J = 2 * FF // (F * LANE)
    n = FF // (F * C)
    row = lambda c, f: (c, 0)
    return pl.pallas_call(
        functools.partial(unpack_ffn_kernel, F, R, J),
        out_shape=(like((C * R, FF), F32), like((C * R, FF), F32), like((C * n, D), F32)),
        grid_spec=pltpu.PrefetchScalarGridSpec(
            num_scalar_prefetch=1,
            grid=(C,),
            in_specs=[pl.BlockSpec((1, rows, LANE), lambda c, f: (c, 0, 0))],
            out_specs=(
                pl.BlockSpec((R, FF), row),
                pl.BlockSpec((R, FF), row),
                pl.BlockSpec((n, D), row),
            ),
        ),
        compiler_params=params(16),
        cost_estimate=cost(8),
        name="unpack_ffn",
    )(f_idx, src)


def join_kernel(p, o, out):
    n, hd = p.shape
    out[:n, :] = p[...]
    rows, wide = o.shape
    for j in range(wide // hd):
        out[n + j * rows : n + (j + 1) * rows, :] = o[:, j * hd : (j + 1) * hd]


def join_call(p, summed, n_o):
    n, hd = p.shape
    total, D = summed.shape
    rows = n + n_o * D // hd
    return pl.pallas_call(
        join_kernel,
        out_shape=like((rows, hd), BF),
        grid=(1,),
        in_specs=[
            pl.BlockSpec((n, hd), lambda i: (0, 0)),
            pl.BlockSpec((n_o, D), lambda i: (total // n_o - 1, 0)),
        ],
        out_specs=pl.BlockSpec((rows, hd), lambda i: (0, 0)),
        compiler_params=params(8),
        cost_estimate=cost(2),
        name="join",
    )(p, summed)


def unpack_attn_kernel(heads, hd, rep, src, q_out, k_out, v_out, o_out, small_out):
    C = src.shape[0]
    rows = q_out.shape[0]
    n = o_out.shape[0] // C
    small = jnp.zeros((8, hd), F32)
    for c in range(C):
        for h in range(heads):
            at = (c * heads + h) * hd
            q_out[:, at : at + hd] = src[c, h * rows : (h + 1) * rows, :].astype(F32)
        lane = slice((c // rep) * hd, (c // rep + 1) * hd)
        for h, out in ((heads, k_out), (heads + 1, v_out)):
            value = src[c, h * rows : (h + 1) * rows, :].astype(F32)
            if c % rep == 0:
                out[:, lane] = value
            else:
                out[:, lane] += value
        at = (heads + 2) * rows
        both = src[c, at : at + 16, :].astype(F32)
        small = small + both[:8] + both[8:]
        for j in range(o_out.shape[1] // hd):
            o_out[c * n : (c + 1) * n, j * hd : (j + 1) * hd] = src[
                c, at + 16 + j * n : at + 16 + (j + 1) * n, :
            ].astype(F32)
    small_out[...] = small


def unpack_attn_call(src, heads, hd, rep, rows, n_o, D):
    C = src.shape[0]
    return pl.pallas_call(
        functools.partial(unpack_attn_kernel, heads, hd, rep),
        out_shape=(
            like((rows, C * heads * hd), F32),
            like((rows, C * hd // rep), F32),
            like((rows, C * hd // rep), F32),
            like((C * n_o, D), F32),
            like((8, hd), F32),
        ),
        in_specs=[VMEM],
        out_specs=(VMEM,) * 5,
        compiler_params=params(20),
        cost_estimate=cost(5),
        name="unpack_attn",
    )(src)


def after(value, *others):
    return lax.optimization_barrier((value,) + others)[0]


def body(
    block_input,
    cotangent,
    seq_lengths,
    block_table,
    query_proj,
    key_proj,
    value_proj,
    output_proj,
    gate_proj,
    up_proj,
    down_proj,
    attn_norm,
    ffn_norm,
    query_norm,
    key_norm,
):
    C = lax.axis_size("ctx")
    F = lax.axis_size("fsdp")
    c_at = lax.axis_index("ctx")
    f_at = lax.axis_index("fsdp")
    core = lax.rem(c_at, 2)
    c_idx, f_idx = c_at[None].astype(jnp.int32), f_at[None].astype(jnp.int32)
    T, D = block_input.shape[1:]
    S = T * C
    blocks = block_table.shape[0]
    blk = S // blocks
    hd = query_norm.shape[0] * F
    HQ = query_proj.shape[1] // hd
    KV = key_proj.shape[1] // hd
    FF = gate_proj.shape[1]
    heads = HQ // C
    rep = max(1, C // KV)
    FFl = FF // F
    R = D // (F * C)
    scale = 1.0 / math.sqrt(hd)
    length = seq_lengths.astype(jnp.int32)
    own_blocks = lax.dynamic_slice_in_dim(block_table, c_at * (blocks // C), blocks // C)
    own_pos = (own_blocks[:, None] * blk + jnp.arange(blk, dtype=jnp.int32)[None, :]).reshape(-1)
    live = (own_pos < length[0]).astype(F32)[:, None]
    order = jnp.argsort(block_table).astype(jnp.int32)

    def gather_f(v):
        return lax.all_to_all(jnp.broadcast_to(v[None], (F,) + v.shape), "fsdp", 0, 0)

    def exchange_c(v):
        return lax.all_to_all(v, "ctx", 0, 0)

    def to_partner(v, s):
        return lax.ppermute(v, "fsdp", [(i, i ^ s) for i in range(F)])

    def gather_x(v):
        return [v] + [to_partner(v, s) for s in range(1, F)]

    def exchange_x(vs):
        return [vs[0]] + [to_partner(vs[s], s) for s in range(1, F)]

    def other_core(v):
        return lax.ppermute(v, "ctx", [(i, i ^ 1) for i in range(C)])

    def gather_c(v):
        parts = [v] + [
            lax.ppermute(v, "ctx", [(i, i ^ (2 * k)) for i in range(C)]) for k in range(1, C // 2)
        ]
        return [p for v in parts for p in (v, other_core(v))]

    x_all = lax.all_gather(block_input[0], "ctx", axis=0, tiled=True)
    kv_at = (c_at // rep) * hd
    cols = (heads + 2) * hd
    w_own = jnp.concatenate(
        [
            lax.dynamic_slice_in_dim(query_proj, c_at * heads * hd, heads * hd, 1),
            lax.dynamic_slice_in_dim(key_proj, kv_at, hd, 1),
            lax.dynamic_slice_in_dim(value_proj, kv_at, hd, 1),
        ],
        axis=1,
    ).astype(BF)
    gains_own = jnp.concatenate([attn_norm, ffn_norm, query_norm, key_norm]).astype(BF)
    lanes = D // 2
    w_own = jnp.pad(w_own, ((0, 0), (0, lanes - cols)))
    gain_rows = -(-gains_own.shape[0] // (16 * lanes)) * 16
    gains_own = jnp.pad(gains_own, (0, gain_rows * lanes - gains_own.shape[0]))
    wo_rows = output_proj.shape[0] // 2
    wo_half = lax.dynamic_slice_in_dim(output_proj, core * wo_rows, wo_rows, 0).astype(BF)
    n_wo = 2 * wo_rows
    moved = gather_f(
        jnp.concatenate(
            [wo_half[:, :lanes], wo_half[:, lanes:], w_own, gains_own.reshape(gain_rows, lanes)],
            axis=0,
        )
    )
    gains = moved[:, n_wo + D // F :].reshape(F, gain_rows * lanes).astype(F32)
    g1 = gains[:, : D // F].reshape(1, D)
    g2 = gains[:, D // F : 2 * D // F].reshape(1, D)
    gq = gains[:, 2 * D // F : (2 * D + hd) // F].reshape(1, hd)
    gk = gains[:, (2 * D + hd) // F : (2 * D + 2 * hd) // F].reshape(1, hd)
    wo_a = moved
    wo_b = other_core(moved[:, :n_wo])
    gu_rows = D // F // 2
    half_of = lambda w: lax.dynamic_slice_in_dim(w, core * gu_rows, gu_rows, 0).astype(BF)
    wgu_half = jnp.concatenate(
        [half_of(gate_proj).reshape(gu_rows, F, FFl), half_of(up_proj).reshape(gu_rows, F, FFl)],
        axis=2,
    )
    wgu_a = lax.all_to_all(after(jnp.swapaxes(wgu_half, 0, 1), moved), "fsdp", 0, 0)
    wd = down_proj.astype(BF)
    gy = (cotangent[0].astype(F32) * live).astype(BF)
    gys = gather_x(after(gy, wgu_a))

    half = hd // 2
    frequency = THETA ** (-(jnp.arange(half).astype(F32) * 2.0 / hd))
    angles = jnp.arange(S, dtype=jnp.int32).astype(F32)[:, None] * frequency[None, :]
    cos_t, sin_t = jnp.cos(angles), jnp.sin(angles)
    cos_t = jnp.concatenate([cos_t, cos_t], -1)
    sin_t = jnp.concatenate([-sin_t, sin_t], -1)
    raw, low = qkv_call(order, x_all, g1, moved, gq, gk, cos_t, sin_t, heads, hd, blk)
    o_even, o_odd, o32, lse = attn_call(order, length, low, heads, hd, blk, scale)


    x = block_input[0]
    o_nat = [exchange_c(after(o_even, wgu_a))]
    o_nat.append(exchange_c(after(o_odd, o_nat[0])))
    hs, ms, os, hiddens, dgus, dhs, dhbs, dos, fgains = [], [], [], [], [], [], [], [], []
    for b in range(2):
        o_b = o_nat[b] if b == 0 else after(o_nat[b], *gys)
        h, m_own, *o_parts = resid_call(b, f_idx, c_idx, o_b, wo_a, wo_b, x, g2)
        hs.append(h)
        os.append(o_parts)
        ms.append(gather_x(m_own))
    dms = []
    wgu_a = after(wgu_a, hs[0])
    wgu_b = other_core(wgu_a)
    for b in range(2):
        hidden, dgu, *dm_parts = ffn_call(b, f_idx, c_idx, ms[b], gys, wgu_a, wgu_b, wd)
        hiddens.append(hidden)
        dgus.append(dgu)
        dms.append(exchange_x(dm_parts))
    hiddens[1] = after(hiddens[1], *dms[0])
    packed = wgrad_call(f_idx, ms[0] + ms[1], gys, hiddens, dgus, C)
    hs[1] = after(hs[1], packed)
    for b in range(2):
        dh, dhb, do_nat, fgain = resid_back_call(b, c_idx, dms[b], hs[b], gy, g2, wo_a, wo_b)
        dhs.append(dh)
        dhbs.append(dhb)
        fgains.append(fgain)
        dos.append(exchange_c(do_nat))

    owned = lax.psum_scatter(packed.reshape(-1, LANE), "ctx", scatter_dimension=0, tiled=True)
    owned = after(owned, dos[1])
    n_s = 2 * FFl // LANE * R
    owned_gu = exchange_x([owned[s * n_s : (s + 1) * n_s] for s in range(F)])
    all_ffn = lax.all_gather(jnp.concatenate(owned_gu + [owned[F * n_s :]], axis=0), "ctx", axis=0)
    grad_gate, grad_up, grad_down = unpack_ffn_call(f_idx, all_ffn, F, R, FF, D)

    ffn_parts = exchange_x([after(v, *owned_gu) for v in ffn_out_call(hiddens, wd, F)])
    ffn = sum(p.astype(F32) for p in ffn_parts)
    block_output = ((jnp.concatenate(hs, axis=0) + ffn) * live).astype(BF)[None]

    dq, dkv = attn_back_call(order, length, low, dos[0], dos[1], o32, lse, heads, hd, blk, scale)
    o_f = [p for parts in os for p in exchange_x([after(v, dhbs[1]) for v in parts])]
    dhb_f = [p for v in dhbs for p in gather_x(v)]
    go = go_call(o_f, dhb_f, C)
    n_o = go.shape[1]
    send, *grad_parts = head_back_call(
        order, f_idx, x_all, after(dq, *ffn_parts), dkv, raw, moved, go, g1, gq, gk, fgains, cos_t, sin_t,
        heads, hd, blk, F,
    )
    summed = lax.psum_scatter(after(send, all_ffn).reshape(-1, D), "ctx", scatter_dimension=0, tiled=True)
    dx, _ = norm_back(x.astype(F32), g1, summed[:T].astype(F32))
    grad_input = (jnp.concatenate(dhs, axis=0) + dx)[None]

    own_p = combine_call(exchange_x(grad_parts))
    joined = lax.all_gather(join_call(own_p, summed, n_o), "ctx", axis=0)
    grad_query, grad_key, grad_value, grad_output, small = unpack_attn_call(
        joined, heads, hd, rep, D // F, n_o, D
    )
    n_r = D // F // hd
    own_gain = lambda r: lax.dynamic_slice_in_dim(small[2 * n_r + r], f_at * (hd // F), hd // F)

    return (
        block_output,
        grad_input,
        grad_query,
        grad_key,
        grad_value,
        grad_output,
        grad_gate,
        grad_up,
        grad_down,
        small[:n_r].reshape(-1),
        small[n_r : 2 * n_r].reshape(-1),
        own_gain(0),
        own_gain(1),
    )


def solution(mesh):
    matrix, vector = P("fsdp", None), P("fsdp")
    rows = P("fsdp", "ctx", None)
    in_specs = (rows, rows, vector, P()) + (matrix,) * 7 + (vector,) * 4
    out_specs = (rows, rows) + (matrix,) * 7 + (vector,) * 4
    return jax.shard_map(body, mesh=mesh, in_specs=in_specs, out_specs=out_specs, check_vma=False)
```
